32 devices in a mesh: dp: 4 (over x, core), ctx: 4 (over z), tensor: 2 (over y).
Axes of the slice: x: 2, y: 2, z: 4, core: 2. Of those that a mesh axis runs over, the one named last changes fastest.
Arguments:
- block_input: bfloat16 [12288, 2048], P(('dp', 'ctx'), 'tensor'), may hold values from -6 to 6
- cotangent: bfloat16 [12288, 2048], P(('dp', 'ctx'), 'tensor'), may hold values from -6 to 6
- deal_order: int32 [4, 4], P('dp'), may hold values from 0 to 3, as said below
- seq_lengths: int32 [12], P('dp'), may hold values from 96 to 2880, as said below
- seq_adapter: int32 [12], P('dp'), may hold values from 0 to 7
- mixer_gain: bfloat16 [2048], replicated, may hold values from 0.099609375 to 1.8984375
- ffn_gain: bfloat16 [2048], replicated, may hold values from 0.099609375 to 1.8984375
- conv_taps: bfloat16 [3, 2048], P(None, 'tensor'), may hold values from -3.5 to 3.5
- in_weight: bfloat16 [3, 2048, 2048], P(None, 'dp', 'tensor'), may hold values from -0.125 to 0.125
- out_weight: bfloat16 [2048, 2048], P('tensor', 'dp'), may hold values from -0.125 to 0.125
- gateup_weight: bfloat16 [2, 2048, 5632], P(None, 'dp', 'tensor'), may hold values from -0.125 to 0.125
- down_weight: bfloat16 [5632, 2048], P('tensor', 'dp'), may hold values from -0.078125 to 0.078125
- input_adapter_shrink: bfloat16 [2048, 128], replicated, may hold values from -0.125 to 0.125
- in_expand: bfloat16 [3, 128, 2048], P(None, None, 'tensor'), may hold values from -1.5 to 1.5
- out_shrink: bfloat16 [2048, 128], P('tensor'), may hold values from -0.125 to 0.125
- output_adapter_expand: bfloat16 [128, 2048], replicated, may hold values from -1.5 to 1.5
- ffn_shrink: bfloat16 [2048, 256], replicated, may hold values from -0.125 to 0.125
- ffn_expand: bfloat16 [2, 128, 5632], P(None, None, 'tensor'), may hold values from -1.5 to 1.5
- down_shrink: bfloat16 [5632, 128], P('tensor'), may hold values from -0.078125 to 0.078125
- down_adapter_expand: bfloat16 [128, 2048], replicated, may hold values from -1.5 to 1.5
Outputs:
- block_output: bfloat16 [12288, 2048], P(('dp', 'ctx'), 'tensor')
- input_grad: float32 [12288, 2048], P(('dp', 'ctx'), 'tensor')
- in_shrink_grad: float32 [2048, 128], replicated
- input_expand_gradient: float32 [3, 128, 2048], P(None, None, 'tensor')
- out_shrink_grad: float32 [2048, 128], P('tensor')
- output_expand_gradient: float32 [128, 2048], replicated
- ffn_shrink_grad: float32 [2048, 256], replicated
- feedforward_expand_gradient: float32 [2, 128, 5632], P(None, None, 'tensor')
- down_shrink_grad: float32 [5632, 128], P('tensor')
- down_adapter_expand_gradient: float32 [128, 2048], replicated
The draws below stay inside these ranges and needn't reach their ends.
Inputs may be any that keep to these rules, and one draw needn't show every extreme that they name: `deal_order`: each row is a permutation of the 4 shard numbers. `seq_lengths`: each data group's 3 entries sum to 3072; all but one of them lie between 96 and 192.
All inputs are finite; a program needn't handle non-finite values.
Results may differ from the reference program's by a relative error of at most 0.013.
Values may be sent and summed in bfloat16 or wider, within the bound.
No kernel may reach another device: no remote copies, remote signals or barrier semaphores. Data moves between devices by JAX's collectives and lax.ppermute only.
A program may use at most 256 MiB of HBM per device.

```python
import jax
import jax.numpy as jnp
from jax import lax

D = 2048
FF = 5632
RANK = 16
ADAPTERS = 8
KW = 3
SEQ_G = 3
TOK_DEV = 768
EXPAND_COLUMNS = 128
SUB = 192
GROUP_TOKENS = 3072
MINLEN = 96
TOKENS = 12288
SEQS = 12
N_DP = 4
N_CTX = 4


def draw_deal_order(key, part):
    group_count = SEQS // SEQ_G
    keys = jax.random.split(jax.random.fold_in(key, 17), group_count)
    rows = jax.vmap(lambda single: jax.random.permutation(single, group_count))(keys)
    return rows.astype(jnp.int32)


def draw_seq_lengths(key, part):
    group_count = SEQS // SEQ_G
    key_short, key_pick, key_place = jax.random.split(key, 3)
    shorts = jax.random.randint(key_short, (group_count, SEQ_G - 1), MINLEN, 2 * MINLEN + 1, dtype=jnp.int32)
    chosen = jax.random.randint(key_pick, (), 0, group_count, dtype=jnp.int32)
    group_ids = jnp.arange(group_count, dtype=jnp.int32)
    shorts = jnp.where((group_ids == chosen)[:, None], MINLEN, shorts).astype(jnp.int32)
    longest = (N_CTX * TOK_DEV - jnp.sum(shorts, axis=1)).astype(jnp.int32)
    long_slot = jax.random.randint(key_place, (group_count,), 0, SEQ_G, dtype=jnp.int32)
    slot_ids = jnp.arange(SEQ_G, dtype=jnp.int32)[None, :]
    short_pick = jnp.clip(slot_ids - (slot_ids > long_slot[:, None]).astype(jnp.int32), 0, SEQ_G - 2)
    chosen_short = jnp.take_along_axis(shorts, short_pick, axis=1)
    lengths = jnp.where(slot_ids == long_slot[:, None], longest[:, None], chosen_short)
    return lengths.reshape(-1).astype(jnp.int32)


def with_ends(array, rng, smallest, largest):
    longest = array.shape.index(max(array.shape))
    spots = []
    for shift in (0, 1):
        where = [jax.random.randint(jax.random.fold_in(rng, axis), (), 0, length) for axis, length in enumerate(array.shape)]
        where[longest] = (where[longest] + shift) % array.shape[longest]
        spots.append(tuple(where))
    return array.at[spots[0]].set(smallest).at[spots[1]].set(largest)


def block_levels(rng, extent, shards, least, top_value):
    gain, own = 1.0, jax.random.fold_in(rng, 6)
    for position, parts in shards:
        steps = jnp.exp(jax.random.uniform(jax.random.fold_in(own, position), (parts,), jnp.float32, least / len(shards), top_value / len(shards)))
        gain = gain * jnp.repeat(steps, extent[position] // parts).reshape([-1 if axis == position else 1 for axis in range(len(extent))])
    return gain


def normal_values(rng, dims, width, limit, pieces=(), held_as=jnp.bfloat16):
    values = width * jax.random.normal(rng, dims, jnp.float32)
    if pieces:
        values = values * block_levels(rng, dims, pieces, -0.22, 0.18)
    return jnp.clip(values, -limit, limit).astype(held_as)


def setup_inputs(seed: int = 0) -> dict:
    key_list = jax.random.split(jax.random.key(seed), 21)
    block_input = normal_values(key_list[0], (TOKENS, D), 1.0, 6.0, ((0, 16), (1, 2)))
    cotangent = normal_values(key_list[1], (TOKENS, D), 1.0, 6.0, ((0, 16), (1, 2)))
    deal_order = draw_deal_order(jax.random.fold_in(key_list[20], 71), 0)
    seq_lengths = draw_seq_lengths(jax.random.fold_in(key_list[20], 71), 0)
    seq_adapter = with_ends(jax.random.randint(key_list[4], (SEQS,), 0, ADAPTERS), jax.random.fold_in(key_list[4], 1), 0, ADAPTERS - 1).astype(jnp.int32)
    mixer_gain = jnp.clip(1.0 + 0.18 * jax.random.normal(key_list[5], (D,), jnp.float32), 0.099609375, 1.8984375).astype(jnp.bfloat16)
    ffn_gain = jnp.clip(1.0 + 0.18 * jax.random.normal(key_list[6], (D,), jnp.float32), 0.099609375, 1.8984375).astype(jnp.bfloat16)
    conv_taps = normal_values(key_list[7], (KW, D), KW ** -0.5, 3.5, ((1, 2),))
    in_weight = normal_values(key_list[8], (3, D, D), D ** -0.5, 0.125, ((1, 4), (2, 2)))
    out_weight = normal_values(key_list[9], (D, D), D ** -0.5, 0.125, ((0, 2), (1, 4)))
    gateup_weight = normal_values(key_list[10], (2, D, FF), D ** -0.5, 0.125, ((1, 4), (2, 2)))
    down_weight = normal_values(key_list[11], (FF, D), FF ** -0.5, 0.078125, ((0, 2), (1, 4)))
    input_adapter_shrink = normal_values(key_list[12], (D, EXPAND_COLUMNS), D ** -0.5, 0.125)
    in_expand = normal_values(key_list[13], (3, EXPAND_COLUMNS, D), RANK ** -0.5, 1.5, ((2, 2),))
    out_shrink = normal_values(key_list[14], (D, EXPAND_COLUMNS), D ** -0.5, 0.125, ((0, 2),))
    output_adapter_expand = normal_values(key_list[15], (EXPAND_COLUMNS, D), RANK ** -0.5, 1.5)
    ffn_shrink = normal_values(key_list[16], (D, 2 * EXPAND_COLUMNS), D ** -0.5, 0.125)
    ffn_expand = normal_values(key_list[17], (2, EXPAND_COLUMNS, FF), RANK ** -0.5, 1.5, ((2, 2),))
    down_shrink = normal_values(key_list[18], (FF, EXPAND_COLUMNS), FF ** -0.5, 0.078125, ((0, 2),))
    down_adapter_expand = normal_values(key_list[19], (EXPAND_COLUMNS, D), RANK ** -0.5, 1.5)
    return {"block_input": block_input, "cotangent": cotangent, "deal_order": deal_order, "seq_lengths": seq_lengths, "seq_adapter": seq_adapter, "mixer_gain": mixer_gain, "ffn_gain": ffn_gain, "conv_taps": conv_taps, "in_weight": in_weight, "out_weight": out_weight, "gateup_weight": gateup_weight, "down_weight": down_weight, "input_adapter_shrink": input_adapter_shrink, "in_expand": in_expand, "out_shrink": out_shrink, "output_adapter_expand": output_adapter_expand, "ffn_shrink": ffn_shrink, "ffn_expand": ffn_expand, "down_shrink": down_shrink, "down_adapter_expand": down_adapter_expand}


@jax.custom_vjp
def rank_rows(v):
    return lax.optimization_barrier(v.astype(jnp.bfloat16)).astype(jnp.float32)

@jax.custom_vjp
def rank_rows_backward(v):
    return v

def low_keep(v):
    return (rank_rows(v), None)

def low_pass(kept, grad):
    return (grad,)

def back_keep(v):
    return (v, None)

def back_low(kept, grad):
    return (rank_rows(grad),)
rank_rows.defvjp(low_keep, low_pass)
rank_rows_backward.defvjp(back_keep, back_low)
norm_eps = 1e-05
adapter_scale = 0.5
highest_precision = lax.Precision.HIGHEST

def rms_scale(values):
    return lax.rsqrt(lax.optimization_barrier(jnp.mean(values * values, axis=-1, keepdims=True)) + norm_eps)

def segment_of(positions, seq_ends):
    return lax.optimization_barrier(jnp.sum((positions[:, None] >= seq_ends[None, :]).astype(jnp.int32), axis=1)).astype(jnp.int32)

def group_lookup_tables(group_length_values, adapter_group_ids):
    seq_ends = jnp.cumsum(group_length_values).astype(jnp.int32)[:-1]
    positions = jnp.arange(GROUP_TOKENS, dtype=jnp.int32)
    segment = segment_of(positions, seq_ends)
    slot_ids = jnp.arange(SEQ_G, dtype=jnp.int32)
    token_adapter_index = lax.optimization_barrier(jnp.sum(jnp.where(segment[:, None] == slot_ids[None, :], adapter_group_ids[None, :], 0), axis=1)).astype(jnp.int32)
    column_group_index = jnp.arange(EXPAND_COLUMNS, dtype=jnp.int32) // RANK
    adapter_mask = (column_group_index[None, :] == token_adapter_index[:, None]).astype(jnp.float32)
    matching_first = ((positions >= 1) & (segment_of(positions - 1, seq_ends) == segment)).astype(jnp.float32)[:, None]
    matching_second = ((positions >= 2) & (segment_of(positions - 2, seq_ends) == segment)).astype(jnp.float32)[:, None]
    return (adapter_mask, matching_first, matching_second)

def pack_group(slab, deal_row):
    picked = jnp.take(slab, deal_row, axis=0)
    return jnp.transpose(picked, (1, 0, 2, 3)).reshape(GROUP_TOKENS, D)

def unpack_group(rows, inverse_row):
    blocks = rows.reshape(N_CTX, N_DP, SUB, D)
    return jnp.take(blocks, inverse_row, axis=1)

def reference(block_input, cotangent, deal_order, seq_lengths, seq_adapter, mixer_gain, ffn_gain, conv_taps, in_weight, out_weight, gateup_weight, down_weight, input_adapter_shrink, in_expand, out_shrink, output_adapter_expand, ffn_shrink, ffn_expand, down_shrink, down_adapter_expand):
    mixer_f = mixer_gain.astype(jnp.float32)
    ffn_f = ffn_gain.astype(jnp.float32)
    taps_f = conv_taps.astype(jnp.float32)
    input_matrix = in_weight.astype(jnp.float32)
    output_matrix = out_weight.astype(jnp.float32)
    gate_up_matrix = gateup_weight.astype(jnp.float32)
    down_matrix = down_weight.astype(jnp.float32)
    adapters = (input_adapter_shrink.astype(jnp.float32), in_expand.astype(jnp.float32), out_shrink.astype(jnp.float32), output_adapter_expand.astype(jnp.float32), ffn_shrink.astype(jnp.float32), ffn_expand.astype(jnp.float32), down_shrink.astype(jnp.float32), down_adapter_expand.astype(jnp.float32))
    group_count = N_DP
    input_slabs = jnp.moveaxis(block_input.reshape(N_DP, N_CTX, N_DP, SUB, D), 2, 0)
    cot_slabs = jnp.moveaxis(cotangent.reshape(N_DP, N_CTX, N_DP, SUB, D), 2, 0)
    deal_rows = deal_order.astype(jnp.int32)
    inverse_rows = jnp.argsort(deal_rows, axis=1).astype(jnp.int32)
    length_groups = seq_lengths.reshape(group_count, SEQ_G)
    adapter_groups = seq_adapter.reshape(group_count, SEQ_G)

    def group_step(carry, inputs):
        input_slab, cot_slab, deal_row, inverse_row, group_length_values, adapter_group_ids = inputs
        input_group = pack_group(input_slab, deal_row)
        cot_group = pack_group(cot_slab, deal_row)
        adapter_mask, matching_first, matching_second = group_lookup_tables(group_length_values, adapter_group_ids)
        adapter_mask_pair = jnp.concatenate([adapter_mask, adapter_mask], axis=1)

        def forward(x_float, in_first_factor, in_second_factor, out_first_factor, out_second_factor, a_ffn, ffn_second_factor, down_first_factor, down_second_factor):
            normalized_rows = rank_rows(x_float * rms_scale(x_float) * mixer_f)
            input_rank_rows = rank_rows_backward(rank_rows(jnp.dot(normalized_rows, in_first_factor, precision=highest_precision)) * adapter_mask)
            projected_rows = rank_rows_backward(jnp.einsum('px,sxa->psa', normalized_rows, input_matrix, precision=highest_precision) + adapter_scale * jnp.einsum('fw,kwo->fko', input_rank_rows, in_second_factor, precision=highest_precision))
            gate_b = projected_rows[:, 0]
            gate_c = projected_rows[:, 1]
            values = projected_rows[:, 2]
            mixed = rank_rows(gate_b * values)
            padded = jnp.pad(mixed, ((2, 0), (0, 0)))
            conv_out = taps_f[0] * mixed + taps_f[1] * padded[1:-1] * matching_first + taps_f[2] * padded[:-2] * matching_second
            gated_rows = rank_rows(gate_c * conv_out)
            output_rank_rows = rank_rows_backward(rank_rows(jnp.dot(gated_rows, out_first_factor, precision=highest_precision)) * adapter_mask)
            adapter_branch = rank_rows_backward(jnp.dot(gated_rows, output_matrix, precision=highest_precision) + adapter_scale * jnp.dot(output_rank_rows, out_second_factor, precision=highest_precision))
            hidden_state_rows = x_float + adapter_branch
            feedforward_input = rank_rows(hidden_state_rows * rms_scale(hidden_state_rows) * ffn_f)
            feedforward_rank_rows = rank_rows_backward(rank_rows(jnp.dot(feedforward_input, a_ffn, precision=highest_precision)) * adapter_mask_pair)
            gate_up_output = rank_rows_backward(jnp.einsum('cm,ame->cae', feedforward_input, gate_up_matrix, precision=highest_precision) + adapter_scale * jnp.einsum('vmc,mcb->vmb', feedforward_rank_rows.reshape(GROUP_TOKENS, 2, EXPAND_COLUMNS), ffn_second_factor, precision=highest_precision))
            activated_rows = rank_rows(jax.nn.silu(gate_up_output[:, 0]) * gate_up_output[:, 1])
            down_rank_rows = rank_rows_backward(rank_rows(jnp.dot(activated_rows, down_first_factor, precision=highest_precision)) * adapter_mask)
            return hidden_state_rows + jnp.dot(activated_rows, down_matrix, precision=highest_precision) + adapter_scale * jnp.dot(down_rank_rows, down_second_factor, precision=highest_precision)
        result, pullback = jax.vjp(forward, input_group.astype(jnp.float32), *adapters)
        grads = pullback(cot_group.astype(jnp.float32))
        new_carry = jax.tree.map(lambda total, update: total + update, carry, tuple(grads[1:]))
        return (new_carry, (unpack_group(result.astype(jnp.bfloat16), inverse_row), unpack_group(grads[0], inverse_row)))
    zeros = tuple((jnp.zeros(item.shape, jnp.float32) for item in adapters))
    totals, outputs = lax.scan(group_step, zeros, (input_slabs, cot_slabs, deal_rows, inverse_rows, length_groups, adapter_groups))
    block_output = jnp.transpose(outputs[0], (2, 1, 0, 3, 4)).reshape(TOKENS, D)
    input_grad = jnp.transpose(outputs[1], (2, 1, 0, 3, 4)).reshape(TOKENS, D)
    return (block_output, input_grad, totals[0], totals[1], totals[2], totals[3], totals[4], totals[5], totals[6], totals[7])
```

```python
import jax
import jax.numpy as jnp
from jax import lax
from jax.sharding import PartitionSpec as P

RANK = 16
CHUNKS = 2

norm_eps = 1e-05
adapter_scale = 0.5

f32 = jnp.float32
bf16 = jnp.bfloat16


def dot(left, right):
    return jnp.dot(left, right, preferred_element_type=f32)


def dot_nt(left, right):
    return lax.dot_general(left, right, (((1,), (1,)), ((), ())), preferred_element_type=f32)


def dot_tn(left, right):
    return lax.dot_general(left, right, (((0,), (0,)), ((), ())), preferred_element_type=f32)


def rms_scale(values):
    return lax.rsqrt(jnp.mean(values * values, axis=-1, keepdims=True) + norm_eps)


def block_order(array, axis, index_list, width):
    pieces = [lax.dynamic_slice_in_dim(array, i * width, width, axis) for i in index_list]
    return jnp.concatenate(pieces, axis=axis)


def swap_tensor(array):
    return lax.ppermute(array, "tensor", [(0, 1), (1, 0)])


def body(
    block_input,
    cotangent,
    deal_order,
    seq_lengths,
    seq_adapter,
    mixer_gain,
    ffn_gain,
    conv_taps,
    in_weight,
    out_weight,
    gateup_weight,
    down_weight,
    input_adapter_shrink,
    in_expand,
    out_shrink,
    output_adapter_expand,
    ffn_shrink,
    ffn_expand,
    down_shrink,
    down_adapter_expand,
):
    tok_count, half = block_input.shape
    width = 2 * half
    rank_cols = input_adapter_shrink.shape[1]
    groups = lax.axis_size("dp")
    pieces = lax.axis_size("ctx")
    sub = tok_count // groups
    group_tokens = pieces * tok_count
    seqs = seq_lengths.shape[0]
    special = groups == 4 and pieces % 2 == 0
    me = lax.axis_index("dp")
    ctx = lax.axis_index("ctx")
    tens = lax.axis_index("tensor")
    if special:
        xb, cb, zb = me // 2, me % 2, ctx % 2
    else:
        xb = cb = zb = jnp.int32(0)
    pair_flip = xb ^ tens
    sub_width = width // 8

    actual = []
    in_stack = []
    for rx in (0, 1):
        for rc in (0, 1):
            for rh in (0, 1):
                low = (rc ^ cb) * 2 + (rh ^ (zb & rx))
                actual.append((rx ^ xb) * 4 + low)
                in_stack.append((rx ^ pair_flip) * 4 + low)
    inner = []
    for bc in (0, 1):
        for bh in (0, 1):
            inner.append((bc ^ cb) * 2 + (bh ^ (zb & pair_flip)))

    def relative(array, axis):
        return block_order(array, axis, actual, sub_width) if special else array

    def own_half(array, axis):
        return lax.dynamic_slice_in_dim(array, pair_flip * half, half, axis)

    def other_half(array, axis):
        return lax.dynamic_slice_in_dim(array, (1 - pair_flip) * half, half, axis)

    def restored(array, axis):
        return block_order(array, axis, inner, sub_width) if special else array

    core_route = [(0, 1), (1, 0), (2, 3), (3, 2)]
    x_route = [(0, 2), (2, 0), (1, 3), (3, 1)]
    z_route = [(i, i ^ 1) for i in range(pieces)]

    def fetch(shard, axis):
        if not special:
            return [lax.all_gather(shard, "dp", axis=axis, tiled=True)]
        n = shard.shape[axis] // 2
        mine = lax.dynamic_slice_in_dim(shard, zb * n, n, axis)
        over_x = lax.ppermute(mine, "dp", x_route)
        over_z = lax.ppermute(over_x, "ctx", z_route)
        return [
            shard,
            lax.ppermute(shard, "dp", core_route),
            over_x,
            over_z,
            lax.ppermute(over_x, "dp", core_route),
            lax.ppermute(over_z, "dp", core_route),
        ]

    span = tok_count // CHUNKS
    nb = groups // CHUNKS
    x_own = [block_input[i * span : (i + 1) * span] for i in range(CHUNKS)]
    g_own = [cotangent[i * span : (i + 1) * span] for i in range(CHUNKS)]
    x_got = [swap_tensor(v) for v in x_own]

    in_shards = [fetch(in_weight[j], 0) for j in range(3)]
    out_shards = fetch(out_weight, 1)

    table = jnp.concatenate([deal_order[0], seq_lengths, seq_adapter])
    table = lax.all_gather(table, "dp", axis=0, tiled=False)
    deal_all = table[:, :groups]
    lengths_all = table[:, groups : groups + seqs]
    adapter_all = table[:, groups + seqs :]
    device_ids = jnp.arange(groups, dtype=jnp.int32)
    slot = jnp.sum(
        jnp.where(deal_all[:, :, None] == device_ids[None, None, :], device_ids[None, :, None], 0), axis=1
    )
    my_slot = jnp.sum(jnp.where(device_ids[None, :] == me, slot, 0), axis=1)

    x_blocks = block_input.reshape(groups, sub, half)
    g_blocks = cotangent.reshape(groups, sub, half)
    edges = jnp.concatenate([x_blocks[:, :2], g_blocks[:, :2], x_blocks[:, sub - 2 :]], axis=1)
    all_edges = lax.all_gather(edges, "dp", axis=0, tiled=False)
    slot_of = slot.T[:, :, None, None]
    want = my_slot[None, :, None, None]

    def pick(test, rows):
        return jnp.sum(jnp.where(test, rows.astype(f32), 0.0), axis=0).astype(bf16)

    heads, tails = all_edges[:, :, :4], all_edges[:, :, 4:]
    first_heads = pick(slot_of == 0, heads)
    last_tails = pick(slot_of == groups - 1, tails)
    from_next = lax.ppermute(first_heads, "ctx", [(i + 1, i) for i in range(pieces - 1)])
    from_prev = lax.ppermute(last_tails, "ctx", [(i, i + 1) for i in range(pieces - 1)])
    edge = my_slot[:, None, None]
    next_rows = jnp.where(edge == groups - 1, from_next, pick(slot_of == want + 1, heads))
    prev_rows = jnp.where(edge == 0, from_prev, pick(slot_of == want - 1, tails))
    halo_own = jnp.concatenate([next_rows, prev_rows], axis=1)
    halo_got = swap_tensor(halo_own)
    g_got = [swap_tensor(v) for v in g_own]

    gu_shards = [fetch(gateup_weight[j], 0) for j in range(2)]
    down_shards = fetch(down_weight, 1)

    in_first = relative(input_adapter_shrink, 0)
    out_second = relative(output_adapter_expand, 1)
    ffn_first = relative(ffn_shrink, 0)
    down_second = relative(down_adapter_expand, 1)
    mixer_f = relative(mixer_gain, 0).astype(f32)
    ffn_f = relative(ffn_gain, 0).astype(f32)
    conv_w = conv_taps.astype(f32)

    half_scale = jnp.asarray(adapter_scale, bf16)
    in_full = [jnp.concatenate([*in_shards[j], in_expand[j] * half_scale], axis=0) for j in range(3)]
    out_full = jnp.concatenate([*out_shards, out_shrink], axis=1)
    blank = jnp.zeros((rank_cols, gateup_weight.shape[2]), bf16)
    gu_full = [
        jnp.concatenate([*gu_shards[0], ffn_expand[0] * half_scale, blank], axis=0),
        jnp.concatenate([*gu_shards[1], blank, ffn_expand[1] * half_scale], axis=0),
    ]
    down_full = jnp.concatenate([*down_shards, down_shrink], axis=1)

    def full_rows(own, got):
        stack = jnp.concatenate([own, got], axis=1)
        return block_order(stack, 1, in_stack, sub_width)

    offsets = jnp.concatenate(
        [jnp.arange(sub + 2, dtype=jnp.int32), jnp.arange(-2, 0, dtype=jnp.int32)]
    )
    seq_ends = []
    total = jnp.zeros((groups,), jnp.int32)
    for i in range(seqs - 1):
        total = total + lengths_all[:, i]
        seq_ends.append(total)

    def segment_of(positions, ends):
        found = jnp.zeros(positions.shape, jnp.int32)
        for end in ends:
            found = found + (positions >= end[:, None]).astype(jnp.int32)
        return found

    chunk = []
    for i in range(CHUNKS):
        blocks = slice(i * nb, (i + 1) * nb)
        base = ctx * tok_count + my_slot[blocks] * sub
        positions = base[:, None] + offsets[None, :]
        ends = [end[blocks] for end in seq_ends]
        segment = segment_of(positions, ends)
        adapter = jnp.zeros(positions.shape, jnp.int32)
        for j in range(seqs):
            adapter = adapter + jnp.where(segment == j, adapter_all[blocks, j][:, None], 0)
        inside = positions < group_tokens
        same_one = (positions >= 1) & inside & (segment_of(positions - 1, ends) == segment)
        same_two = (positions >= 2) & inside & (segment_of(positions - 2, ends) == segment)
        same_one = same_one.astype(f32)[:, : sub + 2, None]
        same_two = same_two.astype(f32)[:, : sub + 2, None]

        def in_rows(array):
            tail = array.shape[2:]
            return jnp.concatenate(
                [
                    array[:, :sub].reshape((nb * sub,) + tail),
                    array[:, sub : sub + 2].reshape((nb * 2,) + tail),
                    array[:, sub + 2 :].reshape((nb * 2,) + tail),
                ],
                axis=0,
            )

        columns = jnp.arange(rank_cols, dtype=jnp.int32) // RANK
        adapter_rows = in_rows(adapter[:, :, None])
        mask = (columns[None, :] == adapter_rows).astype(bf16)

        def with_halo(main, halo, first):
            edge_rows = halo[blocks]
            nxt = edge_rows[:, first : first + 2].reshape(nb * 2, half)
            prv = edge_rows[:, 4:].reshape(nb * 2, half)
            return jnp.concatenate([main, nxt, prv], axis=0)

        x_full = full_rows(with_halo(x_own[i], halo_own, 0), with_halo(x_got[i], halo_got, 0))
        rows = nb * (sub + 2)
        g_full = full_rows(
            with_halo(g_own[i], halo_own, 2)[:rows], with_halo(g_got[i], halo_got, 2)[:rows]
        )
        chunk.append(dict(x=x_full, g=g_full, mask=mask, s1=same_one, s2=same_two))

    rows = nb * (sub + 2)
    main = nb * sub

    def blocked(array):
        return array[:main].reshape(nb, sub, -1), array[main:rows].reshape(nb, 2, -1)

    for c in chunk:
        x = c["x"].astype(f32)
        scale = rms_scale(x)
        normed = (x * scale * mixer_f).astype(bf16)
        low = dot(normed, in_first).astype(bf16) * c["mask"]
        lhs = jnp.concatenate([normed, low], axis=1)
        gate_b, gate_c, values = (dot(lhs, in_full[j]) for j in range(3))
        mixed = (gate_b * values).astype(bf16)
        mid, nxt = blocked(mixed)
        prv = mixed[rows:].reshape(nb, 2, -1)
        ext = jnp.concatenate([prv, mid, nxt], axis=1).astype(f32)
        conv = (
            conv_w[0] * ext[:, 2:]
            + conv_w[1] * ext[:, 1:-1] * c["s1"]
            + conv_w[2] * ext[:, :-2] * c["s2"]
        )
        conv = jnp.concatenate(
            [conv[:, :sub].reshape(main, -1), conv[:, sub:].reshape(rows - main, -1)], axis=0
        )
        gated = (gate_c[:rows] * conv).astype(bf16)
        part = dot(gated, out_full).astype(bf16)
        c.update(
            scale=scale[:rows], normed=normed, low=low, b=gate_b, c=gate_c[:rows], v=values,
            conv=conv, gated=gated, part=part, got=swap_tensor(part), m=c["mask"][:rows],
        )

    for c in chunk:
        both = c["part"].astype(f32) + c["got"].astype(f32)
        out_low = both[:, width:].astype(bf16) * c["m"]
        hidden = c["x"][:rows].astype(f32) + (both[:, :width] + adapter_scale * dot(out_low, out_second))
        scale = rms_scale(hidden)
        ffn_in = (hidden * scale * ffn_f).astype(bf16)
        m2 = jnp.concatenate([c["m"], c["m"]], axis=1)
        low = dot(ffn_in, ffn_first).astype(bf16) * m2
        lhs = jnp.concatenate([ffn_in, low], axis=1)
        gate, up = dot(lhs, gu_full[0]), dot(lhs, gu_full[1])
        sig = jax.nn.sigmoid(gate)
        act = (gate * sig * up).astype(bf16)
        g = c["g"]
        g_low = (adapter_scale * dot_nt(g, down_second)).astype(bf16) * c["m"]
        grad_act = dot_nt(jnp.concatenate([g, g_low], axis=1), down_full)
        gg = (grad_act * up * sig * (1.0 + gate * (1.0 - sig))).astype(bf16)
        gu = (grad_act * gate * sig).astype(bf16)
        part = (dot_nt(gg, gu_full[0]) + dot_nt(gu, gu_full[1])).astype(bf16)
        c.update(f_part=part, f_got=swap_tensor(part))
        down = dot(act[:main], down_full).astype(bf16)
        own = jnp.concatenate([own_half(down, 1), down[:, width:]], axis=1)
        send = jnp.concatenate([other_half(down, 1), down[:, width:]], axis=1)
        c.update(
            out_low=out_low, hidden=hidden, scale_two=scale, ffn_in=ffn_in, ffn_low=low, act=act,
            g_low=g_low, gg=gg, gu=gu, m2=m2, d_own=own, d_got=swap_tensor(send),
        )

    for c in chunk:
        both = c["f_part"].astype(f32) + c["f_got"].astype(f32)
        grad_low = both[:, width:].astype(bf16) * c["m2"]
        grad_in = both[:, :width] + dot_nt(grad_low, ffn_first)
        scale, hidden = c["scale_two"], c["hidden"]
        unit = hidden * scale
        grad_unit = grad_in * ffn_f
        grad_hidden = c["g"].astype(f32) + scale * (
            grad_unit - unit * jnp.mean(grad_unit * unit, axis=-1, keepdims=True)
        )
        branch = grad_hidden.astype(bf16)
        b_low = (adapter_scale * dot_nt(branch, out_second)).astype(bf16) * c["m"]
        grad_gated = dot_nt(jnp.concatenate([branch, b_low], axis=1), out_full)
        grad_c = grad_gated[:main] * c["conv"][:main]
        grad_conv = grad_gated * c["c"]
        mid, nxt = blocked(grad_conv)
        ext = jnp.concatenate([mid, nxt], axis=1)
        grad_mixed = (
            conv_w[0] * mid
            + conv_w[1] * (ext * c["s1"])[:, 1:-1]
            + conv_w[2] * (ext * c["s2"])[:, 2:]
        ).reshape(main, -1)
        proj = [
            (grad_mixed * c["v"][:main]).astype(bf16),
            grad_c.astype(bf16),
            (grad_mixed * c["b"][:main]).astype(bf16),
        ]
        part = sum(dot_nt(proj[j], in_full[j]) for j in range(3)).astype(bf16)
        x = c["x"][:main].astype(f32)
        unit = x * c["scale"][:main]
        stat = jnp.sum(part[:, :width].astype(f32) * (unit * mixer_f), axis=-1, keepdims=True)
        own = jnp.concatenate([own_half(part, 1), part[:, width:]], axis=1)
        send = jnp.concatenate([other_half(part, 1), part[:, width:]], axis=1)
        c.update(
            f_low=grad_low, grad_hidden=grad_hidden, branch=branch, b_low=b_low, proj=proj,
            n_own=own, n_got=swap_tensor(send), stat=stat, stat_got=swap_tensor(stat), unit=unit,
        )

    out_rows, grad_rows = [], []
    mixer_half = own_half(mixer_f, 0)
    for c in chunk:
        both = c["d_own"].astype(f32) + c["d_got"].astype(f32)
        down_low = both[:, half:].astype(bf16) * c["m"][:main]
        c["down_low"] = down_low
        hidden = own_half(c["hidden"], 1)[:main]
        rows_out = hidden + (
            both[:, :half] + adapter_scale * dot(down_low, own_half(down_second, 1))
        )
        out_rows.append(restored(rows_out.astype(bf16), 1))
        both = c["n_own"].astype(f32) + c["n_got"].astype(f32)
        grad_low = both[:, half:].astype(bf16) * c["m"][:main]
        c["n_low"] = grad_low
        added = dot_nt(grad_low, in_first)
        stat = (
            c["stat"]
            + c["stat_got"]
            + jnp.sum(added * (c["unit"] * mixer_f), axis=-1, keepdims=True)
        ) / width
        grad_unit = (both[:, :half] + own_half(added, 1)) * mixer_half
        grad_x = own_half(c["grad_hidden"], 1)[:main] + c["scale"][:main] * (
            grad_unit - own_half(c["unit"], 1) * stat
        )
        grad_rows.append(restored(grad_x, 1))
    block_output = jnp.concatenate(out_rows, axis=0)
    input_grad = jnp.concatenate(grad_rows, axis=0)

    def over_rows(left, right):
        return sum(dot_tn(left(c)[:main], right(c)[:main]) for c in chunk)

    def reduced(*parts):
        return lax.psum(tuple(p.astype(bf16) for p in parts), ("dp", "ctx"))

    def joined(part, axis):
        got = swap_tensor(part)
        first = jnp.where(tens == 0, part, got)
        second = jnp.where(tens == 0, got, part)
        return jnp.concatenate([first, second], axis=axis).astype(f32)

    down_first_grad = over_rows(lambda c: c["act"], lambda c: c["g_low"])
    down_second_grad = adapter_scale * over_rows(
        lambda c: c["down_low"], lambda c: own_half(c["g"], 1)
    )
    ffn_second_grad = [
        adapter_scale
        * over_rows(lambda c: c["ffn_low"][:, j * rank_cols : (j + 1) * rank_cols], lambda c: c[k])
        for j, k in enumerate(("gg", "gu"))
    ]
    early = reduced(
        down_first_grad, restored(down_second_grad, 1), ffn_second_grad[0], ffn_second_grad[1]
    )
    ffn_first_grad = over_rows(lambda c: own_half(c["ffn_in"], 1), lambda c: c["f_low"])
    out_first_grad = over_rows(lambda c: c["gated"], lambda c: c["b_low"])
    out_second_grad = adapter_scale * over_rows(
        lambda c: c["out_low"], lambda c: own_half(c["branch"], 1)
    )
    middle = reduced(restored(ffn_first_grad, 0), out_first_grad, restored(out_second_grad, 1))
    in_second_grad = [
        adapter_scale * over_rows(lambda c: c["low"], lambda c: c["proj"][j]) for j in range(3)
    ]
    in_first_grad = over_rows(lambda c: own_half(c["normed"], 1), lambda c: c["n_low"])
    late = reduced(*in_second_grad, restored(in_first_grad, 0))
    return (
        block_output,
        input_grad,
        joined(late[3], 0),
        jnp.stack(late[:3], axis=0).astype(f32),
        middle[1].astype(f32),
        joined(middle[2], 1),
        joined(middle[0], 0),
        jnp.stack(early[2:], axis=0).astype(f32),
        early[0].astype(f32),
        joined(early[1], 1),
    )


def solution(mesh):
    placed = (
        P(("dp", "ctx"), "tensor"),
        P(("dp", "ctx"), "tensor"),
        P("dp", None),
        P("dp"),
        P("dp"),
        P(),
        P(),
        P(None, "tensor"),
        P(None, "dp", "tensor"),
        P("tensor", "dp"),
        P(None, "dp", "tensor"),
        P("tensor", "dp"),
        P(),
        P(None, None, "tensor"),
        P("tensor", None),
        P(),
        P(),
        P(None, None, "tensor"),
        P("tensor", None),
        P(),
    )
    return jax.shard_map(
        body,
        mesh=mesh,
        in_specs=placed,
        out_specs=(
            P(("dp", "ctx"), "tensor"),
            P(("dp", "ctx"), "tensor"),
            P(),
            P(None, None, "tensor"),
            P("tensor", None),
            P(),
            P(),
            P(None, None, "tensor"),
            P("tensor", None),
            P(),
        ),
        check_vma=False,
    )
```

```python
import functools

import jax
import jax.numpy as jnp
from jax import lax
from jax.experimental import pallas as pl
from jax.experimental.pallas import tpu as pltpu
from jax.sharding import PartitionSpec as P

RANK = 16
CHUNKS = 2
TILE = 256
VMEM_BYTES = 56 * 1024 * 1024

norm_eps = 1e-05
adapter_scale = 0.5

f32 = jnp.float32
bf16 = jnp.bfloat16


def dot(left, right):
    return jnp.dot(left, right, preferred_element_type=f32)


def dot_nt(left, right):
    return lax.dot_general(left, right, (((1,), (1,)), ((), ())), preferred_element_type=f32)


def dot_tn(left, right):
    return lax.dot_general(left, right, (((0,), (0,)), ((), ())), preferred_element_type=f32)


def over_row_blocks(rows, step, visit):
    def one(i, carry):
        visit(pl.ds(pl.multiple_of(i * step, step), step))
        return carry

    lax.fori_loop(0, rows // step, one, 0)


def lanes_at(index, width):
    return pl.ds(pl.multiple_of(index * width, width), width)


def call(kernel, grid, scalars, ins, outs, scratch=(), flops=0):
    in_specs = []
    for array, block, index in ins:
        if block is None:
            zeros = (0,) * array.ndim
            in_specs.append(
                pl.BlockSpec(array.shape, lambda *_, z=zeros: z, pipeline_mode=pl.Buffered(1))
            )
        else:
            in_specs.append(pl.BlockSpec(block, index))
    out_specs, out_shape = [], []
    for shape, dtype, block, index in outs:
        zeros = (0,) * len(shape)
        out_specs.append(
            pl.BlockSpec(shape, lambda *_, z=zeros: z) if block is None else pl.BlockSpec(block, index)
        )
        out_shape.append(jax.ShapeDtypeStruct(shape, dtype))
    moved = sum(a.size * a.dtype.itemsize for a, _, _ in ins)
    return pl.pallas_call(
        kernel,
        grid_spec=pltpu.PrefetchScalarGridSpec(
            num_scalar_prefetch=len(scalars),
            grid=grid,
            in_specs=in_specs,
            out_specs=out_specs,
            scratch_shapes=list(scratch),
        ),
        out_shape=out_shape,
        compiler_params=pltpu.CompilerParams(
            dimension_semantics=("arbitrary",) * len(grid), vmem_limit_bytes=VMEM_BYTES
        ),
        cost_estimate=pl.CostEstimate(flops=flops, transcendentals=0, bytes_accessed=moved),
    )(*scalars, *[a for a, _, _ in ins])


def tables_kernel(dims, table, info, mask_ref, one_ref, two_ref):
    groups, seqs, sub, nb, rows, tok_count, group_tokens = dims
    chunk = pl.program_id(0)
    me, ctx = info[0], info[1]
    span = nb * sub
    row = lax.broadcasted_iota(jnp.int32, (rows, 128), 0)
    col = lax.broadcasted_iota(jnp.int32, (rows, 128), 1)
    far = jnp.full((rows, 128), -9, jnp.int32)
    pos, first_src, second_src = far, far, far
    ends = [far] * (seqs - 1)
    names = [far] * seqs
    for b in range(nb):
        group = chunk * nb + b
        slot = jnp.int32(0)
        for s in range(groups):
            slot = slot + jnp.where(table[group, s] == me, s, 0)
        base = ctx * tok_count + slot * sub
        low, top = b * sub, (b + 1) * sub
        edge = span + 4 * b
        inner = (row >= low) & (row < top)
        before = (row >= edge) & (row < edge + 2)
        after = (row >= edge + 2) & (row < edge + 4)
        here = inner | before | after
        pos = jnp.where(inner, base + row - low, pos)
        pos = jnp.where(before, base - 2 + row - edge, pos)
        pos = jnp.where(after, base + sub + row - (edge + 2), pos)
        first_src = jnp.where(inner, jnp.where(row == low, edge + 1, row - 1), first_src)
        first_src = jnp.where(after, jnp.where(row == edge + 2, top - 1, row - 1), first_src)
        second_src = jnp.where(inner, jnp.where(row < low + 2, edge + row - low, row - 2), second_src)
        second_src = jnp.where(after, top - 2 + row - (edge + 2), second_src)
        end = jnp.int32(0)
        for j in range(seqs - 1):
            end = end + table[group, groups + j]
            ends[j] = jnp.where(here, end, ends[j])
        for j in range(seqs):
            names[j] = jnp.where(here, table[group, groups + seqs + j], names[j])

    def segment_of(positions):
        found = jnp.zeros((rows, 128), jnp.int32)
        for end in ends:
            found = found + jnp.where(positions >= end, 1, 0)
        return found

    segment = segment_of(pos)
    adapter = names[0]
    for j in range(1, seqs):
        adapter = jnp.where(segment == j, names[j], adapter)
    picked = (col >= adapter * RANK) & (col < adapter * RANK + RANK)
    mask_ref[...] = jnp.where(picked, 1.0, 0.0).astype(bf16)
    source = lax.broadcasted_iota(jnp.int32, (rows, rows), 1)
    for lag, src, ref in ((1, first_src, one_ref), (2, second_src, two_ref)):
        same = (pos >= lag) & (pos < group_tokens) & (segment_of(pos - lag) == segment)
        src = jnp.where(same, src, -9)
        ref[...] = jnp.where(source == src[:, :1], 1.0, 0.0).astype(bf16)


def edges_kernel(dims, table, info, edges_ref, first_ref, last_ref, next_ref, prev_ref):
    groups = dims
    me = info[0]
    for g in range(groups):
        slot = jnp.int32(0)
        for s in range(groups):
            slot = slot + jnp.where(table[g, s] == me, s, 0)
        first_ref[g] = edges_ref[table[g, 0], g, 0:4]
        last_ref[g] = edges_ref[table[g, groups - 1], g, 4:6]
        after = table[g, jnp.minimum(slot + 1, groups - 1)]
        before = table[g, jnp.maximum(slot - 1, 0)]
        rows = edges_ref[after, g, 0:4]
        next_ref[g] = jnp.where(slot < groups - 1, rows, jnp.zeros_like(rows))
        rows = edges_ref[before, g, 4:6]
        prev_ref[g] = jnp.where(slot > 0, rows, jnp.zeros_like(rows))


ACTUAL, STACK, INNER = 4, 12, 20


def stack_rows(info, own, got, halo_own, halo_got, stack, span, half, into):
    block = half // 4
    stack[:span, :half] = own[...]
    stack[:span, half:] = got[...]
    stack[span:, :half] = halo_own[...]
    stack[span:, half:] = halo_got[...]
    for r in range(8):
        into[:, r * block : (r + 1) * block] = stack[:, lanes_at(info[STACK + r], block)]


def input_kernel(info, own, got, halo_own, halo_got, gain, first, mask, x_ref, lhs_ref, scale_ref, stack, first_rel, gain_rel):
    span, half = own.shape
    rows, width = x_ref.shape
    block = half // 4
    stack_rows(info, own, got, halo_own, halo_got, stack, span, half, x_ref)
    for r in range(8):
        first_rel[r * block : (r + 1) * block, :] = first[lanes_at(info[ACTUAL + r], block), :]
        gain_rel[:, r * block : (r + 1) * block] = gain[:, lanes_at(info[ACTUAL + r], block)]

    def visit(at):
        x = x_ref[at, :].astype(f32)
        scale = lax.rsqrt(jnp.mean(x * x, axis=-1, keepdims=True) + norm_eps)
        lhs_ref[at, :width] = (x * scale * gain_rel[0:1, :]).astype(bf16)
        scale_ref[at, :] = jnp.broadcast_to(scale, (scale.shape[0], 128))

    over_row_blocks(rows, 16, visit)
    lhs_ref[:, width:] = dot(lhs_ref[:, :width], first_rel[...]).astype(bf16) * mask[...]


def cotangent_kernel(info, own, got, halo_own, halo_got, second, mask, lhs_ref, stack, second_rel):
    span, half = own.shape
    width = 2 * half
    block = half // 4
    stack_rows(info, own, got, halo_own, halo_got, stack, span, half, lhs_ref)
    for r in range(8):
        second_rel[:, r * block : (r + 1) * block] = second[:, lanes_at(info[ACTUAL + r], block)]
    low = adapter_scale * dot_nt(lhs_ref[:, :width], second_rel[...])
    lhs_ref[:, width:] = low.astype(bf16) * mask[...]


def mixer_kernel(cuts, lhs, one, two, taps, in_expand, out_shrink, *refs):
    count = len(cuts)
    in_parts, out_parts = refs[:count], refs[count : 2 * count]
    b_ref, c_ref, v_ref, conv_ref, gated_ref, part_ref, acc = refs[2 * count :]
    width = cuts[-1][1]
    step = pl.program_id(0)

    def project(j):
        total = dot(lhs[:, width:], in_expand[j] * jnp.asarray(adapter_scale, bf16))
        for (low, top), part in zip(cuts, in_parts):
            total = total + dot(lhs[:, low:top], part[j])
        return total

    b, c, v = project(0), project(1), project(2)
    b_ref[...] = b
    c_ref[...] = c
    v_ref[...] = v
    mixed = (b * v).astype(bf16)
    w = taps[...].astype(f32)
    conv = w[0:1] * mixed.astype(f32) + w[1:2] * dot(one[...], mixed) + w[2:3] * dot(two[...], mixed)
    conv_ref[...] = conv
    gated = (c * conv).astype(bf16)
    gated_ref[...] = gated

    @pl.when(step == 0)
    def _():
        acc[...] = jnp.zeros_like(acc)

    for (low, top), part in zip(cuts, out_parts):
        acc[:, low:top] += dot(gated, part[...])
    acc[:, width:] += dot(gated, out_shrink[...])

    @pl.when(step == pl.num_programs(0) - 1)
    def _():
        part_ref[...] = acc[...].astype(bf16)


def feed_kernel(cuts, span, info, x, part, got, glhs, mask, gain, out_second, ffn_first, ffn_expand, down_shrink, *refs):
    count = len(cuts)
    gu_parts, down_parts = refs[:count], refs[count : 2 * count]
    (f_ref, own_ref, send_ref, hidden_ref, lhs, low_ref, grads,
     acc_d, acc_f, first_rel, second_rel, gain_rel) = refs[2 * count :]
    width = cuts[-1][1]
    half = width // 2
    block = width // 8
    rank = mask.shape[1]
    step = pl.program_id(0)

    @pl.when(step == 0)
    def _():
        for r in range(8):
            at = lanes_at(info[ACTUAL + r], block)
            here = slice(r * block, (r + 1) * block)
            first_rel[here, :] = ffn_first[at, :]
            second_rel[:, here] = out_second[:, at]
            gain_rel[:, here] = gain[:, at]
        low = (part[:, width:].astype(f32) + got[:, width:].astype(f32)).astype(bf16) * mask[...]
        low_ref[...] = low
        acc_d[:, :width] = dot(low, second_rel[...])

        def visit(at):
            both = part[at, :width].astype(f32) + got[at, :width].astype(f32)
            hidden = x[at, :].astype(f32) + (both + adapter_scale * acc_d[at, :width])
            hidden_ref[at, :] = hidden
            scale = lax.rsqrt(jnp.mean(hidden * hidden, axis=-1, keepdims=True) + norm_eps)
            lhs[at, :width] = (hidden * scale * gain_rel[0:1, :]).astype(bf16)

        over_row_blocks(x.shape[0], 16, visit)
        low = dot(lhs[:, :width], first_rel[...]).astype(bf16)
        lhs[:, width : width + rank] = low[:, :rank] * mask[...]
        lhs[:, width + rank :] = low[:, rank:] * mask[...]
        acc_d[...] = jnp.zeros_like(acc_d)
        acc_f[...] = jnp.zeros_like(acc_f)

    lows = [lhs[:, width : width + rank], lhs[:, width + rank :]]
    half_scale = jnp.asarray(adapter_scale, bf16)

    def project(j):
        total = dot(lows[j], ffn_expand[j] * half_scale)
        for (low, top), w in zip(cuts, gu_parts):
            total = total + dot(lhs[:, low:top], w[j])
        return total

    gate, up = project(0), project(1)
    sig = jax.nn.sigmoid(gate)
    silu = gate * sig
    act = (silu * up).astype(bf16)
    g_low = glhs[:, width:]
    grad_act = dot_nt(g_low, down_shrink[...])
    for (low, top), w in zip(cuts, down_parts):
        grad_act = grad_act + dot_nt(glhs[:, low:top], w[...])
    gg = (grad_act * up * (sig * (1.0 + gate * (1.0 - sig)))).astype(bf16)
    gu = (grad_act * silu).astype(bf16)
    for (low, top), w in zip(cuts, down_parts):
        acc_d[:span, low:top] += dot(act[:span], w[...])
    acc_d[:span, width:] += dot(act[:span], down_shrink[...])
    for (low, top), w in zip(cuts, gu_parts):
        acc_f[:, low:top] += dot_nt(gg, w[0]) + dot_nt(gu, w[1])
    acc_f[:, width : width + rank] += dot_nt(gg, ffn_expand[0] * half_scale)
    acc_f[:, width + rank :] += dot_nt(gu, ffn_expand[1] * half_scale)
    grads[0] = dot_tn(g_low[:span], act[:span])
    grads[1] = adapter_scale * dot_tn(lows[0][:span], gg[:span])
    grads[2] = adapter_scale * dot_tn(lows[1][:span], gu[:span])

    @pl.when(step == pl.num_programs(0) - 1)
    def _():
        f_ref[...] = acc_f[...].astype(bf16)
        place = info[3]
        own_ref[:, :half] = acc_d[:span, lanes_at(place, half)].astype(bf16)
        send_ref[:, :half] = acc_d[:span, lanes_at(1 - place, half)].astype(bf16)
        own_ref[:, half:] = acc_d[:span, width:].astype(bf16)
        send_ref[:, half:] = acc_d[:span, width:].astype(bf16)


def back_kernel(cuts, span, info, part, got, hidden, glhs, lhs_two, out_low, lhs_one, mask, gain, out_second, ffn_first,
                one, two, taps, in_expand, out_shrink, b_ref, c_ref, v_ref, conv_ref, gated_ref, *refs):
    count = len(cuts)
    in_parts, out_parts = refs[:count], refs[count : 2 * count]
    (own_ref, send_ref, gh_ref, ffn_grad, second_grad, grads,
     acc, branch, first_rel, second_rel, gain_rel) = refs[2 * count :]
    width = cuts[-1][1]
    half = width // 2
    block = width // 8
    rank = mask.shape[1]
    step = pl.program_id(0)
    place = info[3]

    @pl.when(step == 0)
    def _():
        for r in range(8):
            at = lanes_at(info[ACTUAL + r], block)
            here = slice(r * block, (r + 1) * block)
            first_rel[here, :] = ffn_first[at, :]
            second_rel[:, here] = out_second[:, at]
            gain_rel[:, here] = gain[:, at]
        low = (part[:, width:].astype(f32) + got[:, width:].astype(f32)).astype(bf16)
        low = jnp.concatenate([low[:, :rank] * mask[...], low[:, rank:] * mask[...]], axis=1)
        acc[:, :width] = dot_nt(low, first_rel[...])

        def visit(at):
            both = part[at, :width].astype(f32) + got[at, :width].astype(f32)
            h = hidden[at, :]
            scale = lax.rsqrt(jnp.mean(h * h, axis=-1, keepdims=True) + norm_eps)
            unit = h * scale
            grad_unit = (both + acc[at, :width]) * gain_rel[0:1, :]
            grad = glhs[at, :width].astype(f32) + scale * (
                grad_unit - unit * jnp.mean(grad_unit * unit, axis=-1, keepdims=True)
            )
            gh_ref[at, :] = grad
            branch[at, :width] = grad.astype(bf16)

        over_row_blocks(hidden.shape[0], 16, visit)
        b_low = adapter_scale * dot_nt(branch[:, :width], second_rel[...])
        branch[:, width:] = b_low.astype(bf16) * mask[...]
        for i in range(4):
            at = lanes_at(place * 4 + info[INNER + i], block)
            here = slice(i * block, (i + 1) * block)
            ffn_grad[:, here] = dot_tn(low[:span], lhs_two[:span, at])
            second_grad[:, here] = adapter_scale * dot_tn(out_low[:span, :], branch[:span, at])
        acc[...] = jnp.zeros_like(acc)

    total = dot_nt(branch[:, width:], out_shrink[...])
    for (low, top), w in zip(cuts, out_parts):
        total = total + dot_nt(branch[:, low:top], w[...])
    grad_c = total * conv_ref[...]
    conv = total * c_ref[...]
    w = taps[...].astype(f32)
    high = conv.astype(bf16)
    rest = (conv - high.astype(f32)).astype(bf16)
    mixed = (
        w[0:1] * conv
        + w[1:2] * (dot_tn(one[...], high) + dot_tn(one[...], rest))
        + w[2:3] * (dot_tn(two[...], high) + dot_tn(two[...], rest))
    )
    proj = [
        (mixed * v_ref[...]).astype(bf16)[:span],
        grad_c.astype(bf16)[:span],
        (mixed * b_ref[...]).astype(bf16)[:span],
    ]
    half_scale = jnp.asarray(adapter_scale, bf16)
    for (low, top), w in zip(cuts, in_parts):
        acc[:span, low:top] += dot_nt(proj[0], w[0]) + dot_nt(proj[1], w[1]) + dot_nt(proj[2], w[2])
    acc[:span, width:] += (
        dot_nt(proj[0], in_expand[0] * half_scale)
        + dot_nt(proj[1], in_expand[1] * half_scale)
        + dot_nt(proj[2], in_expand[2] * half_scale)
    )
    low_one = lhs_one[:span, width:]
    for j in range(3):
        grads[j] = adapter_scale * dot_tn(low_one, proj[j])
    grads[3] = dot_tn(branch[:span, width:], gated_ref[:span, :])

    @pl.when(step == pl.num_programs(0) - 1)
    def _():
        own_ref[:, :half] = acc[:span, lanes_at(place, half)].astype(bf16)
        send_ref[:, :half] = acc[:span, lanes_at(1 - place, half)].astype(bf16)
        own_ref[:, half : half + rank] = acc[:span, width:].astype(bf16)
        send_ref[:, half : half + rank] = acc[:span, width:].astype(bf16)

        def visit(at):
            sums = acc[at, :width].astype(bf16).astype(f32) * lhs_one[at, :width].astype(f32)
            stat = jnp.sum(sums, axis=-1, keepdims=True)
            high = stat.astype(bf16).astype(f32)
            middle = (stat - high).astype(bf16).astype(f32)
            rest = stat - high - middle
            lane = lax.broadcasted_iota(jnp.int32, (stat.shape[0], 128), 1)
            packed = jnp.where(lane == 0, high, jnp.where(lane == 1, middle, jnp.where(lane == 2, rest, 0.0)))
            own_ref[at, half + rank :] = packed.astype(bf16)
            send_ref[at, half + rank :] = packed.astype(bf16)

        over_row_blocks(span, 16, visit)


def final_kernel(width, info, n_own, n_got, nt_own, nt_got, d_own, d_got, dl_own, dl_got, hidden, gh, x, normed, low, scale, mask,
                 g, gain, in_first, down_second, out_ref, grad_ref, in_grad, down_grad):
    rank = mask.shape[1]
    sums = nt_own[...].astype(f32) + nt_got[...].astype(f32)
    n_low = sums[:, :rank].astype(bf16) * mask[...]
    stat = jnp.sum(sums[:, rank:], axis=-1, keepdims=True)
    stat = stat + jnp.sum(n_low.astype(f32) * low[...].astype(f32), axis=-1, keepdims=True)
    stat = stat / width
    scale_rows = scale[:, 0:1]
    unit = x[...].astype(f32) * scale_rows
    grad = n_own[...].astype(f32) + n_got[...].astype(f32) + dot_nt(n_low, in_first[...])
    grad_ref[...] = gh[...] + scale_rows * (grad * gain[0:1, :].astype(f32) - unit * stat)
    d_low = (dl_own[...].astype(f32) + dl_got[...].astype(f32)).astype(bf16) * mask[...]
    down = d_own[...].astype(f32) + d_got[...].astype(f32)
    out_ref[...] = (hidden[...] + (down + adapter_scale * dot(d_low, down_second[...]))).astype(bf16)
    in_grad[...] = dot_tn(n_low, normed[...])
    down_grad[...] = adapter_scale * dot_tn(d_low, g[...])


def swap_tensor(array):
    return lax.ppermute(array, "tensor", [(0, 1), (1, 0)])


def body(
    block_input,
    cotangent,
    deal_order,
    seq_lengths,
    seq_adapter,
    mixer_gain,
    ffn_gain,
    conv_taps,
    in_weight,
    out_weight,
    gateup_weight,
    down_weight,
    input_adapter_shrink,
    in_expand,
    out_shrink,
    output_adapter_expand,
    ffn_shrink,
    ffn_expand,
    down_shrink,
    down_adapter_expand,
):
    tok_count, half = block_input.shape
    width = 2 * half
    rank = input_adapter_shrink.shape[1]
    hidden_units = gateup_weight.shape[2]
    groups = lax.axis_size("dp")
    pieces = lax.axis_size("ctx")
    sub = tok_count // groups
    group_tokens = pieces * tok_count
    seqs = seq_lengths.shape[0]
    nb = groups // CHUNKS
    span = nb * sub
    halo = -(-4 * nb // 16) * 16
    rows = span + halo
    special = groups == 4 and pieces % 2 == 0
    me = lax.axis_index("dp")
    ctx = lax.axis_index("ctx")
    tens = lax.axis_index("tensor")
    if special:
        xb, cb, zb = me // 2, me % 2, ctx % 2
    else:
        xb = cb = zb = jnp.int32(0)
    flip = xb ^ tens

    actual, in_stack, inner = [], [], []
    for rx in (0, 1):
        for rc in (0, 1):
            for rh in (0, 1):
                low = (rc ^ cb) * 2 + (rh ^ (zb & rx))
                actual.append((rx ^ xb) * 4 + low)
                in_stack.append((rx ^ flip) * 4 + low)
    for bc in (0, 1):
        for bh in (0, 1):
            inner.append((bc ^ cb) * 2 + (bh ^ (zb & flip)))
    info = jnp.stack([me, ctx, tens, flip, *actual, *in_stack, *inner]).astype(jnp.int32)

    core_route = [(0, 1), (1, 0), (2, 3), (3, 2)]
    x_route = [(0, 2), (2, 0), (1, 3), (3, 1)]
    z_route = [(i, i ^ 1) for i in range(pieces)]

    def fetch(shard, axis):
        if not special:
            return [lax.all_gather(shard, "dp", axis=axis, tiled=True)]
        n = shard.shape[axis] // 2
        mine = lax.dynamic_slice_in_dim(shard, zb * n, n, axis)
        over_x = lax.ppermute(mine, "dp", x_route)
        over_z = lax.ppermute(over_x, "ctx", z_route)
        return [
            shard,
            lax.ppermute(shard, "dp", core_route),
            over_x,
            over_z,
            lax.ppermute(over_x, "dp", core_route),
            lax.ppermute(over_z, "dp", core_route),
        ]

    x_got = swap_tensor(block_input)
    in_parts = fetch(in_weight, 1)
    out_parts = fetch(out_weight, 1)
    if special:
        n = width // 8
        cuts = ((0, 2 * n), (2 * n, 4 * n), (4 * n, 5 * n), (5 * n, 6 * n), (6 * n, 7 * n), (7 * n, 8 * n))
    else:
        cuts = ((0, width),)

    table = jnp.concatenate([deal_order[0], seq_lengths, seq_adapter])
    table = lax.all_gather(table, "dp", axis=0, tiled=False)
    dims = (groups, seqs, sub, nb, rows, tok_count, group_tokens)
    per_chunk = lambda c, *_: (c, 0, 0)
    mask, one, two = call(
        functools.partial(tables_kernel, dims), (CHUNKS,), (table, info), [],
        [
            ((CHUNKS, rows, rank), bf16, (None, rows, rank), per_chunk),
            ((CHUNKS, rows, rows), bf16, (None, rows, rows), per_chunk),
            ((CHUNKS, rows, rows), bf16, (None, rows, rows), per_chunk),
        ],
    )
    x_blocks = block_input.reshape(groups, sub, half)
    g_blocks = cotangent.reshape(groups, sub, half)
    edges = jnp.concatenate([x_blocks[:, :2], g_blocks[:, :2], x_blocks[:, sub - 2 :]], axis=1)
    all_edges = lax.all_gather(edges, "dp", axis=0, tiled=False)
    first_heads, last_tails, next_near, prev_near = call(
        functools.partial(edges_kernel, groups), (1,), (table, info), [(all_edges, None, None)],
        [
            ((groups, 4, half), bf16, None, None),
            ((groups, 2, half), bf16, None, None),
            ((groups, 4, half), bf16, None, None),
            ((groups, 2, half), bf16, None, None),
        ],
    )
    from_next = lax.ppermute(first_heads, "ctx", [(i + 1, i) for i in range(pieces - 1)])
    from_prev = lax.ppermute(last_tails, "ctx", [(i, i + 1) for i in range(pieces - 1)])
    deal_all = table[:, :groups]
    at_end = (deal_all[:, groups - 1] == me)[:, None, None]
    at_start = (deal_all[:, 0] == me)[:, None, None]
    next_rows = jnp.where(at_end, from_next, next_near)
    prev_rows = jnp.where(at_start, from_prev, prev_near)
    halo_x = jnp.concatenate([prev_rows, next_rows[:, :2]], axis=1)
    halo_g = jnp.concatenate([jnp.zeros_like(prev_rows), next_rows[:, 2:]], axis=1)
    halo_own = jnp.stack([halo_x, halo_g]).reshape(2, CHUNKS, 4 * nb, half)
    halo_own = jnp.pad(halo_own, ((0, 0), (0, 0), (0, halo - 4 * nb), (0, 0)))
    halo_got = swap_tensor(halo_own)
    g_got = swap_tensor(cotangent)
    gu_parts = fetch(gateup_weight, 1)
    down_parts = fetch(down_weight, 1)

    gain_one, gain_two = mixer_gain[None, :].astype(f32), ffn_gain[None, :].astype(f32)
    ext_one, ext_two = width + rank, width + 2 * rank

    def stacked(array, last):
        return (array, (None,) + array.shape[1:], lambda c, *_: (c, 0, 0))

    def joined_inputs(own, got, which):
        def rows_of(array):
            return (array, (span, half), lambda c, *_: (c, 0))

        def halo_of(array):
            return (array, (None, None, halo, half), lambda c, *_: (which, c, 0, 0))

        return [rows_of(own), rows_of(got), halo_of(halo_own), halo_of(halo_got)]

    x_full, lhs_one, scale = call(
        input_kernel, (CHUNKS,), (info,),
        joined_inputs(block_input, x_got, 0)
        + [(gain_one, None, None), (input_adapter_shrink, None, None), stacked(mask, rank)],
        [
            ((CHUNKS, rows, width), bf16, (None, rows, width), per_chunk),
            ((CHUNKS, rows, ext_one), bf16, (None, rows, ext_one), per_chunk),
            ((CHUNKS, rows, 128), f32, (None, rows, 128), per_chunk),
        ],
        [
            pltpu.VMEM((rows, width), bf16),
            pltpu.VMEM((width, rank), bf16),
            pltpu.VMEM((1, width), f32),
        ],
    )
    (glhs,) = call(
        cotangent_kernel, (CHUNKS,), (info,),
        joined_inputs(cotangent, g_got, 1) + [(down_adapter_expand, None, None), stacked(mask, rank)],
        [((CHUNKS, rows, ext_one), bf16, (None, rows, ext_one), per_chunk)],
        [pltpu.VMEM((rows, width), bf16), pltpu.VMEM((rank, width), bf16)],
    )

    def picked(array, c):
        return (array, (None,) + array.shape[1:], lambda *_: (c, 0, 0))

    def columns(array):
        return (array, array.shape[:-1] + (TILE,), lambda h, *_: (0,) * (array.ndim - 1) + (h,))

    def row_tiles(array):
        return (array, (TILE, array.shape[1]), lambda h, *_: (h, 0))

    mixer_steps = half // TILE
    feed_steps = hidden_units // TILE
    column_out = lambda h, *_: (0, h)
    chunks = []
    for c in range(CHUNKS):
        gate_b, gate_c, values, conv, gated, part = call(
            functools.partial(mixer_kernel, cuts), (mixer_steps,), (),
            [picked(lhs_one, c), picked(one, c), picked(two, c), columns(conv_taps), columns(in_expand), row_tiles(out_shrink)]
            + [columns(w) for w in in_parts]
            + [row_tiles(w) for w in out_parts],
            [((rows, half), f32, (rows, TILE), column_out)] * 4
            + [((rows, half), bf16, (rows, TILE), column_out), ((rows, ext_one), bf16, None, None)],
            [pltpu.VMEM((rows, ext_one), f32)],
            flops=2 * rows * half * ext_one * 4,
        )
        chunks.append(dict(b=gate_b, c=gate_c, v=values, conv=conv, gated=gated, part=part))
    for c in chunks:
        c["got"] = swap_tensor(c["part"])

    for i, c in enumerate(chunks):
        f_part, d_own, d_send, hidden, lhs_two, out_low, grads = call(
            functools.partial(feed_kernel, cuts, span), (feed_steps,), (info,),
            [picked(x_full, i), (c["part"], None, None), (c["got"], None, None), picked(glhs, i), picked(mask, i),
             (gain_two, None, None), (output_adapter_expand, None, None), (ffn_shrink, None, None),
             columns(ffn_expand), row_tiles(down_shrink)]
            + [columns(w) for w in gu_parts]
            + [row_tiles(w) for w in down_parts],
            [
                ((rows, ext_two), bf16, None, None),
                ((span, half + rank), bf16, None, None),
                ((span, half + rank), bf16, None, None),
                ((rows, width), f32, None, None),
                ((rows, ext_two), bf16, None, None),
                ((rows, rank), bf16, None, None),
                ((3, rank, hidden_units), f32, (3, rank, TILE), lambda h, *_: (0, 0, h)),
            ],
            [
                pltpu.VMEM((rows, ext_one), f32),
                pltpu.VMEM((rows, ext_two), f32),
                pltpu.VMEM((width, 2 * rank), bf16),
                pltpu.VMEM((rank, width), bf16),
                pltpu.VMEM((1, width), f32),
            ],
            flops=2 * rows * hidden_units * ext_two * 6,
        )
        c.update(f_own=f_part, d_own=d_own, d_send=d_send, hidden=hidden, lhs=lhs_two, low=out_low, feed_grads=grads)
    for c in chunks:
        c["f_got"] = swap_tensor(c["f_own"])
    for c in chunks:
        c["d_got"] = swap_tensor(c["d_send"])

    sent = half + 2 * rank
    for i, c in enumerate(chunks):
        n_own, n_send, grad_hidden, ffn_grad, second_grad, grads = call(
            functools.partial(back_kernel, cuts, span), (mixer_steps,), (info,),
            [(c["f_own"], None, None), (c["f_got"], None, None), (c["hidden"], None, None), picked(glhs, i),
             (c["lhs"], None, None), (c["low"], None, None), picked(lhs_one, i), picked(mask, i),
             (gain_two, None, None), (output_adapter_expand, None, None), (ffn_shrink, None, None),
             picked(one, i), picked(two, i), columns(conv_taps), columns(in_expand), row_tiles(out_shrink),
             columns(c["b"]), columns(c["c"]), columns(c["v"]), columns(c["conv"]), columns(c["gated"])]
            + [columns(w) for w in in_parts]
            + [row_tiles(w) for w in out_parts],
            [
                ((span, sent), bf16, None, None),
                ((span, sent), bf16, None, None),
                ((rows, width), f32, None, None),
                ((2 * rank, half), f32, None, None),
                ((rank, half), f32, None, None),
                ((4, rank, half), f32, (4, rank, TILE), lambda h, *_: (0, 0, h)),
            ],
            [
                pltpu.VMEM((rows, ext_one), f32),
                pltpu.VMEM((rows, ext_one), bf16),
                pltpu.VMEM((width, 2 * rank), bf16),
                pltpu.VMEM((rank, width), bf16),
                pltpu.VMEM((1, width), f32),
            ],
            flops=2 * rows * half * ext_one * 4,
        )
        c.update(n_own=n_own, n_send=n_send, gh=grad_hidden, ffn_grad=ffn_grad, second_grad=second_grad, mixer_grads=grads)
    for c in chunks:
        c["n_got"] = swap_tensor(c["n_send"])

    block = half // 4
    in_half = lambda i, info: (0, info[INNER + i])
    in_full = lambda i, info: (0, info[3] * 4 + info[INNER + i])
    for k, c in enumerate(chunks):
        in_stack_full = lambda i, info, k=k: (k, 0, info[3] * 4 + info[INNER + i])
        tail = (span, rank)
        c["out"], c["grad"], c["in_grad"], c["down_grad"] = call(
            functools.partial(final_kernel, width), (4,), (info,),
            [
                (c["n_own"], (span, block), in_half),
                (c["n_got"], (span, block), in_half),
                (c["n_own"], (span, 2 * rank), lambda i, info: (0, half // (2 * rank))),
                (c["n_got"], (span, 2 * rank), lambda i, info: (0, half // (2 * rank))),
                (c["d_own"], (span, block), in_half),
                (c["d_got"], (span, block), in_half),
                (c["d_own"], tail, lambda i, info: (0, half // rank)),
                (c["d_got"], tail, lambda i, info: (0, half // rank)),
                (c["hidden"], (span, block), in_full),
                (c["gh"], (span, block), in_full),
                (x_full, (None, span, block), in_stack_full),
                (lhs_one, (None, span, block), in_stack_full),
                (lhs_one, (None,) + tail, lambda i, info, k=k: (k, 0, width // rank)),
                (scale, (None, span, 128), lambda i, info, k=k: (k, 0, 0)),
                (mask, (None,) + tail, lambda i, info, k=k: (k, 0, 0)),
                (glhs, (None, span, block), in_stack_full),
                (gain_one, (1, block), lambda i, info: (0, info[2] * 4 + i)),
                (input_adapter_shrink, (block, rank), lambda i, info: (info[2] * 4 + i, 0)),
                (down_adapter_expand, (rank, block), lambda i, info: (0, info[2] * 4 + i)),
            ],
            [
                ((span, half), bf16, (span, block), lambda i, info: (0, i)),
                ((span, half), f32, (span, block), lambda i, info: (0, i)),
                ((rank, half), f32, (rank, block), lambda i, info: (0, i)),
                ((rank, half), f32, (rank, block), lambda i, info: (0, i)),
            ],
        )
    block_output = jnp.concatenate([c["out"] for c in chunks], axis=0)
    input_grad = jnp.concatenate([c["grad"] for c in chunks], axis=0)

    def summed(name):
        return sum(c[name] for c in chunks).astype(bf16)

    def reduced(*parts):
        return lax.psum(parts, ("dp", "ctx"))

    def joined(part):
        got = swap_tensor(part)
        first = jnp.where(tens == 0, part, got)
        second = jnp.where(tens == 0, got, part)
        return jnp.concatenate([first, second], axis=1).astype(f32)

    feed, ffn_grad, second_grad, mixer, in_grad, down_grad = reduced(
        summed("feed_grads"), summed("ffn_grad"), summed("second_grad"), summed("mixer_grads"), summed("in_grad"), summed("down_grad")
    )
    return (
        block_output,
        input_grad,
        joined(in_grad).T,
        mixer[:3].astype(f32),
        mixer[3].astype(f32).T,
        joined(second_grad),
        joined(ffn_grad).T,
        feed[1:].astype(f32),
        feed[0].astype(f32).T,
        joined(down_grad),
    )


def solution(mesh):
    placed = (
        P(("dp", "ctx"), "tensor"),
        P(("dp", "ctx"), "tensor"),
        P("dp", None),
        P("dp"),
        P("dp"),
        P(),
        P(),
        P(None, "tensor"),
        P(None, "dp", "tensor"),
        P("tensor", "dp"),
        P(None, "dp", "tensor"),
        P("tensor", "dp"),
        P(),
        P(None, None, "tensor"),
        P("tensor", None),
        P(),
        P(),
        P(None, None, "tensor"),
        P("tensor", None),
        P(),
    )
    return jax.shard_map(
        body,
        mesh=mesh,
        in_specs=placed,
        out_specs=(
            P(("dp", "ctx"), "tensor"),
            P(("dp", "ctx"), "tensor"),
            P(),
            P(None, None, "tensor"),
            P("tensor", None),
            P(),
            P(),
            P(None, None, "tensor"),
            P("tensor", None),
            P(),
        ),
        check_vma=False,
    )
```

```python
import functools

import jax
import jax.numpy as jnp
from jax import lax
from jax.experimental import pallas as pl
from jax.experimental.pallas import tpu as pltpu
from jax.sharding import PartitionSpec as P

RANK = 16
CHUNKS = 2
TILE = 256
FEED_CUTS = ((0, 2), (2, 4), (4, 6), (6, 8), (8, 10), (10, 11))
VMEM_BYTES = 56 * 1024 * 1024

norm_eps = 1e-05
adapter_scale = 0.5

f32 = jnp.float32
bf16 = jnp.bfloat16


def dot(left, right):
    return jnp.dot(left, right, preferred_element_type=f32)


def dot_nt(left, right):
    return lax.dot_general(left, right, (((1,), (1,)), ((), ())), preferred_element_type=f32)


def dot_tn(left, right):
    return lax.dot_general(left, right, (((0,), (0,)), ((), ())), preferred_element_type=f32)


def over_row_blocks(rows, step, visit):
    def one(i, carry):
        visit(pl.ds(pl.multiple_of(i * step, step), step))
        return carry

    lax.fori_loop(0, rows // step, one, 0)


def lanes_at(index, width):
    return pl.ds(pl.multiple_of(index * width, width), width)


def call(kernel, grid, scalars, ins, outs, scratch=(), flops=0):
    in_specs = []
    for array, block, index in ins:
        if block is None:
            zeros = (0,) * array.ndim
            in_specs.append(
                pl.BlockSpec(array.shape, lambda *_, z=zeros: z, pipeline_mode=pl.Buffered(1))
            )
        else:
            in_specs.append(pl.BlockSpec(block, index))
    out_specs, out_shape = [], []
    for shape, dtype, block, index in outs:
        zeros = (0,) * len(shape)
        out_specs.append(
            pl.BlockSpec(shape, lambda *_, z=zeros: z) if block is None else pl.BlockSpec(block, index)
        )
        out_shape.append(jax.ShapeDtypeStruct(shape, dtype))
    moved = sum(a.size * a.dtype.itemsize for a, _, _ in ins)
    return pl.pallas_call(
        kernel,
        grid_spec=pltpu.PrefetchScalarGridSpec(
            num_scalar_prefetch=len(scalars),
            grid=grid,
            in_specs=in_specs,
            out_specs=out_specs,
            scratch_shapes=list(scratch),
        ),
        out_shape=out_shape,
        compiler_params=pltpu.CompilerParams(
            dimension_semantics=("arbitrary",) * len(grid), vmem_limit_bytes=VMEM_BYTES
        ),
        cost_estimate=pl.CostEstimate(flops=max(flops, 1), transcendentals=0, bytes_accessed=1),
    )(*scalars, *[a for a, _, _ in ins])


def tables_kernel(dims, table, info, mask_ref, one_ref, two_ref):
    groups, seqs, sub, nb, rows, tok_count, group_tokens = dims
    chunk = pl.program_id(0)
    me, ctx = info[0], info[1]
    span = nb * sub
    row = lax.broadcasted_iota(jnp.int32, (rows, 128), 0)
    col = lax.broadcasted_iota(jnp.int32, (rows, 128), 1)
    far = jnp.full((rows, 128), -9, jnp.int32)
    pos, first_src, second_src = far, far, far
    ends = [far] * (seqs - 1)
    names = [far] * seqs
    for b in range(nb):
        group = chunk * nb + b
        slot = jnp.int32(0)
        for s in range(groups):
            slot = slot + jnp.where(table[group, s] == me, s, 0)
        base = ctx * tok_count + slot * sub
        low, top = b * sub, (b + 1) * sub
        edge = span + 4 * b
        inner = (row >= low) & (row < top)
        before = (row >= edge) & (row < edge + 2)
        after = (row >= edge + 2) & (row < edge + 4)
        here = inner | before | after
        pos = jnp.where(inner, base + row - low, pos)
        pos = jnp.where(before, base - 2 + row - edge, pos)
        pos = jnp.where(after, base + sub + row - (edge + 2), pos)
        first_src = jnp.where(inner, jnp.where(row == low, edge + 1, row - 1), first_src)
        first_src = jnp.where(after, jnp.where(row == edge + 2, top - 1, row - 1), first_src)
        second_src = jnp.where(inner, jnp.where(row < low + 2, edge + row - low, row - 2), second_src)
        second_src = jnp.where(after, top - 2 + row - (edge + 2), second_src)
        end = jnp.int32(0)
        for j in range(seqs - 1):
            end = end + table[group, groups + j]
            ends[j] = jnp.where(here, end, ends[j])
        for j in range(seqs):
            names[j] = jnp.where(here, table[group, groups + seqs + j], names[j])

    def segment_of(positions):
        found = jnp.zeros((rows, 128), jnp.int32)
        for end in ends:
            found = found + jnp.where(positions >= end, 1, 0)
        return found

    segment = segment_of(pos)
    adapter = names[0]
    for j in range(1, seqs):
        adapter = jnp.where(segment == j, names[j], adapter)
    picked = (col >= adapter * RANK) & (col < adapter * RANK + RANK)
    mask_ref[...] = jnp.where(picked, 1.0, 0.0).astype(bf16)
    source = lax.broadcasted_iota(jnp.int32, (rows, rows), 1)
    for lag, src, ref in ((1, first_src, one_ref), (2, second_src, two_ref)):
        same = (pos >= lag) & (pos < group_tokens) & (segment_of(pos - lag) == segment)
        src = jnp.where(same, src, -9)
        ref[...] = jnp.where(source == src[:, :1], 1.0, 0.0).astype(bf16)


def edges_kernel(dims, table, info, edges_ref, first_ref, last_ref, next_ref, prev_ref):
    groups = dims
    me = info[0]
    for g in range(groups):
        slot = jnp.int32(0)
        for s in range(groups):
            slot = slot + jnp.where(table[g, s] == me, s, 0)
        first_ref[g] = edges_ref[table[g, 0], g, 0:4]
        last_ref[g] = edges_ref[table[g, groups - 1], g, 4:6]
        after = table[g, jnp.minimum(slot + 1, groups - 1)]
        before = table[g, jnp.maximum(slot - 1, 0)]
        rows = edges_ref[after, g, 0:4]
        next_ref[g] = jnp.where(slot < groups - 1, rows, jnp.zeros_like(rows))
        rows = edges_ref[before, g, 4:6]
        prev_ref[g] = jnp.where(slot > 0, rows, jnp.zeros_like(rows))


ACTUAL, STACK, INNER = 4, 12, 20


def stack_rows(info, own, got_first, got_second, halo_own, halo_got, stack, span, half, into):
    block = half // 4
    stack[:span, :half] = own[...]
    stack[:span, half:] = jnp.where(pl.program_id(0) == 0, got_first[...], got_second[...])
    stack[span:, :half] = halo_own[...]
    stack[span:, half:] = halo_got[...]
    for r in range(8):
        into[:, r * block : (r + 1) * block] = stack[:, lanes_at(info[STACK + r], block)]


def input_kernel(info, own, got_first, got_second, halo_own, halo_got, gain, first, mask, x_ref, lhs_ref, scale_ref, stack, first_rel, gain_rel):
    span, half = own.shape
    rows, width = x_ref.shape
    block = half // 4
    stack_rows(info, own, got_first, got_second, halo_own, halo_got, stack, span, half, x_ref)
    for r in range(8):
        first_rel[r * block : (r + 1) * block, :] = first[lanes_at(info[ACTUAL + r], block), :]
        gain_rel[:, r * block : (r + 1) * block] = gain[:, lanes_at(info[ACTUAL + r], block)]

    def visit(at):
        x = x_ref[at, :].astype(f32)
        scale = lax.rsqrt(jnp.mean(x * x, axis=-1, keepdims=True) + norm_eps)
        lhs_ref[at, :width] = (x * scale * gain_rel[0:1, :]).astype(bf16)
        scale_ref[at, :] = jnp.broadcast_to(scale, (scale.shape[0], 128))

    over_row_blocks(rows, 16, visit)
    lhs_ref[:, width:] = dot(lhs_ref[:, :width], first_rel[...]).astype(bf16) * mask[...]


def cotangent_kernel(info, own, got_first, got_second, halo_own, halo_got, second, mask, lhs_ref, stack, second_rel):
    span, half = own.shape
    width = 2 * half
    block = half // 4
    stack_rows(info, own, got_first, got_second, halo_own, halo_got, stack, span, half, lhs_ref)
    for r in range(8):
        second_rel[:, r * block : (r + 1) * block] = second[:, lanes_at(info[ACTUAL + r], block)]
    low = adapter_scale * dot_nt(lhs_ref[:, :width], second_rel[...])
    lhs_ref[:, width:] = low.astype(bf16) * mask[...]


def mixer_parts(refs, cuts):
    if len(cuts) == 1:
        return [[refs[0].at[j] for j in range(3)]], [refs[1]], refs[2:]
    ins = [[refs[0].at[k, j] for j in range(3)] for k in range(2)]
    outs = [refs[1].at[k] for k in range(2)]
    early = pl.program_id(0) < 2
    for k in range(4):
        first, second = refs[2 + 2 * k], refs[3 + 2 * k]
        tiles = [jnp.where(early, first[j], second[j]) for j in range(4)]
        ins.append(tiles[:3])
        outs.append(tiles[3])
    return ins, outs, refs[10:]


def mixer_kernel(cuts, lhs, one, two, taps, in_expand, out_shrink, *refs):
    in_parts, out_parts, refs = mixer_parts(refs, cuts)
    b_ref, c_ref, v_ref, conv_ref, gated_ref, part_first, part_second, acc = refs
    width = cuts[-1][1]
    step = pl.program_id(0)

    def project(j):
        total = dot(lhs[:, width:], in_expand[j] * jnp.asarray(adapter_scale, bf16))
        for (low, top), part in zip(cuts, in_parts):
            total = total + dot(lhs[:, low:top], part[j][...])
        return total

    b, c, v = project(0), project(1), project(2)
    b_ref[...] = b
    c_ref[...] = c
    v_ref[...] = v
    mixed = (b * v).astype(bf16)
    w = taps[...].astype(f32)
    conv = w[0:1] * mixed.astype(f32) + w[1:2] * dot(one[...], mixed) + w[2:3] * dot(two[...], mixed)
    conv_ref[...] = conv
    gated = (c * conv).astype(bf16)
    gated_ref[...] = gated

    @pl.when(step == 0)
    def _():
        acc[...] = jnp.zeros_like(acc)

    for (low, top), part in zip(cuts, out_parts):
        acc[:, low:top] += dot(gated, part[...])
    acc[:, width:] += dot(gated, out_shrink[...])

    @pl.when(step == pl.num_programs(0) - 1)
    def _():
        cut = part_first.shape[0]
        part_first[...] = acc[:cut, :].astype(bf16)
        part_second[...] = acc[cut:, :].astype(bf16)


def feed_kernel(cuts, span, info, x, part_first, part_second, got_first, got_second, glhs, mask, gain, out_second, ffn_first, ffn_expand, down_shrink, *refs):
    if len(cuts) == 1:
        gu_parts, down_parts, refs = [[refs[0].at[0], refs[0].at[1]]], [refs[1]], refs[2:]
    else:
        gu_parts = [[refs[0].at[k, j] for j in range(2)] for k in range(2)]
        down_parts = [refs[1].at[k] for k in range(2)]
        count = len(FEED_CUTS)
        far, refs = refs[2 : 2 + 4 * count], refs[2 + 4 * count :]
        here, refs = refs[-1], refs[:-1]
        for i, (low, top) in enumerate(FEED_CUTS):

            @pl.when((pl.program_id(0) >= low) & (pl.program_id(0) < top))
            def _(i=i):
                for k in range(4):
                    here[k] = far[k * count + i][...]

        for k in range(4):
            gu_parts.append([here.at[k, 0], here.at[k, 1]])
            down_parts.append(here.at[k, 2])
    (f_ref, own_ref, send_ref, hidden_ref, lhs, low_ref, grads,
     acc_d, acc_f, first_rel, second_rel, gain_rel) = refs
    width = cuts[-1][1]
    half = width // 2
    block = width // 8
    rank = mask.shape[1]
    step = pl.program_id(0)

    @pl.when(step == 0)
    def _():
        for r in range(8):
            at = lanes_at(info[ACTUAL + r], block)
            here = slice(r * block, (r + 1) * block)
            first_rel[here, :] = ffn_first[at, :]
            second_rel[:, here] = out_second[:, at]
            gain_rel[:, here] = gain[:, at]
        cut = part_first.shape[0]
        for own, got, base in ((part_first, got_first, 0), (part_second, got_second, cut)):
            n = own.shape[0]
            acc_d[base : base + n, :] = own[...].astype(f32) + got[...].astype(f32)
        low = acc_d[:, width:].astype(bf16) * mask[...]
        low_ref[...] = low
        acc_f[:, :width] = dot(low, second_rel[...])

        def visit(at):
            both = acc_d[at, :width]
            hidden = x[at, :].astype(f32) + (both + adapter_scale * acc_f[at, :width])
            hidden_ref[at, :] = hidden
            scale = lax.rsqrt(jnp.mean(hidden * hidden, axis=-1, keepdims=True) + norm_eps)
            lhs[at, :width] = (hidden * scale * gain_rel[0:1, :]).astype(bf16)

        over_row_blocks(x.shape[0], 16, visit)
        low = dot(lhs[:, :width], first_rel[...]).astype(bf16)
        lhs[:, width : width + rank] = low[:, :rank] * mask[...]
        lhs[:, width + rank :] = low[:, rank:] * mask[...]
        acc_d[...] = jnp.zeros_like(acc_d)
        acc_f[...] = jnp.zeros_like(acc_f)

    lows = [lhs[:, width : width + rank], lhs[:, width + rank :]]
    half_scale = jnp.asarray(adapter_scale, bf16)

    def project(j):
        total = dot(lows[j], ffn_expand[j] * half_scale)
        for (low, top), w in zip(cuts, gu_parts):
            total = total + dot(lhs[:, low:top], w[j][...])
        return total

    gate, up = project(0), project(1)
    sig = jax.nn.sigmoid(gate)
    silu = gate * sig
    act = (silu * up).astype(bf16)
    g_low = glhs[:, width:]
    grad_act = dot_nt(g_low, down_shrink[...])
    for (low, top), w in zip(cuts, down_parts):
        grad_act = grad_act + dot_nt(glhs[:, low:top], w[...])
    gg = (grad_act * up * (sig * (1.0 + gate * (1.0 - sig)))).astype(bf16)
    gu = (grad_act * silu).astype(bf16)
    for (low, top), w in zip(cuts, down_parts):
        acc_d[:span, low:top] += dot(act[:span], w[...])
    acc_d[:span, width:] += dot(act[:span], down_shrink[...])
    for (low, top), w in zip(cuts, gu_parts):
        acc_f[:, low:top] += dot_nt(gg, w[0][...]) + dot_nt(gu, w[1][...])
    acc_f[:, width : width + rank] += dot_nt(gg, ffn_expand[0] * half_scale)
    acc_f[:, width + rank :] += dot_nt(gu, ffn_expand[1] * half_scale)
    grads[0] = dot_tn(g_low[:span], act[:span])
    grads[1] = adapter_scale * dot_tn(lows[0][:span], gg[:span])
    grads[2] = adapter_scale * dot_tn(lows[1][:span], gu[:span])

    @pl.when(step == pl.num_programs(0) - 1)
    def _():
        f_ref[...] = acc_f[...].astype(bf16)
        place = info[3]
        own_ref[:, :half] = acc_d[:span, lanes_at(place, half)].astype(bf16)
        send_ref[:, :half] = acc_d[:span, lanes_at(1 - place, half)].astype(bf16)
        own_ref[:, half:] = acc_d[:span, width:].astype(bf16)
        send_ref[:, half:] = acc_d[:span, width:].astype(bf16)


def back_kernel(cuts, span, info, part, got, hidden, glhs, lhs_two, out_low, lhs_one, mask, gain, out_second, ffn_first,
                one, two, taps, in_expand, out_shrink, b_ref, c_ref, v_ref, conv_ref, gated_ref, *refs):
    in_parts, out_parts, refs = mixer_parts(refs, cuts)
    (own_ref, send_ref, rank_ref, gh_ref, ffn_grad, second_grad, grads,
     acc, branch, first_rel, second_rel, gain_rel) = refs
    width = cuts[-1][1]
    half = width // 2
    block = width // 8
    rank = mask.shape[1]
    step = pl.program_id(0)
    place = info[3]

    @pl.when(step == 0)
    def _():
        for r in range(8):
            at = lanes_at(info[ACTUAL + r], block)
            here = slice(r * block, (r + 1) * block)
            first_rel[here, :] = ffn_first[at, :]
            second_rel[:, here] = out_second[:, at]
            gain_rel[:, here] = gain[:, at]
        low = (part[:, width:].astype(f32) + got[:, width:].astype(f32)).astype(bf16)
        low = jnp.concatenate([low[:, :rank] * mask[...], low[:, rank:] * mask[...]], axis=1)
        acc[:, :width] = dot_nt(low, first_rel[...])

        def visit(at):
            both = part[at, :width].astype(f32) + got[at, :width].astype(f32)
            h = hidden[at, :]
            scale = lax.rsqrt(jnp.mean(h * h, axis=-1, keepdims=True) + norm_eps)
            unit = h * scale
            grad_unit = (both + acc[at, :width]) * gain_rel[0:1, :]
            grad = glhs[at, :width].astype(f32) + scale * (
                grad_unit - unit * jnp.mean(grad_unit * unit, axis=-1, keepdims=True)
            )
            gh_ref[at, :] = grad
            branch[at, :width] = grad.astype(bf16)

        over_row_blocks(hidden.shape[0], 16, visit)
        b_low = adapter_scale * dot_nt(branch[:, :width], second_rel[...])
        branch[:, width:] = b_low.astype(bf16) * mask[...]
        for i in range(4):
            at = lanes_at(place * 4 + info[INNER + i], block)
            here = slice(i * block, (i + 1) * block)
            ffn_grad[:, here] = dot_tn(low[:span], lhs_two[:span, at])
            second_grad[:, here] = adapter_scale * dot_tn(out_low[:span, :], branch[:span, at])
        acc[...] = jnp.zeros_like(acc)

    total = dot_nt(branch[:, width:], out_shrink[...])
    for (low, top), w in zip(cuts, out_parts):
        total = total + dot_nt(branch[:, low:top], w[...])
    grad_c = total * conv_ref[...]
    conv = total * c_ref[...]
    w = taps[...].astype(f32)
    high = conv.astype(bf16)
    rest = (conv - high.astype(f32)).astype(bf16)
    mixed = (
        w[0:1] * conv
        + w[1:2] * (dot_tn(one[...], high) + dot_tn(one[...], rest))
        + w[2:3] * (dot_tn(two[...], high) + dot_tn(two[...], rest))
    )
    proj = [
        (mixed * v_ref[...]).astype(bf16)[:span],
        grad_c.astype(bf16)[:span],
        (mixed * b_ref[...]).astype(bf16)[:span],
    ]
    half_scale = jnp.asarray(adapter_scale, bf16)
    for (low, top), w in zip(cuts, in_parts):
        acc[:span, low:top] += dot_nt(proj[0], w[0][...]) + dot_nt(proj[1], w[1][...]) + dot_nt(proj[2], w[2][...])
    acc[:span, width:] += (
        dot_nt(proj[0], in_expand[0] * half_scale)
        + dot_nt(proj[1], in_expand[1] * half_scale)
        + dot_nt(proj[2], in_expand[2] * half_scale)
    )
    low_one = lhs_one[:span, width:]
    for j in range(3):
        grads[j] = adapter_scale * dot_tn(low_one, proj[j])
    grads[3] = dot_tn(branch[:span, width:], gated_ref[:span, :])

    @pl.when(step == pl.num_programs(0) - 1)
    def _():
        own_ref[...] = acc[:span, lanes_at(place, half)].astype(bf16)
        send_ref[...] = acc[:span, lanes_at(1 - place, half)].astype(bf16)
        rank_ref[:, :rank] = acc[:span, width:].astype(bf16)

        def visit(at):
            sums = acc[at, :width].astype(bf16).astype(f32) * lhs_one[at, :width].astype(f32)
            stat = jnp.sum(sums, axis=-1, keepdims=True)
            high = stat.astype(bf16).astype(f32)
            middle = (stat - high).astype(bf16).astype(f32)
            rest = stat - high - middle
            lane = lax.broadcasted_iota(jnp.int32, (stat.shape[0], 128), 1)
            packed = jnp.where(lane == 0, high, jnp.where(lane == 1, middle, jnp.where(lane == 2, rest, 0.0)))
            rank_ref[at, rank:] = packed.astype(bf16)

        over_row_blocks(span, 16, visit)


def rank_rows(own, got, mask):
    rank = mask.shape[1]
    sums = own[...].astype(f32) + got[...].astype(f32)
    return sums[:, :rank].astype(bf16) * mask[...], sums[:, rank:]


def output_kernel(info, own, got, rank_own, rank_got, hidden, mask, g, second, out_ref, grad_ref):
    low, _ = rank_rows(rank_own, rank_got, mask)
    down = own[...].astype(f32) + got[...].astype(f32)
    out_ref[...] = (hidden[...] + (down + adapter_scale * dot(low, second[...]))).astype(bf16)
    grad_ref[...] = adapter_scale * dot_tn(low, g[...])


def rank_kernel(info, own, got, mask, normed, grad_ref):
    low, _ = rank_rows(own, got, mask)
    grad_ref[...] = dot_tn(low, normed[...])


def final_kernel(width, info, own, got, rank_own, rank_got, gh, x, low, scale, mask, gain, first, grad_ref):
    n_low, stat = rank_rows(rank_own, rank_got, mask)
    stat = jnp.sum(stat, axis=-1, keepdims=True)
    stat = stat + jnp.sum(n_low.astype(f32) * low[...].astype(f32), axis=-1, keepdims=True)
    stat = stat / width
    scale_rows = scale[:, 0:1]
    unit = x[...].astype(f32) * scale_rows
    grad = own[...].astype(f32) + got[...].astype(f32) + dot_nt(n_low, first[...])
    grad_ref[...] = gh[...] + scale_rows * (grad * gain[0:1, :].astype(f32) - unit * stat)


def after(array, *gates):
    return lax.optimization_barrier((array,) + gates)[0] if gates else array


def swap_tensor(array):
    return lax.ppermute(array, "tensor", [(0, 1), (1, 0)])


def body(
    block_input,
    cotangent,
    deal_order,
    seq_lengths,
    seq_adapter,
    mixer_gain,
    ffn_gain,
    conv_taps,
    in_weight,
    out_weight,
    gateup_weight,
    down_weight,
    input_adapter_shrink,
    in_expand,
    out_shrink,
    output_adapter_expand,
    ffn_shrink,
    ffn_expand,
    down_shrink,
    down_adapter_expand,
):
    tok_count, half = block_input.shape
    width = 2 * half
    rank = input_adapter_shrink.shape[1]
    hidden_units = gateup_weight.shape[2]
    groups = lax.axis_size("dp")
    pieces = lax.axis_size("ctx")
    sub = tok_count // groups
    group_tokens = pieces * tok_count
    seqs = seq_lengths.shape[0]
    nb = groups // CHUNKS
    span = nb * sub
    halo = -(-4 * nb // 16) * 16
    rows = span + halo
    special = groups == 4 and pieces % 2 == 0
    me = lax.axis_index("dp")
    ctx = lax.axis_index("ctx")
    tens = lax.axis_index("tensor")
    if special:
        xb, cb, zb = me // 2, me % 2, ctx % 2
    else:
        xb = cb = zb = jnp.int32(0)
    flip = xb ^ tens

    actual, in_stack, inner = [], [], []
    for rx in (0, 1):
        for rc in (0, 1):
            for rh in (0, 1):
                low = (rc ^ (cb & rx)) * 2 + (rh ^ (zb & rx))
                actual.append((rx ^ xb) * 4 + low)
                in_stack.append((rx ^ flip) * 4 + low)
    for bc in (0, 1):
        for bh in (0, 1):
            inner.append((bc ^ (cb & flip)) * 2 + (bh ^ (zb & flip)))
    info = jnp.stack([me, ctx, tens, flip, *actual, *in_stack, *inner]).astype(jnp.int32)

    core_route = [(0, 1), (1, 0), (2, 3), (3, 2)]
    x_route = [(0, 2), (2, 0), (1, 3), (3, 1)]
    z_route = [(i, i ^ 1) for i in range(pieces)]
    gates = []

    def wait(*values):
        gates[:] = values

    def begin(axis, route, array):
        return lax.ppermute(after(array, *gates), axis, route)

    def core(array):
        return begin("dp", core_route, array)

    def over_x(array):
        return begin("dp", x_route, array)

    def over_z(array):
        return begin("ctx", z_route, array)

    def over_y(array):
        return begin("tensor", [(0, 1), (1, 0)], array)

    def tiles_beside(array):
        tiles = array.reshape(-1, TILE, array.shape[1])
        return jnp.concatenate([tiles[i] for i in range(tiles.shape[0])], axis=1)

    def mixer_piece(k):
        at = slice(k * half // 2, (k + 1) * half // 2)
        return jnp.concatenate([mine(in_weight[:, :, at], 1), tiles_beside(mine(out_weight[at], 1))[None]], axis=0)

    def feed_piece(k):
        low, top = FEED_CUTS[k]
        at = slice(low * TILE, top * TILE)
        return jnp.concatenate([mine(gateup_weight[:, :, at], 1), tiles_beside(mine(down_weight[at], 1))[None]], axis=0)

    def chip_pair(array):
        return lax.all_gather(after(array, *gates), "dp", axis_index_groups=[[0, 1], [2, 3]])

    def mine(shard, axis):
        n = shard.shape[axis] // 2
        return lax.dynamic_slice_in_dim(shard, zb * n, n, axis)

    numbers = jnp.concatenate([deal_order[0], seq_lengths, seq_adapter])
    digits = jnp.concatenate([numbers // 64, numbers % 64]).astype(bf16)
    x_blocks = block_input.reshape(groups, sub, half)
    g_blocks = cotangent.reshape(groups, sub, half)
    digit_rows = jnp.zeros((groups, 2, half), bf16).at[0, 0, : digits.shape[0]].set(digits)
    edges = jnp.concatenate([x_blocks[:, :2], g_blocks[:, :2], x_blocks[:, sub - 2 :], digit_rows], axis=1)

    all_edges = lax.all_gather(edges, "dp", axis=0, tiled=False)
    digits = all_edges[:, 0, 6, : 2 * numbers.shape[0]].astype(jnp.int32)
    table = digits[:, : numbers.shape[0]] * 64 + digits[:, numbers.shape[0] :]
    dims = (groups, seqs, sub, nb, rows, tok_count, group_tokens)
    per_chunk = lambda c, *_: (c, 0, 0)
    mask, one, two = call(
        functools.partial(tables_kernel, dims), (CHUNKS,), (table, info), [],
        [
            ((CHUNKS, rows, rank), bf16, (None, rows, rank), per_chunk),
            ((CHUNKS, rows, rows), bf16, (None, rows, rows), per_chunk),
            ((CHUNKS, rows, rows), bf16, (None, rows, rows), per_chunk),
        ],
    )
    first_heads, last_tails, next_near, prev_near = call(
        functools.partial(edges_kernel, groups), (1,), (table, info), [(all_edges, None, None)],
        [
            ((groups, 4, half), bf16, None, None),
            ((groups, 2, half), bf16, None, None),
            ((groups, 4, half), bf16, None, None),
            ((groups, 2, half), bf16, None, None),
        ],
    )
    if special:
        in_own = chip_pair(in_weight)
        mixer_x, mixer_z, mixer_xc, mixer_zc = ([None] * 2 for _ in range(4))
        feed_x, feed_z, feed_xc, feed_zc = ([None] * len(FEED_CUTS) for _ in range(4))
        mixer_packed = [mixer_piece(k) for k in range(2)]
        feed_packed = [feed_piece(k) for k in range(len(FEED_CUTS))]
    wait(all_edges)
    x_got = [over_y(block_input[:span]), None]
    if special:
        mixer_x[0] = over_x(mixer_packed[0])
    from_next = begin("ctx", [(i + 1, i) for i in range(pieces - 1)], first_heads)
    from_prev = begin("ctx", [(i, i + 1) for i in range(pieces - 1)], last_tails)
    deal_all = table[:, :groups]
    at_end = (deal_all[:, groups - 1] == me)[:, None, None]
    at_start = (deal_all[:, 0] == me)[:, None, None]
    next_rows = jnp.where(at_end, from_next, next_near)
    prev_rows = jnp.where(at_start, from_prev, prev_near)
    halo_x = jnp.concatenate([prev_rows, next_rows[:, :2]], axis=1)
    halo_g = jnp.concatenate([jnp.zeros_like(prev_rows), next_rows[:, 2:]], axis=1)
    halo_own = jnp.stack([halo_x, halo_g]).reshape(2, CHUNKS, 4 * nb, half)
    halo_own = jnp.pad(halo_own, ((0, 0), (0, 0), (0, halo - 4 * nb), (0, 0)))
    stage = [from_next, from_prev, x_got[0]] + ([mixer_x[0], in_own, mixer_packed[1]] if special else [])
    wait(*stage)
    halo_got = over_y(halo_own)
    x_got[1] = over_y(block_input[span:])
    stage = [halo_got, x_got[1]]
    if special:
        mixer_x[1], mixer_z[0], mixer_xc[0] = over_x(mixer_packed[1]), over_z(mixer_x[0]), core(mixer_x[0])
        out_own = chip_pair(out_weight)
        stage += [mixer_x[1], mixer_z[0], mixer_xc[0], out_own, feed_packed[0]]
    wait(*stage)
    g_got = [over_y(cotangent[:span]), None]
    stage = [g_got[0]]
    if special:
        feed_x[0], mixer_z[1] = over_x(feed_packed[0]), over_z(mixer_x[1])
        mixer_xc[1], mixer_zc[0] = core(mixer_x[1]), core(mixer_z[0])
        gu_own = chip_pair(gateup_weight)
        stage += [feed_x[0], mixer_z[1], mixer_xc[1], mixer_zc[0], feed_packed[1]]

    gain_one, gain_two = mixer_gain[None, :].astype(f32), ffn_gain[None, :].astype(f32)
    ext_one, ext_two = width + rank, width + 2 * rank

    def stacked(array, last):
        return (array, (None,) + array.shape[1:], lambda c, *_: (c, 0, 0))

    def joined_inputs(own, got, which):
        def halo_of(array):
            return (array, (None, None, halo, half), lambda c, *_: (which, c, 0, 0))

        return [
            (own, (span, half), lambda c, *_: (c, 0)),
            (got[0], None, None),
            (got[1], None, None),
            halo_of(halo_own),
            halo_of(halo_got),
        ]

    x_full, lhs_one, scale = call(
        input_kernel, (CHUNKS,), (info,),
        joined_inputs(block_input, x_got, 0)
        + [(gain_one, None, None), (input_adapter_shrink, None, None), stacked(mask, rank)],
        [
            ((CHUNKS, rows, width), bf16, (None, rows, width), per_chunk),
            ((CHUNKS, rows, ext_one), bf16, (None, rows, ext_one), per_chunk),
            ((CHUNKS, rows, 128), f32, (None, rows, 128), per_chunk),
        ],
        [
            pltpu.VMEM((rows, width), bf16),
            pltpu.VMEM((width, rank), bf16),
            pltpu.VMEM((1, width), f32),
        ],
    )
    wait(*stage, lhs_one)
    g_got[1] = over_y(cotangent[span:])
    stage = [g_got[1]]
    if special:
        n = width // 8
        cuts = ((0, 2 * n), (2 * n, 4 * n), (4 * n, 5 * n), (5 * n, 6 * n), (6 * n, 7 * n), (7 * n, 8 * n))
        mixer_zc[1] = core(mixer_z[1])
        feed_x[1], feed_z[0], feed_xc[0] = over_x(feed_packed[1]), over_z(feed_x[0]), core(feed_x[0])
        stage += [feed_x[1], feed_z[0], feed_xc[0], feed_packed[2]]
        mixer_inputs = lambda: (
            [(in_own, (2, 3, in_own.shape[2], TILE), lambda h, *_: (0, 0, 0, h)),
             (out_own, (2, TILE, out_own.shape[2]), lambda h, *_: (0, h, 0))]
            + [(w, (4, TILE, TILE), (lambda h, *_: (0, 0, jnp.minimum(h, 1))) if i == 0 else (lambda h, *_: (0, 0, jnp.maximum(h - 2, 0))))
               for part in (mixer_x, mixer_z, mixer_xc, mixer_zc) for i, w in enumerate(part)]
        )
    else:
        cuts = ((0, width),)
        in_parts = [lax.all_gather(in_weight, "dp", axis=1, tiled=True)]
        out_parts = [lax.all_gather(out_weight, "dp", axis=1, tiled=True)]
        gu_parts = [lax.all_gather(gateup_weight, "dp", axis=1, tiled=True)]
        down_parts = [lax.all_gather(down_weight, "dp", axis=1, tiled=True)]
        mixer_inputs = lambda: [columns(in_parts[0]), row_tiles(out_parts[0])]

    def picked(array, c):
        return (array, (None,) + array.shape[1:], lambda *_: (c, 0, 0))

    def columns(array):
        return (array, array.shape[:-1] + (TILE,), lambda h, *_: (0,) * (array.ndim - 1) + (h,))

    def row_tiles(array):
        lead = array.ndim - 2
        return (array, array.shape[:lead] + (TILE, array.shape[-1]), lambda h, *_: (0,) * lead + (h, 0))

    def feed_step(k):
        count = len(FEED_CUTS)
        if k < count:
            feed_x[k] = over_x(feed_packed[k])
            stage.extend([feed_x[k]] + feed_packed[k + 1 : k + 2])
        if 0 <= k - 1 < count:
            feed_z[k - 1], feed_xc[k - 1] = over_z(feed_x[k - 1]), core(feed_x[k - 1])
            stage.extend([feed_z[k - 1], feed_xc[k - 1]])
        if 0 <= k - 2 < count:
            feed_zc[k - 2] = core(feed_z[k - 2])
            stage.append(feed_zc[k - 2])

    mixer_steps = half // TILE
    feed_steps = hidden_units // TILE
    column_out = lambda h, *_: (0, h)
    row_halves = (rows // 32 * 16, rows - rows // 32 * 16)
    chunks = []
    for c in range(CHUNKS):
        gate_b, gate_c, values, conv, gated, *part = call(
            functools.partial(mixer_kernel, cuts), (mixer_steps,), (),
            [picked(lhs_one, c), picked(one, c), picked(two, c), columns(conv_taps), columns(in_expand), row_tiles(out_shrink)]
            + mixer_inputs(),
            [((rows, half), f32, (rows, TILE), column_out)] * 4
            + [((rows, half), bf16, (rows, TILE), column_out)]
            + [((n, ext_one), bf16, None, None) for n in row_halves],
            [pltpu.VMEM((rows, ext_one), f32)],
            flops=2 * rows * half * ext_one * 4,
        )
        chunks.append(dict(b=gate_b, c=gate_c, v=values, conv=conv, gated=gated, part=part))
        if c == 0:
            wait(*stage, *part)
            chunks[0]["got"] = [over_y(part[0]), None]
            stage = [chunks[0]["got"][0]]
            if special:
                feed_step(2)
                down_own = chip_pair(down_weight)
    wait(*stage, *chunks[1]["part"])
    chunks[0]["got"][1] = over_y(chunks[0]["part"][1])
    stage = [chunks[0]["got"][1]]
    if special:
        feed_step(3)
    wait(*stage)
    chunks[1]["got"] = [over_y(chunks[1]["part"][0]), None]
    stage = [chunks[1]["got"][0]]
    if special:
        feed_step(4)
    (glhs,) = call(
        cotangent_kernel, (CHUNKS,), (info,),
        joined_inputs(cotangent, g_got, 1) + [(down_adapter_expand, None, None), stacked(mask, rank)],
        [((CHUNKS, rows, ext_one), bf16, (None, rows, ext_one), per_chunk)],
        [pltpu.VMEM((rows, width), bf16), pltpu.VMEM((rank, width), bf16)],
    )

    wait(*stage, glhs)
    chunks[1]["got"][1] = over_y(chunks[1]["part"][1])
    stage = []
    if special:
        feed_step(5)
        wait(*stage)
        stage = []
        feed_step(6)
        wait(*stage)
        feed_step(7)
        whole = [(gu_own, (2, 2, gu_own.shape[2], TILE), lambda h, *_: (0, 0, 0, h)),
                 (down_own, (2, TILE, down_own.shape[2]), lambda h, *_: (0, h, 0))]
        feed_inputs = whole + [
            (w, (3, TILE, TILE), lambda h, *_, low=low, top=top: (0, 0, jnp.clip(h - low, 0, top - low - 1)))
            for part in (feed_x, feed_z, feed_xc, feed_zc)
            for w, (low, top) in zip(part, FEED_CUTS)
        ]
    else:
        feed_inputs = [columns(gu_parts[0]), row_tiles(down_parts[0])]

    for i, c in enumerate(chunks):
        f_part, d_own, d_send, hidden, lhs_two, out_low, grads = call(
            functools.partial(feed_kernel, cuts, span), (feed_steps,), (info,),
            [picked(x_full, i)] + [(w, None, None) for w in (*c["part"], *c["got"])] + [picked(glhs, i), picked(mask, i),
             (gain_two, None, None), (output_adapter_expand, None, None), (ffn_shrink, None, None),
             columns(ffn_expand), row_tiles(down_shrink)]
            + feed_inputs,
            [
                ((rows, ext_two), bf16, None, None),
                ((span, half + rank), bf16, None, None),
                ((span, half + rank), bf16, None, None),
                ((rows, width), f32, None, None),
                ((rows, ext_two), bf16, None, None),
                ((rows, rank), bf16, None, None),
                ((3, rank, hidden_units), f32, (3, rank, TILE), lambda h, *_: (0, 0, h)),
            ],
            [
                pltpu.VMEM((rows, ext_one), f32),
                pltpu.VMEM((rows, ext_two), f32),
                pltpu.VMEM((width, 2 * rank), bf16),
                pltpu.VMEM((rank, width), bf16),
                pltpu.VMEM((1, width), f32),
            ]
            + ([pltpu.VMEM((4, 3, TILE, TILE), bf16)] if special else []),
            flops=2 * rows * hidden_units * ext_two * 6,
        )
        c.update(f_own=f_part, d_own=d_own, d_send=d_send, hidden=hidden, lhs=lhs_two, low=out_low, feed_grads=grads)
    def summed(name):
        return sum(c[name] for c in chunks).astype(bf16)

    def joined(own, got, axis):
        first = jnp.where(tens == 0, own, got)
        second = jnp.where(tens == 0, got, own)
        return jnp.concatenate([first, second], axis=axis)

    def take(array, i):
        return lax.dynamic_index_in_dim(array, i, 0, keepdims=False)

    def add(*terms):
        return sum(t.astype(f32) for t in terms).astype(bf16)

    core_bit, x_bit = me % 2, me // 2
    shifts = [[(i, (i + k) % pieces) for i in range(pieces)] for k in range(1, pieces)]

    def cut(arrays):
        return jnp.concatenate([a.reshape(-1, half) for a in arrays], axis=0).reshape(2, 2, pieces, -1, half)

    def scatter_core(total):
        return add(take(total, core_bit), lax.ppermute(take(total, 1 - core_bit), "dp", core_route))

    def scatter_x(total):
        return add(take(total, x_bit), lax.ppermute(take(total, 1 - x_bit), "dp", x_route))

    def scatter_z(total):
        sent = [lax.ppermute(take(total, (ctx + k) % pieces), "ctx", route) for k, route in enumerate(shifts, 1)]
        return add(take(total, ctx), *sent)

    def gather_z(total):
        got = [total] + [lax.ppermute(total, "ctx", route) for route in shifts]
        total = jnp.zeros((pieces,) + total.shape, bf16)
        for k, piece in enumerate(got):
            total = lax.dynamic_update_index_in_dim(total, piece, (ctx + pieces - k) % pieces, 0)
        return total

    def gather_pair(total, route, bit):
        got = lax.ppermute(total, "dp", route)
        return jnp.where(bit == 0, jnp.stack([total, got]), jnp.stack([got, total]))

    def gather_chip(total):
        return gather_pair(gather_pair(total, x_route, x_bit), core_route, core_bit)

    def both_halves(total, h):
        return total[:, : 2 * h].reshape(4 * pieces, 2, h, half).transpose(0, 2, 1, 3).reshape(-1, width)

    def plain(*arrays):
        return lax.psum(arrays, ("dp", "ctx"))

    for c in chunks:
        c["f_got"] = swap_tensor(c["f_own"])
    feed = summed("feed_grads")
    if special:
        feed_sum = scatter_core(cut([after(feed, chunks[0]["f_got"])]))
    for i, c in enumerate(chunks):
        f_got = after(c["f_got"], feed_sum) if special and i == 1 else c["f_got"]
        n_own, n_send, n_rank, grad_hidden, ffn_grad, second_grad, grads = call(
            functools.partial(back_kernel, cuts, span), (mixer_steps,), (info,),
            [(c["f_own"], None, None), (f_got, None, None), (c["hidden"], None, None), picked(glhs, i),
             (c["lhs"], None, None), (c["low"], None, None), picked(lhs_one, i), picked(mask, i),
             (gain_two, None, None), (output_adapter_expand, None, None), (ffn_shrink, None, None),
             picked(one, i), picked(two, i), columns(conv_taps), columns(in_expand), row_tiles(out_shrink),
             columns(c["b"]), columns(c["c"]), columns(c["v"]), columns(c["conv"]), columns(c["gated"])]
            + mixer_inputs(),
            [
                ((span, half), bf16, None, None),
                ((span, half), bf16, None, None),
                ((span, 2 * rank), bf16, None, None),
                ((rows, width), f32, None, None),
                ((2 * rank, half), f32, None, None),
                ((rank, half), f32, None, None),
                ((4, rank, half), f32, (4, rank, TILE), lambda h, *_: (0, 0, h)),
            ],
            [
                pltpu.VMEM((rows, ext_one), f32),
                pltpu.VMEM((rows, ext_one), bf16),
                pltpu.VMEM((width, 2 * rank), bf16),
                pltpu.VMEM((rank, width), bf16),
                pltpu.VMEM((1, width), f32),
            ],
            flops=2 * rows * half * ext_one * 4,
        )
        c.update(n_own=n_own, n_send=n_send, n_rank=n_rank, gh=grad_hidden, ffn_grad=ffn_grad, second_grad=second_grad, mixer_grads=grads)
        c["rank_got"] = swap_tensor(n_rank)
        c["n_got"] = swap_tensor(after(n_send, c["rank_got"]))
        if special:
            feed_sum = scatter_x(after(feed_sum, n_rank)) if i == 0 else scatter_z(after(feed_sum, n_rank))
    for c in chunks:
        c["d_got"] = swap_tensor(after(c["d_send"], chunks[0]["n_rank"]))

    block = half // 4
    in_half = lambda i, info: (0, info[INNER + i])
    in_full = lambda i, info: (0, info[3] * 4 + info[INNER + i])
    whole_block = lambda i, info: (0, 0)
    grad_out = ((rank, half), f32, (rank, block), lambda i, info: (0, i))
    for k, c in enumerate(chunks):
        in_stack_full = lambda i, info, k=k: (k, 0, info[3] * 4 + info[INNER + i])
        masks = (mask, (None, span, rank), lambda i, info, k=k: (k, 0, 0))
        ranks = [(c[name], (span, 2 * rank), whole_block) for name in ("n_rank", "rank_got")]
        d_got = after(c["d_got"], chunks[1]["n_rank"])
        c["out"], c["down_grad"] = call(
            output_kernel, (4,), (info,),
            [
                (c["d_own"], (span, block), in_half),
                (d_got, (span, block), in_half),
                (c["d_own"], (span, rank), lambda i, info: (0, half // rank)),
                (d_got, (span, rank), lambda i, info: (0, half // rank)),
                (c["hidden"], (span, block), in_full),
                masks,
                (glhs, (None, span, block), in_stack_full),
                (down_adapter_expand, (rank, block), lambda i, info: (0, info[2] * 4 + i)),
            ],
            [((span, half), bf16, (span, block), lambda i, info: (0, i)), grad_out],
        )
        (c["in_grad"],) = call(
            rank_kernel, (4,), (info,), ranks + [masks, (lhs_one, (None, span, block), in_stack_full)], [grad_out]
        )
        (c["grad"],) = call(
            functools.partial(final_kernel, width), (4,), (info,),
            [(c["n_own"], (span, block), in_half), (c["n_got"], (span, block), in_half)]
            + ranks
            + [
                (c["gh"], (span, block), in_full),
                (x_full, (None, span, block), in_stack_full),
                (lhs_one, (None, span, rank), lambda i, info, k=k: (k, 0, width // rank)),
                (scale, (None, span, 128), lambda i, info, k=k: (k, 0, 0)),
                masks,
                (gain_one, (1, block), lambda i, info: (0, info[2] * 4 + i)),
                (input_adapter_shrink, (block, rank), lambda i, info: (info[2] * 4 + i, 0)),
            ],
            [((span, half), f32, (span, block), lambda i, info: (0, i))],
        )
    block_output = jnp.concatenate([c["out"] for c in chunks], axis=0)
    input_grad = jnp.concatenate([c["grad"] for c in chunks], axis=0)

    if special:
        early_halves, early_others = [summed("ffn_grad"), summed("second_grad")], [summed("mixer_grads")]
        late_halves = [summed("in_grad"), summed("down_grad")]
        early = jnp.concatenate([cut(early_halves), cut(early_others)], axis=3)
        early = scatter_z(scatter_x(scatter_core(early)))
        late = scatter_z(scatter_x(scatter_core(cut(late_halves))))
        h = 3 * rank * half // (4 * pieces * half)
        early = jnp.concatenate([joined(early[:h], swap_tensor(early[:h]), 0), early[h:]], axis=0)
        late = joined(late, swap_tensor(late), 0)
        feed = gather_chip(gather_z(feed_sum)).reshape(feed.shape)
        early = gather_chip(gather_z(early)).reshape(4 * pieces, -1, half)
        late = gather_chip(gather_z(late)).reshape(4 * pieces, -1, half)
        both = both_halves(early, h)
        ffn_grad, second_grad = both[: 2 * rank], both[2 * rank :]
        mixer = early[:, 2 * h :].reshape(4, rank, half)
        both = both_halves(late, late.shape[1] // 2)
        in_grad, down_grad = both[:rank], both[rank:]
    else:
        feed, mixer, ffn_grad, second_grad, in_grad, down_grad = plain(
            feed, summed("mixer_grads"), summed("ffn_grad"), summed("second_grad"), summed("in_grad"), summed("down_grad")
        )
        ffn_grad, second_grad, in_grad, down_grad = (
            joined(v, swap_tensor(v), 1) for v in (ffn_grad, second_grad, in_grad, down_grad)
        )
    return (
        block_output,
        input_grad,
        in_grad.astype(f32).T,
        mixer[:3].astype(f32),
        mixer[3].astype(f32).T,
        second_grad.astype(f32),
        ffn_grad.astype(f32).T,
        feed[1:].astype(f32),
        feed[0].astype(f32).T,
        down_grad.astype(f32),
    )


def solution(mesh):
    placed = (
        P(("dp", "ctx"), "tensor"),
        P(("dp", "ctx"), "tensor"),
        P("dp", None),
        P("dp"),
        P("dp"),
        P(),
        P(),
        P(None, "tensor"),
        P(None, "dp", "tensor"),
        P("tensor", "dp"),
        P(None, "dp", "tensor"),
        P("tensor", "dp"),
        P(),
        P(None, None, "tensor"),
        P("tensor", None),
        P(),
        P(),
        P(None, None, "tensor"),
        P("tensor", None),
        P(),
    )
    return jax.shard_map(
        body,
        mesh=mesh,
        in_specs=placed,
        out_specs=(
            P(("dp", "ctx"), "tensor"),
            P(("dp", "ctx"), "tensor"),
            P(),
            P(None, None, "tensor"),
            P("tensor", None),
            P(),
            P(),
            P(None, None, "tensor"),
            P("tensor", None),
            P(),
        ),
        check_vma=False,
    )
```

```python
import functools

import jax
import jax.numpy as jnp
from jax import lax
from jax.experimental import pallas as pl
from jax.experimental.pallas import tpu as pltpu
from jax.sharding import PartitionSpec as P

RANK = 16
CHUNKS = 2
TILE = 256
FEED_CUTS = ((0, 2), (2, 4), (4, 6), (6, 8), (8, 10), (10, 11))
VMEM_BYTES = 56 * 1024 * 1024

norm_eps = 1e-05
adapter_scale = 0.5

f32 = jnp.float32
bf16 = jnp.bfloat16


def dot(left, right):
    return jnp.dot(left, right, preferred_element_type=f32)


def dot_nt(left, right):
    return lax.dot_general(left, right, (((1,), (1,)), ((), ())), preferred_element_type=f32)


def dot_tn(left, right):
    return lax.dot_general(left, right, (((0,), (0,)), ((), ())), preferred_element_type=f32)


def over_row_blocks(rows, step, visit):
    def one(i, carry):
        visit(pl.ds(pl.multiple_of(i * step, step), step))
        return carry

    lax.fori_loop(0, rows // step, one, 0)


def lanes_at(index, width):
    return pl.ds(pl.multiple_of(index * width, width), width)


def call(kernel, grid, scalars, ins, outs, scratch=(), flops=0, aliases=None):
    in_specs = []
    for array, block, index in ins:
        if block == "any":
            in_specs.append(pl.BlockSpec(memory_space=pl.ANY))
        elif block is None:
            zeros = (0,) * array.ndim
            in_specs.append(
                pl.BlockSpec(array.shape, lambda *_, z=zeros: z, pipeline_mode=pl.Buffered(1))
            )
        else:
            in_specs.append(pl.BlockSpec(block, index))
    out_specs, out_shape = [], []
    for shape, dtype, block, index in outs:
        zeros = (0,) * len(shape)
        out_specs.append(
            pl.BlockSpec(shape, lambda *_, z=zeros: z) if block is None else pl.BlockSpec(block, index)
        )
        out_shape.append(jax.ShapeDtypeStruct(shape, dtype))
    moved = sum(a.size * a.dtype.itemsize for a, _, _ in ins)
    return pl.pallas_call(
        kernel,
        grid_spec=pltpu.PrefetchScalarGridSpec(
            num_scalar_prefetch=len(scalars),
            grid=grid,
            in_specs=in_specs,
            out_specs=out_specs,
            scratch_shapes=list(scratch),
        ),
        out_shape=out_shape,
        input_output_aliases=aliases or {},
        compiler_params=pltpu.CompilerParams(
            dimension_semantics=("arbitrary",) * len(grid), vmem_limit_bytes=VMEM_BYTES
        ),
        cost_estimate=pl.CostEstimate(flops=max(flops, 1), transcendentals=0, bytes_accessed=1),
    )(*scalars, *[a for a, _, _ in ins])


def tables_kernel(dims, table, info, mask_ref, one_ref, two_ref):
    groups, seqs, sub, nb, rows, tok_count, group_tokens = dims
    chunk = pl.program_id(0)
    me, ctx = info[0], info[1]
    span = nb * sub
    row = lax.broadcasted_iota(jnp.int32, (rows, 128), 0)
    col = lax.broadcasted_iota(jnp.int32, (rows, 128), 1)
    far = jnp.full((rows, 128), -9, jnp.int32)
    pos, first_src, second_src = far, far, far
    ends = [far] * (seqs - 1)
    names = [far] * seqs
    for b in range(nb):
        group = chunk * nb + b
        slot = jnp.int32(0)
        for s in range(groups):
            slot = slot + jnp.where(table[group, s] == me, s, 0)
        base = ctx * tok_count + slot * sub
        low, top = b * sub, (b + 1) * sub
        edge = span + 4 * b
        inner = (row >= low) & (row < top)
        before = (row >= edge) & (row < edge + 2)
        after = (row >= edge + 2) & (row < edge + 4)
        here = inner | before | after
        pos = jnp.where(inner, base + row - low, pos)
        pos = jnp.where(before, base - 2 + row - edge, pos)
        pos = jnp.where(after, base + sub + row - (edge + 2), pos)
        first_src = jnp.where(inner, jnp.where(row == low, edge + 1, row - 1), first_src)
        first_src = jnp.where(after, jnp.where(row == edge + 2, top - 1, row - 1), first_src)
        second_src = jnp.where(inner, jnp.where(row < low + 2, edge + row - low, row - 2), second_src)
        second_src = jnp.where(after, top - 2 + row - (edge + 2), second_src)
        end = jnp.int32(0)
        for j in range(seqs - 1):
            end = end + table[group, groups + j]
            ends[j] = jnp.where(here, end, ends[j])
        for j in range(seqs):
            names[j] = jnp.where(here, table[group, groups + seqs + j], names[j])

    def segment_of(positions):
        found = jnp.zeros((rows, 128), jnp.int32)
        for end in ends:
            found = found + jnp.where(positions >= end, 1, 0)
        return found

    segment = segment_of(pos)
    adapter = names[0]
    for j in range(1, seqs):
        adapter = jnp.where(segment == j, names[j], adapter)
    picked = (col >= adapter * RANK) & (col < adapter * RANK + RANK)
    mask_ref[...] = jnp.where(picked, 1.0, 0.0).astype(bf16)
    source = lax.broadcasted_iota(jnp.int32, (rows, rows), 1)
    for lag, src, ref in ((1, first_src, one_ref), (2, second_src, two_ref)):
        same = (pos >= lag) & (pos < group_tokens) & (segment_of(pos - lag) == segment)
        src = jnp.where(same, src, -9)
        ref[...] = jnp.where(source == src[:, :1], 1.0, 0.0).astype(bf16)


def edges_kernel(dims, table, info, edges_ref, first_ref, last_ref, next_ref, prev_ref):
    groups = dims
    me = info[0]
    for g in range(groups):
        slot = jnp.int32(0)
        for s in range(groups):
            slot = slot + jnp.where(table[g, s] == me, s, 0)
        first_ref[g] = edges_ref[table[g, 0], g, 0:4]
        last_ref[g] = edges_ref[table[g, groups - 1], g, 4:6]
        after = table[g, jnp.minimum(slot + 1, groups - 1)]
        before = table[g, jnp.maximum(slot - 1, 0)]
        rows = edges_ref[after, g, 0:4]
        next_ref[g] = jnp.where(slot < groups - 1, rows, jnp.zeros_like(rows))
        rows = edges_ref[before, g, 4:6]
        prev_ref[g] = jnp.where(slot > 0, rows, jnp.zeros_like(rows))


ACTUAL, STACK, INNER = 4, 12, 20


def stack_rows(info, own, got_first, got_second, halo_own, halo_got, stack, span, half, into):
    block = half // 4
    stack[:span, :half] = own[...]
    stack[:span, half:] = jnp.where(pl.program_id(0) == 0, got_first[...], got_second[...])
    stack[span:, :half] = halo_own[...]
    stack[span:, half:] = halo_got[...]
    for r in range(8):
        into[:, r * block : (r + 1) * block] = stack[:, lanes_at(info[STACK + r], block)]


def input_kernel(info, own, got_first, got_second, halo_own, halo_got, gain, first, mask, x_ref, lhs_ref, scale_ref, stack, first_rel, gain_rel):
    span, half = own.shape
    rows, width = x_ref.shape
    block = half // 4
    stack_rows(info, own, got_first, got_second, halo_own, halo_got, stack, span, half, x_ref)
    for r in range(8):
        first_rel[r * block : (r + 1) * block, :] = first[lanes_at(info[ACTUAL + r], block), :]
        gain_rel[:, r * block : (r + 1) * block] = gain[:, lanes_at(info[ACTUAL + r], block)]

    def visit(at):
        x = x_ref[at, :].astype(f32)
        scale = lax.rsqrt(jnp.mean(x * x, axis=-1, keepdims=True) + norm_eps)
        lhs_ref[at, :width] = (x * scale * gain_rel[0:1, :]).astype(bf16)
        scale_ref[at, :] = jnp.broadcast_to(scale, (scale.shape[0], 128))

    over_row_blocks(rows, 16, visit)
    lhs_ref[:, width:] = dot(lhs_ref[:, :width], first_rel[...]).astype(bf16) * mask[...]


def cotangent_kernel(info, own, got_first, got_second, halo_own, halo_got, second, mask, lhs_ref, stack, second_rel):
    span, half = own.shape
    width = 2 * half
    block = half // 4
    stack_rows(info, own, got_first, got_second, halo_own, halo_got, stack, span, half, lhs_ref)
    for r in range(8):
        second_rel[:, r * block : (r + 1) * block] = second[:, lanes_at(info[ACTUAL + r], block)]
    low = adapter_scale * dot_nt(lhs_ref[:, :width], second_rel[...])
    lhs_ref[:, width:] = low.astype(bf16) * mask[...]


def mixer_parts(refs, cuts):
    if len(cuts) == 1:
        return [[refs[0].at[j] for j in range(3)]], [refs[1]], refs[2:]
    ins = [[refs[0].at[k, j] for j in range(3)] for k in range(2)]
    outs = [refs[1].at[k] for k in range(2)]
    early = pl.program_id(0) < 2
    for k in range(4):
        first, second = refs[2 + 2 * k], refs[3 + 2 * k]
        tiles = [jnp.where(early, first[j], second[j]) for j in range(4)]
        ins.append(tiles[:3])
        outs.append(tiles[3])
    return ins, outs, refs[10:]


def mixer_kernel(cuts, lhs, one, two, taps, in_expand, out_shrink, *refs):
    in_parts, out_parts, refs = mixer_parts(refs, cuts)
    b_ref, c_ref, v_ref, conv_ref, gated_ref, part_first, part_second, acc = refs
    width = cuts[-1][1]
    step = pl.program_id(0)

    def project(j):
        total = dot(lhs[:, width:], in_expand[j] * jnp.asarray(adapter_scale, bf16))
        for (low, top), part in zip(cuts, in_parts):
            total = total + dot(lhs[:, low:top], part[j][...])
        return total

    b, c, v = project(0), project(1), project(2)
    b_ref[...] = b
    c_ref[...] = c
    v_ref[...] = v
    mixed = (b * v).astype(bf16)
    w = taps[...].astype(f32)
    conv = w[0:1] * mixed.astype(f32) + w[1:2] * dot(one[...], mixed) + w[2:3] * dot(two[...], mixed)
    conv_ref[...] = conv
    gated = (c * conv).astype(bf16)
    gated_ref[...] = gated

    @pl.when(step == 0)
    def _():
        acc[...] = jnp.zeros_like(acc)

    for (low, top), part in zip(cuts, out_parts):
        acc[:, low:top] += dot(gated, part[...])
    acc[:, width:] += dot(gated, out_shrink[...])

    @pl.when(step == pl.num_programs(0) - 1)
    def _():
        cut = part_first.shape[0]
        part_first[...] = acc[:cut, :].astype(bf16)
        part_second[...] = acc[cut:, :].astype(bf16)


def blocks_across(ref, value):
    for i in range(value.shape[1] // 128):
        ref[i] = value[:, i * 128 : (i + 1) * 128]


def blocks_down(ref, value):
    for i in range(value.shape[0] // 128):
        ref[i] = value[i * 128 : (i + 1) * 128, :]


def middle_kernel(info, x, part_first, part_second, got_first, got_second, mask, gain, out_second, ffn_first,
                  hidden_ref, lhs, low_ref, both_ref, added, first_rel, second_rel, gain_rel):
    width = x.shape[1]
    block = width // 8
    rank = mask.shape[1]
    for r in range(8):
        at = lanes_at(info[ACTUAL + r], block)
        here = slice(r * block, (r + 1) * block)
        first_rel[here, :] = ffn_first[at, :]
        second_rel[:, here] = out_second[:, at]
        gain_rel[:, here] = gain[:, at]
    cut = part_first.shape[0]
    for own, got, base in ((part_first, got_first, 0), (part_second, got_second, cut)):
        both_ref[base : base + own.shape[0], :] = own[...].astype(f32) + got[...].astype(f32)
    low = both_ref[:, width:].astype(bf16) * mask[...]
    low_ref[...] = low
    added[...] = dot(low, second_rel[...])

    def visit(at):
        hidden = x[at, :].astype(f32) + (both_ref[at, :width] + adapter_scale * added[at, :])
        hidden_ref[at, :] = hidden
        scale = lax.rsqrt(jnp.mean(hidden * hidden, axis=-1, keepdims=True) + norm_eps)
        lhs[at, :width] = (hidden * scale * gain_rel[0:1, :]).astype(bf16)

    over_row_blocks(x.shape[0], 16, visit)
    low = dot(lhs[:, :width], first_rel[...]).astype(bf16)
    lhs[:, width : width + rank] = low[:, :rank] * mask[...]
    lhs[:, width + rank :] = low[:, rank:] * mask[...]


def feed_kernel(cuts, span, info, lhs, glhs, ffn_expand, down_shrink, *refs):
    if len(cuts) == 1:
        gu_parts, down_parts, refs = [[refs[0].at[0], refs[0].at[1]]], [refs[1]], refs[2:]
        arrived = lambda: None
    else:
        gu_parts = [[refs[0].at[k, j] for j in range(2)] for k in range(2)]
        down_parts = [refs[1].at[k] for k in range(2)]
        count = len(FEED_CUTS)
        far, refs = refs[2 : 2 + 4 * count], refs[2 + 4 * count :]
        slots, sems, refs = refs[-2], refs[-1], refs[:-2]
        step, steps = pl.program_id(0), FEED_CUTS[-1][1]

        def fetch(tile):
            for i, (low, top) in enumerate(FEED_CUTS):

                @pl.when((tile >= low) & (tile < top))
                def _(i=i, low=low):
                    at = pl.ds(pl.multiple_of((tile - low) * TILE, TILE), TILE)
                    for k in range(4):
                        slot = lax.rem(tile, 2)
                        pltpu.make_async_copy(far[k * count + i].at[:, :, at], slots.at[slot, k], sems.at[slot, k]).start()

        @pl.when(step == 0)
        def _():
            fetch(step)

        @pl.when(step + 1 < steps)
        def _():
            fetch(step + 1)

        slot = lax.rem(step, 2)
        here = slots.at[slot]
        for k in range(4):
            gu_parts.append([here.at[k, 0], here.at[k, 1]])
            down_parts.append(here.at[k, 2])

        def arrived():
            for k in range(4):
                pltpu.make_async_copy(far[k * count].at[:, :, :TILE], slots.at[slot, k], sems.at[slot, k]).wait()
    f_ref, own_ref, send_ref, grads, acc_d, acc_f = refs
    width = cuts[-1][1]
    half = width // 2
    rank = down_shrink.shape[1]
    step = pl.program_id(0)

    @pl.when(step == 0)
    def _():
        acc_d[...] = jnp.zeros_like(acc_d)
        acc_f[...] = jnp.zeros_like(acc_f)

    arrived()
    lows = [lhs[:, width : width + rank], lhs[:, width + rank :]]
    half_scale = jnp.asarray(adapter_scale, bf16)

    def project(j):
        total = dot(lows[j], ffn_expand[j] * half_scale)
        for (low, top), w in zip(cuts, gu_parts):
            total = total + dot(lhs[:, low:top], w[j][...])
        return total

    gate, up = project(0), project(1)
    sig = jax.nn.sigmoid(gate)
    silu = gate * sig
    act = (silu * up).astype(bf16)
    g_low = glhs[:, width:]
    grad_act = dot_nt(g_low, down_shrink[...])
    for (low, top), w in zip(cuts, down_parts):
        grad_act = grad_act + dot_nt(glhs[:, low:top], w[...])
    gg = (grad_act * up * (sig * (1.0 + gate * (1.0 - sig)))).astype(bf16)
    gu = (grad_act * silu).astype(bf16)
    for (low, top), w in zip(cuts, down_parts):
        acc_d[:span, low:top] += dot(act[:span], w[...])
    acc_d[:span, width:] += dot(act[:span], down_shrink[...])
    for (low, top), w in zip(cuts, gu_parts):
        acc_f[:, low:top] += dot_nt(gg, w[0][...]) + dot_nt(gu, w[1][...])
    acc_f[:, width : width + rank] += dot_nt(gg, ffn_expand[0] * half_scale)
    acc_f[:, width + rank :] += dot_nt(gu, ffn_expand[1] * half_scale)
    blocks_down(grads.at[0], dot_tn(act[:span], g_low[:span]))
    blocks_across(grads.at[1], adapter_scale * dot_tn(lows[0][:span], gg[:span]))
    blocks_across(grads.at[2], adapter_scale * dot_tn(lows[1][:span], gu[:span]))

    @pl.when(step == pl.num_programs(0) - 1)
    def _():
        f_ref[...] = acc_f[...].astype(bf16)
        place = info[3]
        own_ref[:, :half] = acc_d[:span, lanes_at(place, half)].astype(bf16)
        send_ref[:, :half] = acc_d[:span, lanes_at(1 - place, half)].astype(bf16)
        own_ref[:, half:] = acc_d[:span, width:].astype(bf16)
        send_ref[:, half:] = acc_d[:span, width:].astype(bf16)


def back_kernel(cuts, span, info, part, got, hidden, glhs, lhs_two, out_low, lhs_one, mask, gain, out_second, ffn_first,
                one, two, taps, in_expand, out_shrink, b_ref, c_ref, v_ref, conv_ref, gated_ref, *refs):
    in_parts, out_parts, refs = mixer_parts(refs, cuts)
    (own_ref, send_ref, rank_ref, gh_ref, ffn_grad, second_grad, grads,
     acc, branch, first_rel, second_rel, gain_rel) = refs
    width = cuts[-1][1]
    half = width // 2
    block = width // 8
    rank = mask.shape[1]
    step = pl.program_id(0)
    place = info[3]

    @pl.when(step == 0)
    def _():
        for r in range(8):
            at = lanes_at(info[ACTUAL + r], block)
            here = slice(r * block, (r + 1) * block)
            first_rel[here, :] = ffn_first[at, :]
            second_rel[:, here] = out_second[:, at]
            gain_rel[:, here] = gain[:, at]
        low = (part[:, width:].astype(f32) + got[:, width:].astype(f32)).astype(bf16)
        low = jnp.concatenate([low[:, :rank] * mask[...], low[:, rank:] * mask[...]], axis=1)
        acc[:, :width] = dot_nt(low, first_rel[...])

        def visit(at):
            both = part[at, :width].astype(f32) + got[at, :width].astype(f32)
            h = hidden[at, :]
            scale = lax.rsqrt(jnp.mean(h * h, axis=-1, keepdims=True) + norm_eps)
            unit = h * scale
            grad_unit = (both + acc[at, :width]) * gain_rel[0:1, :]
            grad = glhs[at, :width].astype(f32) + scale * (
                grad_unit - unit * jnp.mean(grad_unit * unit, axis=-1, keepdims=True)
            )
            gh_ref[at, :] = grad
            branch[at, :width] = grad.astype(bf16)

        over_row_blocks(hidden.shape[0], 16, visit)
        b_low = adapter_scale * dot_nt(branch[:, :width], second_rel[...])
        branch[:, width:] = b_low.astype(bf16) * mask[...]
        for i in range(4):
            at = lanes_at(place * 4 + info[INNER + i], block)
            value = dot_tn(lhs_two[:span, at], low[:span])
            for k in range(2):
                blocks_down(ffn_grad.at[i, k], value[:, k * 128 : (k + 1) * 128])
            blocks_across(second_grad.at[i], adapter_scale * dot_tn(out_low[:span, :], branch[:span, at]))
        acc[...] = jnp.zeros_like(acc)

    total = dot_nt(branch[:, width:], out_shrink[...])
    for (low, top), w in zip(cuts, out_parts):
        total = total + dot_nt(branch[:, low:top], w[...])
    grad_c = total * conv_ref[...]
    conv = total * c_ref[...]
    w = taps[...].astype(f32)
    high = conv.astype(bf16)
    rest = (conv - high.astype(f32)).astype(bf16)
    mixed = (
        w[0:1] * conv
        + w[1:2] * (dot_tn(one[...], high) + dot_tn(one[...], rest))
        + w[2:3] * (dot_tn(two[...], high) + dot_tn(two[...], rest))
    )
    proj = [
        (mixed * v_ref[...]).astype(bf16)[:span],
        grad_c.astype(bf16)[:span],
        (mixed * b_ref[...]).astype(bf16)[:span],
    ]
    half_scale = jnp.asarray(adapter_scale, bf16)
    for (low, top), w in zip(cuts, in_parts):
        acc[:span, low:top] += dot_nt(proj[0], w[0][...]) + dot_nt(proj[1], w[1][...]) + dot_nt(proj[2], w[2][...])
    acc[:span, width:] += (
        dot_nt(proj[0], in_expand[0] * half_scale)
        + dot_nt(proj[1], in_expand[1] * half_scale)
        + dot_nt(proj[2], in_expand[2] * half_scale)
    )
    low_one = lhs_one[:span, width:]
    for j in range(3):
        blocks_across(grads.at[j], adapter_scale * dot_tn(low_one, proj[j]))
    blocks_down(grads.at[3], dot_tn(gated_ref[:span, :], branch[:span, width:]))

    @pl.when(step == pl.num_programs(0) - 1)
    def _():
        own_ref[...] = acc[:span, lanes_at(place, half)].astype(bf16)
        send_ref[...] = acc[:span, lanes_at(1 - place, half)].astype(bf16)
        rank_ref[:, :rank] = acc[:span, width:].astype(bf16)

        def visit(at):
            sums = acc[at, :width].astype(bf16).astype(f32) * lhs_one[at, :width].astype(f32)
            stat = jnp.sum(sums, axis=-1, keepdims=True)
            high = stat.astype(bf16).astype(f32)
            middle = (stat - high).astype(bf16).astype(f32)
            rest = stat - high - middle
            lane = lax.broadcasted_iota(jnp.int32, (stat.shape[0], 128), 1)
            packed = jnp.where(lane == 0, high, jnp.where(lane == 1, middle, jnp.where(lane == 2, rest, 0.0)))
            rank_ref[at, rank:] = packed.astype(bf16)

        over_row_blocks(span, 16, visit)


def rank_rows(own, got, mask):
    rank = mask.shape[1]
    sums = own[...].astype(f32) + got[...].astype(f32)
    return sums[:, :rank].astype(bf16) * mask[...], sums[:, rank:]


def output_kernel(info, *refs):
    output_rows(info, *refs[:8], *refs[-2:])


def output_rows(info, own, got, rank_own, rank_got, hidden, mask, g, second, out_ref, grad_ref):
    low, _ = rank_rows(rank_own, rank_got, mask)
    down = own[...].astype(f32) + got[...].astype(f32)
    out_ref[...] = (hidden[...] + (down + adapter_scale * dot(low, second[...]))).astype(bf16)
    blocks_across(grad_ref, adapter_scale * dot_tn(low, g[...]))


def rank_kernel(info, own, got, mask, normed, grad_ref):
    low, _ = rank_rows(own, got, mask)
    blocks_down(grad_ref, dot_tn(normed[...], low))


def final_kernel(width, info, *refs):
    final_rows(width, info, *refs[:11], refs[-1])


def final_rows(width, info, own, got, rank_own, rank_got, gh, x, low, scale, mask, gain, first, grad_ref):
    n_low, stat = rank_rows(rank_own, rank_got, mask)
    stat = jnp.sum(stat, axis=-1, keepdims=True)
    stat = stat + jnp.sum(n_low.astype(f32) * low[...].astype(f32), axis=-1, keepdims=True)
    stat = stat / width
    scale_rows = scale[:, 0:1]
    unit = x[...].astype(f32) * scale_rows
    grad = own[...].astype(f32) + got[...].astype(f32) + dot_nt(n_low, first[...])
    grad_ref[...] = gh[...] + scale_rows * (grad * gain[0:1, :].astype(f32) - unit * stat)


def places(info, pieces):
    me, ctx = info[0], info[1]
    for place in range(4 * pieces):
        c, x, z = place // (2 * pieces), place // pieces % 2, place % pieces
        far_c, far_x = (me % 2) ^ c, (me // 2) ^ x
        yield place, 2 * far_c + far_x, lax.rem(ctx + pieces - z, pieces)


def unpack_feed_kernel(tiles, total, expand_ref, first_ref):
    for h in range(tiles):
        for k in range(2):
            column = h * 256 + k * 128
            for j in range(3):
                row = ((h * 3 + j) * 2 + k) * 128
                value = total[row : row + 128, :].astype(f32)
                if j:
                    expand_ref[j - 1, :, column : column + 128] = value
                else:
                    first_ref[column : column + 128, :] = value


def gather_feed_kernel(pieces, tiles, info, own, x, c, cx, expand_ref, first_ref, kept):
    n = own.shape[1]
    for place, which, distance in places(info, pieces):
        for k, part in enumerate((own, x, c, cx)):

            @pl.when(which == k)
            def _(part=part, place=place, distance=distance):
                kept[place * n : (place + 1) * n, :] = part[distance]

    unpack_feed_kernel(tiles, kept, expand_ref, first_ref)


def gather_rows_kernel(pieces, info, own, x, c, cx, out):
    for place, which, distance in places(info, pieces):
        for k, part in enumerate((own, x, c, cx)):

            @pl.when(which == k)
            def _(part=part, place=place, distance=distance):
                out[place] = part[distance]


def unpack_early_kernel(pieces, info, own, x, c, cx, ffn_ref, second_ref, expand_ref, out_ref, kept):
    gather_rows_kernel(pieces, info, own, x, c, cx, kept)
    tens = info[2]
    for place in range(4 * pieces):
        i, k, part = place // 4, place // 2 % 2, place % 2
        for t in range(2):
            base = pl.multiple_of(jnp.where(tens == t, 0, 192), 64)
            ffn_ref[t * 1024 + i * 256 + part * 128 : t * 1024 + i * 256 + part * 128 + 128, k * 128 : (k + 1) * 128] = (
                kept[place, pl.ds(base, 128), :].astype(f32)
            )
            column = t * 1024 + i * 256 + k * 128
            second_ref[part * 64 : part * 64 + 64, column : column + 128] = kept[
                place, pl.ds(pl.multiple_of(base + 128, 64), 64), :
            ].astype(f32)
        h, j = place // 4, place % 4
        for k in range(2):
            value = kept[place, 384 + k * 128 : 512 + k * 128, :].astype(f32)
            column = h * 256 + k * 128
            if j < 3:
                expand_ref[j, :, column : column + 128] = value
            else:
                out_ref[column : column + 128, :] = value


def unpack_late_kernel(pieces, info, own, x, c, cx, first_ref, second_ref, kept):
    gather_rows_kernel(pieces, info, own, x, c, cx, kept)
    tens = info[2]
    for place in range(4 * pieces):
        for t in range(2):
            base = pl.multiple_of(jnp.where(tens == t, 0, 128), 128)
            row = t * 1024 + place * 64
            first_ref[row : row + 64, :] = kept[place, pl.ds(base, 64), :].astype(f32)
            row, column = place % 2 * 64, t * 1024 + place // 2 * 128
            second_ref[row : row + 64, column : column + 128] = kept[
                place, pl.ds(pl.multiple_of(base + 64, 64), 64), :
            ].astype(f32)


def after(array, *gates):
    return lax.optimization_barrier((array,) + gates)[0] if gates else array


def swap_tensor(array):
    return lax.ppermute(array, "tensor", [(0, 1), (1, 0)])


def body(
    block_input,
    cotangent,
    deal_order,
    seq_lengths,
    seq_adapter,
    mixer_gain,
    ffn_gain,
    conv_taps,
    in_weight,
    out_weight,
    gateup_weight,
    down_weight,
    input_adapter_shrink,
    in_expand,
    out_shrink,
    output_adapter_expand,
    ffn_shrink,
    ffn_expand,
    down_shrink,
    down_adapter_expand,
):
    tok_count, half = block_input.shape
    width = 2 * half
    rank = input_adapter_shrink.shape[1]
    hidden_units = gateup_weight.shape[2]
    groups = lax.axis_size("dp")
    pieces = lax.axis_size("ctx")
    sub = tok_count // groups
    group_tokens = pieces * tok_count
    seqs = seq_lengths.shape[0]
    nb = groups // CHUNKS
    span = nb * sub
    halo = -(-4 * nb // 16) * 16
    rows = span + halo
    special = groups == 4 and pieces % 2 == 0
    me = lax.axis_index("dp")
    ctx = lax.axis_index("ctx")
    tens = lax.axis_index("tensor")
    if special:
        xb, cb, zb = me // 2, me % 2, ctx % 2
    else:
        xb = cb = zb = jnp.int32(0)
    flip = xb ^ tens

    actual, in_stack, inner = [], [], []
    for rx in (0, 1):
        for rc in (0, 1):
            for rh in (0, 1):
                low = (rc ^ (cb & rx)) * 2 + (rh ^ (zb & rx))
                actual.append((rx ^ xb) * 4 + low)
                in_stack.append((rx ^ flip) * 4 + low)
    for bc in (0, 1):
        for bh in (0, 1):
            inner.append((bc ^ (cb & flip)) * 2 + (bh ^ (zb & flip)))
    info = jnp.stack([me, ctx, tens, flip, *actual, *in_stack, *inner]).astype(jnp.int32)

    core_route = [(0, 1), (1, 0), (2, 3), (3, 2)]
    x_route = [(0, 2), (2, 0), (1, 3), (3, 1)]
    z_route = [(i, i ^ 1) for i in range(pieces)]
    gates = []

    def wait(*values):
        gates[:] = values

    def begin(axis, route, array):
        return lax.ppermute(after(array, *gates), axis, route)

    def core(array):
        return begin("dp", core_route, array)

    def over_x(array):
        return begin("dp", x_route, array)

    def over_z(array):
        return begin("ctx", z_route, array)

    def over_y(array):
        return begin("tensor", [(0, 1), (1, 0)], array)

    def tiles_beside(array):
        tiles = array.reshape(-1, TILE, array.shape[1])
        return jnp.concatenate([tiles[i] for i in range(tiles.shape[0])], axis=1)

    def mixer_piece(k):
        at = slice(k * half // 2, (k + 1) * half // 2)
        return jnp.concatenate([mine(in_weight[:, :, at], 1), tiles_beside(mine(out_weight[at], 1))[None]], axis=0)

    def feed_piece(k):
        low, top = FEED_CUTS[k]
        at = slice(low * TILE, top * TILE)
        return jnp.concatenate([mine(gateup_weight[:, :, at], 1), tiles_beside(mine(down_weight[at], 1))[None]], axis=0)

    def chip_pair(array):
        return lax.all_gather(after(array, *gates), "dp", axis_index_groups=[[0, 1], [2, 3]])

    def mine(shard, axis):
        n = shard.shape[axis] // 2
        return lax.dynamic_slice_in_dim(shard, zb * n, n, axis)

    numbers = jnp.concatenate([deal_order[0], seq_lengths, seq_adapter])
    digits = jnp.concatenate([numbers // 64, numbers % 64]).astype(bf16)
    x_blocks = block_input.reshape(groups, sub, half)
    g_blocks = cotangent.reshape(groups, sub, half)
    digit_rows = jnp.zeros((groups, 2, half), bf16).at[0, 0, : digits.shape[0]].set(digits)
    edges = jnp.concatenate([x_blocks[:, :2], g_blocks[:, :2], x_blocks[:, sub - 2 :], digit_rows], axis=1)

    all_edges = lax.all_gather(edges, "dp", axis=0, tiled=False)
    digits = all_edges[:, 0, 6, : 2 * numbers.shape[0]].astype(jnp.int32)
    table = digits[:, : numbers.shape[0]] * 64 + digits[:, numbers.shape[0] :]
    dims = (groups, seqs, sub, nb, rows, tok_count, group_tokens)
    per_chunk = lambda c, *_: (c, 0, 0)
    mask, one, two = call(
        functools.partial(tables_kernel, dims), (CHUNKS,), (table, info), [],
        [
            ((CHUNKS, rows, rank), bf16, (None, rows, rank), per_chunk),
            ((CHUNKS, rows, rows), bf16, (None, rows, rows), per_chunk),
            ((CHUNKS, rows, rows), bf16, (None, rows, rows), per_chunk),
        ],
    )
    first_heads, last_tails, next_near, prev_near = call(
        functools.partial(edges_kernel, groups), (1,), (table, info), [(all_edges, None, None)],
        [
            ((groups, 4, half), bf16, None, None),
            ((groups, 2, half), bf16, None, None),
            ((groups, 4, half), bf16, None, None),
            ((groups, 2, half), bf16, None, None),
        ],
    )
    if special:
        in_own = chip_pair(in_weight)
        mixer_x, mixer_z, mixer_xc, mixer_zc = ([None] * 2 for _ in range(4))
        feed_x, feed_z, feed_xc, feed_zc = ([None] * len(FEED_CUTS) for _ in range(4))
        mixer_packed = [mixer_piece(k) for k in range(2)]
        feed_packed = [feed_piece(k) for k in range(len(FEED_CUTS))]
    wait(all_edges)
    x_got = [over_y(block_input[:span]), None]
    if special:
        mixer_x[0] = over_x(mixer_packed[0])
    from_next = begin("ctx", [(i + 1, i) for i in range(pieces - 1)], first_heads)
    from_prev = begin("ctx", [(i, i + 1) for i in range(pieces - 1)], last_tails)
    deal_all = table[:, :groups]
    at_end = (deal_all[:, groups - 1] == me)[:, None, None]
    at_start = (deal_all[:, 0] == me)[:, None, None]
    next_rows = jnp.where(at_end, from_next, next_near)
    prev_rows = jnp.where(at_start, from_prev, prev_near)
    halo_x = jnp.concatenate([prev_rows, next_rows[:, :2]], axis=1)
    halo_g = jnp.concatenate([jnp.zeros_like(prev_rows), next_rows[:, 2:]], axis=1)
    halo_own = jnp.stack([halo_x, halo_g]).reshape(2, CHUNKS, 4 * nb, half)
    halo_own = jnp.pad(halo_own, ((0, 0), (0, 0), (0, halo - 4 * nb), (0, 0)))
    stage = [from_next, from_prev, x_got[0]] + ([mixer_x[0], in_own, mixer_packed[1]] if special else [])
    wait(*stage)
    halo_got = over_y(halo_own)
    x_got[1] = over_y(block_input[span:])
    stage = [halo_got, x_got[1]]
    if special:
        mixer_x[1], mixer_z[0], mixer_xc[0] = over_x(mixer_packed[1]), over_z(mixer_x[0]), core(mixer_x[0])
        out_own = chip_pair(out_weight)
        stage += [mixer_x[1], mixer_z[0], mixer_xc[0], out_own, feed_packed[0]]
    wait(*stage)
    g_got = [over_y(cotangent[:span]), None]
    stage = [g_got[0]]
    if special:
        feed_x[0], mixer_z[1] = over_x(feed_packed[0]), over_z(mixer_x[1])
        mixer_xc[1], mixer_zc[0] = core(mixer_x[1]), core(mixer_z[0])
        gu_own = chip_pair(gateup_weight)
        stage += [feed_x[0], mixer_z[1], mixer_xc[1], mixer_zc[0], feed_packed[1]]

    gain_one, gain_two = mixer_gain[None, :].astype(f32), ffn_gain[None, :].astype(f32)
    ext_one, ext_two = width + rank, width + 2 * rank

    def stacked(array, last):
        return (array, (None,) + array.shape[1:], lambda c, *_: (c, 0, 0))

    def joined_inputs(own, got, which):
        def halo_of(array):
            return (array, (None, None, halo, half), lambda c, *_: (which, c, 0, 0))

        return [
            (own, (span, half), lambda c, *_: (c, 0)),
            (got[0], None, None),
            (got[1], None, None),
            halo_of(halo_own),
            halo_of(halo_got),
        ]

    x_full, lhs_one, scale = call(
        input_kernel, (CHUNKS,), (info,),
        joined_inputs(block_input, x_got, 0)
        + [(gain_one, None, None), (input_adapter_shrink, None, None), stacked(mask, rank)],
        [
            ((CHUNKS, rows, width), bf16, (None, rows, width), per_chunk),
            ((CHUNKS, rows, ext_one), bf16, (None, rows, ext_one), per_chunk),
            ((CHUNKS, rows, 128), f32, (None, rows, 128), per_chunk),
        ],
        [
            pltpu.VMEM((rows, width), bf16),
            pltpu.VMEM((width, rank), bf16),
            pltpu.VMEM((1, width), f32),
        ],
    )
    wait(*stage, lhs_one)
    g_got[1] = over_y(cotangent[span:])
    stage = [g_got[1]]
    if special:
        n = width // 8
        cuts = ((0, 2 * n), (2 * n, 4 * n), (4 * n, 5 * n), (5 * n, 6 * n), (6 * n, 7 * n), (7 * n, 8 * n))
        mixer_zc[1] = core(mixer_z[1])
        feed_x[1], feed_z[0], feed_xc[0] = over_x(feed_packed[1]), over_z(feed_x[0]), core(feed_x[0])
        stage += [feed_x[1], feed_z[0], feed_xc[0], feed_packed[2]]
        mixer_inputs = lambda: (
            [(in_own, (2, 3, in_own.shape[2], TILE), lambda h, *_: (0, 0, 0, h)),
             (out_own, (2, TILE, out_own.shape[2]), lambda h, *_: (0, h, 0))]
            + [(w, (4, TILE, TILE), (lambda h, *_: (0, 0, jnp.minimum(h, 1))) if i == 0 else (lambda h, *_: (0, 0, jnp.maximum(h - 2, 0))))
               for part in (mixer_x, mixer_z, mixer_xc, mixer_zc) for i, w in enumerate(part)]
        )
    else:
        cuts = ((0, width),)
        in_parts = [lax.all_gather(in_weight, "dp", axis=1, tiled=True)]
        out_parts = [lax.all_gather(out_weight, "dp", axis=1, tiled=True)]
        gu_parts = [lax.all_gather(gateup_weight, "dp", axis=1, tiled=True)]
        down_parts = [lax.all_gather(down_weight, "dp", axis=1, tiled=True)]
        mixer_inputs = lambda: [columns(in_parts[0]), row_tiles(out_parts[0])]

    def picked(array, c):
        return (array, (None,) + array.shape[1:], lambda *_: (c, 0, 0))

    def columns(array):
        return (array, array.shape[:-1] + (TILE,), lambda h, *_: (0,) * (array.ndim - 1) + (h,))

    def row_tiles(array):
        lead = array.ndim - 2
        return (array, array.shape[:lead] + (TILE, array.shape[-1]), lambda h, *_: (0,) * lead + (h, 0))

    def feed_step(k):
        count = len(FEED_CUTS)
        if k < count:
            feed_x[k] = over_x(feed_packed[k])
            stage.extend([feed_x[k]] + feed_packed[k + 1 : k + 2])
        if 0 <= k - 1 < count:
            feed_z[k - 1], feed_xc[k - 1] = over_z(feed_x[k - 1]), core(feed_x[k - 1])
            stage.extend([feed_z[k - 1], feed_xc[k - 1]])
        if 0 <= k - 2 < count:
            feed_zc[k - 2] = core(feed_z[k - 2])
            stage.append(feed_zc[k - 2])

    mixer_steps = half // TILE
    feed_steps = hidden_units // TILE
    column_out = lambda h, *_: (0, h)
    row_halves = (rows // 32 * 16, rows - rows // 32 * 16)
    chunks = []
    for c in range(CHUNKS):
        gate_b, gate_c, values, conv, gated, *part = call(
            functools.partial(mixer_kernel, cuts), (mixer_steps,), (),
            [picked(lhs_one, c), picked(one, c), picked(two, c), columns(conv_taps), columns(in_expand), row_tiles(out_shrink)]
            + mixer_inputs(),
            [((rows, half), f32, (rows, TILE), column_out)] * 4
            + [((rows, half), bf16, (rows, TILE), column_out)]
            + [((n, ext_one), bf16, None, None) for n in row_halves],
            [pltpu.VMEM((rows, ext_one), f32)],
            flops=2 * rows * half * ext_one * 4,
        )
        chunks.append(dict(b=gate_b, c=gate_c, v=values, conv=conv, gated=gated, part=part))
        if c == 0:
            wait(*stage, *part)
            chunks[0]["got"] = [over_y(part[0]), None]
            stage = [chunks[0]["got"][0]]
            if special:
                feed_step(2)
                down_own = chip_pair(down_weight)
    def middle(i):
        c = chunks[i]
        c["hidden"], c["lhs"], c["low"] = call(
            middle_kernel, (1,), (info,),
            [picked(x_full, i)] + [(w, None, None) for w in (*c["part"], *c["got"])]
            + [picked(mask, i), (gain_two, None, None), (output_adapter_expand, None, None), (ffn_shrink, None, None)],
            [((rows, width), f32, None, None), ((rows, ext_two), bf16, None, None), ((rows, rank), bf16, None, None)],
            [
                pltpu.VMEM((rows, ext_one), f32),
                pltpu.VMEM((rows, width), f32),
                pltpu.VMEM((width, 2 * rank), bf16),
                pltpu.VMEM((rank, width), bf16),
                pltpu.VMEM((1, width), f32),
            ],
        )

    wait(*stage, *chunks[1]["part"])
    chunks[0]["got"][1] = over_y(chunks[0]["part"][1])
    stage = [chunks[0]["got"][1]]
    if special:
        feed_step(3)
    wait(*stage)
    chunks[1]["got"] = [over_y(chunks[1]["part"][0]), None]
    stage = [chunks[1]["got"][0]]
    if special:
        feed_step(4)
    (glhs,) = call(
        cotangent_kernel, (CHUNKS,), (info,),
        joined_inputs(cotangent, g_got, 1) + [(down_adapter_expand, None, None), stacked(mask, rank)],
        [((CHUNKS, rows, ext_one), bf16, (None, rows, ext_one), per_chunk)],
        [pltpu.VMEM((rows, width), bf16), pltpu.VMEM((rank, width), bf16)],
    )

    wait(*stage, glhs)
    chunks[1]["got"][1] = over_y(chunks[1]["part"][1])
    stage = [chunks[1]["got"][1]]
    middle(0)
    middle(1)
    if special:
        feed_step(5)
        wait(*stage, chunks[0]["lhs"])
        stage = [chunks[1]["lhs"]]
        feed_step(6)
        wait(*stage)
        feed_step(7)
        whole = [(gu_own, (2, 2, gu_own.shape[2], TILE), lambda h, *_: (0, 0, 0, h)),
                 (down_own, (2, TILE, down_own.shape[2]), lambda h, *_: (0, h, 0))]
        feed_inputs = whole + [(w, "any", None) for part in (feed_x, feed_z, feed_xc, feed_zc) for w in part]
    else:
        feed_inputs = [columns(gu_parts[0]), row_tiles(down_parts[0])]

    for i, c in enumerate(chunks):
        f_part, d_own, d_send, grads = call(
            functools.partial(feed_kernel, cuts, span), (feed_steps,), (info,),
            [(c["lhs"], None, None), picked(glhs, i), columns(ffn_expand), row_tiles(down_shrink)]
            + feed_inputs,
            [
                ((rows, ext_two), bf16, None, None),
                ((span, half + rank), bf16, None, None),
                ((span, half + rank), bf16, None, None),
                ((feed_steps, 3, 2, 128, 128), f32, (None, 3, 2, 128, 128), lambda h, *_: (h, 0, 0, 0, 0)),
            ],
            [
                pltpu.VMEM((rows, ext_one), f32),
                pltpu.VMEM((rows, ext_two), f32),
            ]
            + ([pltpu.VMEM((2, 4, 3, TILE, TILE), bf16), pltpu.SemaphoreType.DMA((2, 4))] if special else []),
            flops=2 * rows * hidden_units * ext_two * 6,
        )
        c.update(f_own=f_part, d_own=d_own, d_send=d_send, feed_grads=grads)
    def summed(name):
        return sum(c[name] for c in chunks).astype(bf16)

    def take(array, i):
        return lax.dynamic_index_in_dim(array, i, 0, keepdims=False)

    def add(*terms):
        return sum(t.astype(f32) for t in terms).astype(bf16)

    core_bit, x_bit = me % 2, me // 2
    shifts = [[(i, (i + k) % pieces) for i in range(pieces)] for k in range(1, pieces)]

    def cut(*arrays):
        return jnp.concatenate([a.reshape(2, 2, pieces, -1, 128) for a in arrays], axis=3)

    def scatter_core(total):
        return add(take(total, core_bit), lax.ppermute(take(total, 1 - core_bit), "dp", core_route))

    def scatter_x(total):
        return add(take(total, x_bit), lax.ppermute(take(total, 1 - x_bit), "dp", x_route))

    def scatter_z(total):
        sent = [lax.ppermute(take(total, (ctx + k) % pieces), "ctx", route) for k, route in enumerate(shifts, 1)]
        return add(take(total, ctx), *sent)

    def gather_z(total):
        return jnp.stack([total] + [lax.ppermute(total, "ctx", route) for route in shifts])

    def gather_chip(total):
        over_x = lax.ppermute(total, "dp", x_route)
        return [total, over_x] + [lax.ppermute(v, "dp", core_route) for v in (total, over_x)]

    for c in chunks:
        c["f_got"] = swap_tensor(c["f_own"])
    feed = summed("feed_grads")
    if special:
        feed_sum = scatter_core(cut(after(feed, chunks[0]["f_got"])))
    for i, c in enumerate(chunks):
        f_got = after(c["f_got"], *([feed_sum] if special and i == 0 else []), *([chunks[0]["n_rank"]] if i else []))
        n_own, n_send, n_rank, grad_hidden, ffn_grad, second_grad, grads = call(
            functools.partial(back_kernel, cuts, span), (mixer_steps,), (info,),
            [(c["f_own"], None, None), (f_got, None, None), (c["hidden"], None, None), picked(glhs, i),
             (c["lhs"], None, None), (c["low"], None, None), picked(lhs_one, i), picked(mask, i),
             (gain_two, None, None), (output_adapter_expand, None, None), (ffn_shrink, None, None),
             picked(one, i), picked(two, i), columns(conv_taps), columns(in_expand), row_tiles(out_shrink),
             columns(c["b"]), columns(c["c"]), columns(c["v"]), columns(c["conv"]), columns(c["gated"])]
            + mixer_inputs(),
            [
                ((span, half), bf16, None, None),
                ((span, half), bf16, None, None),
                ((span, 2 * rank), bf16, None, None),
                ((rows, width), f32, None, None),
                ((4, 2, 2, 128, 128), f32, None, None),
                ((4, 2, 128, 128), f32, None, None),
                ((mixer_steps, 4, 2, 128, 128), f32, (None, 4, 2, 128, 128), lambda h, *_: (h, 0, 0, 0, 0)),
            ],
            [
                pltpu.VMEM((rows, ext_one), f32),
                pltpu.VMEM((rows, ext_one), bf16),
                pltpu.VMEM((width, 2 * rank), bf16),
                pltpu.VMEM((rank, width), bf16),
                pltpu.VMEM((1, width), f32),
            ],
            flops=2 * rows * half * ext_one * 4,
        )
        c.update(n_own=n_own, n_send=n_send, n_rank=n_rank, gh=grad_hidden, ffn_grad=ffn_grad, second_grad=second_grad, mixer_grads=grads)
        if special:
            feed_sum = scatter_x(feed_sum) if i == 0 else feed_sum
    for c in chunks:
        c["d_got"] = swap_tensor(after(c["d_send"], chunks[0]["f_got"]))
    chunks[1]["rank_got"] = swap_tensor(chunks[1]["n_rank"])
    chunks[0]["rank_got"] = swap_tensor(after(chunks[0]["n_rank"], chunks[1]["n_rank"]))
    for c in chunks:
        c["n_got"] = swap_tensor(after(c["n_send"], chunks[1]["rank_got"]))
    if special:
        feed_sum = scatter_z(feed_sum)
        early = cut(after(summed("ffn_grad"), feed_sum, *(c["d_got"] for c in chunks)), summed("second_grad"), summed("mixer_grads"))
        early = scatter_core(early)
        first_step = (early,)
    else:
        first_step = ()

    block = half // 4
    in_half = lambda i, info: (0, info[INNER + i])
    in_full = lambda i, info: (0, info[3] * 4 + info[INNER + i])
    whole_block = lambda i, info: (0, 0)
    grad_out = ((4, 2, 128, 128), f32, (None, 2, 128, 128), lambda i, info: (i, 0, 0, 0))
    for k, c in enumerate(chunks):
        in_stack_full = lambda i, info, k=k: (k, 0, info[3] * 4 + info[INNER + i])
        masks = (mask, (None, span, rank), lambda i, info, k=k: (k, 0, 0))
        d_got = after(c["d_got"], *first_step)
        c["out"], c["down_grad"] = call(
            output_kernel, (4,), (info,),
            [
                (c["d_own"], (span, block), in_half),
                (d_got, (span, block), in_half),
                (c["d_own"], (span, rank), lambda i, info: (0, half // rank)),
                (d_got, (span, rank), lambda i, info: (0, half // rank)),
                (c["hidden"], (span, block), in_full),
                masks,
                (glhs, (None, span, block), in_stack_full),
                (down_adapter_expand, (rank, block), lambda i, info: (0, info[2] * 4 + i)),
            ]
            + ([(chunks[0]["out"], "any", None)] if k else []),
            [((tok_count, half), bf16, (span, block), lambda i, info, k=k: (k, i)), grad_out],
            flops=5 * 10**9,
            aliases={9: 0} if k else None,
        )
    wait()
    if special:
        feed_sum = gather_z(after(feed_sum, early))
        early = after(scatter_x(early), feed_sum, chunks[-1]["out"])
        second_step = (early,)
    else:
        second_step = ()
    for k, c in enumerate(chunks):
        in_stack_full = lambda i, info, k=k: (k, 0, info[3] * 4 + info[INNER + i])
        masks = (mask, (None, span, rank), lambda i, info, k=k: (k, 0, 0))
        ranks = [(w, (span, 2 * rank), whole_block) for w in (c["n_rank"], after(c["rank_got"], *second_step))]
        (c["in_grad"],) = call(
            rank_kernel, (4,), (info,), ranks + [masks, (lhs_one, (None, span, block), in_stack_full)], [grad_out],
            flops=5 * 10**9,
        )
    if special:
        feed_parts = [feed_sum, begin("dp", x_route, after(feed_sum, early))]
        early = after(scatter_z(early), feed_parts[1], *(c["in_grad"] for c in chunks))
        feed_parts += [begin("dp", core_route, v) for v in feed_parts]
        late = scatter_core(cut(summed("in_grad"), summed("down_grad")))
        h = 3 * 1024 // (4 * pieces)
        early = jnp.concatenate([early[:h], swap_tensor(early[:h]), early[h:]], axis=0)
        third_step = (early,)
    else:
        third_step = ()
    for k, c in enumerate(chunks):
        in_stack_full = lambda i, info, k=k: (k, 0, info[3] * 4 + info[INNER + i])
        masks = (mask, (None, span, rank), lambda i, info, k=k: (k, 0, 0))
        ranks = [(w, (span, 2 * rank), whole_block) for w in (c["n_rank"], c["rank_got"])]
        n_got = after(c["n_got"], *third_step)
        (c["grad"],) = call(
            functools.partial(final_kernel, width), (4,), (info,),
            [(c["n_own"], (span, block), in_half), (n_got, (span, block), in_half)]
            + ranks
            + [
                (c["gh"], (span, block), in_full),
                (x_full, (None, span, block), in_stack_full),
                (lhs_one, (None, span, rank), lambda i, info, k=k: (k, 0, width // rank)),
                (scale, (None, span, 128), lambda i, info, k=k: (k, 0, 0)),
                masks,
                (gain_one, (1, block), lambda i, info: (0, info[2] * 4 + i)),
                (input_adapter_shrink, (block, rank), lambda i, info: (info[2] * 4 + i, 0)),
            ]
            + ([(chunks[0]["grad"], "any", None)] if k else []),
            [((tok_count, half), f32, (span, block), lambda i, info, k=k: (k, i))],
            flops=6 * 10**9,
            aliases={12: 0} if k else None,
        )
    block_output, input_grad = chunks[-1]["out"], chunks[-1]["grad"]

    if special:
        late = scatter_x(after(late, early))
        gathered = gather_z(early)
        late = scatter_z(after(late, gathered))
        late = jnp.concatenate([late, swap_tensor(late)], axis=0)
        n = 4 * pieces
        parts = gather_chip(gathered)
        ffn_grad, second_grad, mixer_grad, out_grad = call(
            functools.partial(unpack_early_kernel, pieces), (1,), (info,), [(v, None, None) for v in parts],
            [((width, 2 * rank), f32, None, None), ((rank, width), f32, None, None), ((3, rank, half), f32, None, None),
             ((half, rank), f32, None, None)],
            [pltpu.VMEM((n,) + early.shape, bf16)],
        )
        feed_outs = [((2, rank, hidden_units), f32, None, None), ((hidden_units, rank), f32, None, None)]
        expand_grad, first_grad = call(
            functools.partial(gather_feed_kernel, pieces, feed_steps), (1,), (info,), [(v, None, None) for v in feed_parts],
            feed_outs, [pltpu.VMEM((feed.size // 128, 128), bf16)],
        )
        parts = gather_chip(gather_z(late))
        in_grad, down_grad = call(
            functools.partial(unpack_late_kernel, pieces), (1,), (info,), [(v, None, None) for v in parts],
            [((width, rank), f32, None, None), ((rank, width), f32, None, None)],
            [pltpu.VMEM((n,) + late.shape, bf16)],
        )
    else:
        names = ("mixer_grads", "ffn_grad", "second_grad", "in_grad", "down_grad")
        feed, mixer, ffn_grad, second_grad, in_grad, down_grad = lax.psum(
            (feed, *(summed(name) for name in names)), ("dp", "ctx")
        )

        def whole(part, axis):
            got = swap_tensor(part)
            pair = [jnp.where(tens == 0, part, got), jnp.where(tens == 0, got, part)]
            return jnp.concatenate(pair, axis=axis).astype(f32)

        def across(blocks):
            return blocks.reshape(-1, 128, 128).transpose(1, 0, 2).reshape(128, -1)

        ffn_grad = whole(ffn_grad.transpose(0, 2, 3, 1, 4).reshape(half, 2 * rank), 0)
        second_grad, down_grad = whole(across(second_grad), 1), whole(across(down_grad), 1)
        in_grad = whole(in_grad.reshape(half, rank), 0)
        mixer_grad = jnp.stack([across(mixer[:, j]) for j in range(3)]).astype(f32)
        out_grad = mixer[:, 3].reshape(half, rank).astype(f32)
        expand_grad = jnp.stack([across(feed[:, j]) for j in (1, 2)]).astype(f32)
        first_grad = feed[:, 0].reshape(hidden_units, rank).astype(f32)
    return (
        block_output,
        input_grad,
        in_grad,
        mixer_grad,
        out_grad,
        second_grad,
        ffn_grad,
        expand_grad,
        first_grad,
        down_grad,
    )


def solution(mesh):
    placed = (
        P(("dp", "ctx"), "tensor"),
        P(("dp", "ctx"), "tensor"),
        P("dp", None),
        P("dp"),
        P("dp"),
        P(),
        P(),
        P(None, "tensor"),
        P(None, "dp", "tensor"),
        P("tensor", "dp"),
        P(None, "dp", "tensor"),
        P("tensor", "dp"),
        P(),
        P(None, None, "tensor"),
        P("tensor", None),
        P(),
        P(),
        P(None, None, "tensor"),
        P("tensor", None),
        P(),
    )
    return jax.shard_map(
        body,
        mesh=mesh,
        in_specs=placed,
        out_specs=(
            P(("dp", "ctx"), "tensor"),
            P(("dp", "ctx"), "tensor"),
            P(),
            P(None, None, "tensor"),
            P("tensor", None),
            P(),
            P(),
            P(None, None, "tensor"),
            P("tensor", None),
            P(),
        ),
        check_vma=False,
    )
```

```python
import functools

import jax
import jax.numpy as jnp
from jax import lax
from jax.experimental import pallas as pl
from jax.experimental.pallas import tpu as pltpu
from jax.sharding import PartitionSpec as P

RANK = 16
CHUNKS = 2
TILE = 256
FEED_CUTS = ((0, 2), (2, 4), (4, 6), (6, 8), (8, 10), (10, 11))
VMEM_BYTES = 56 * 1024 * 1024

norm_eps = 1e-05
adapter_scale = 0.5

f32 = jnp.float32
bf16 = jnp.bfloat16


def dot(left, right):
    return jnp.dot(left, right, preferred_element_type=f32)


def dot_nt(left, right):
    return lax.dot_general(left, right, (((1,), (1,)), ((), ())), preferred_element_type=f32)


def dot_tn(left, right):
    return lax.dot_general(left, right, (((0,), (0,)), ((), ())), preferred_element_type=f32)


def over_row_blocks(rows, step, visit):
    def one(i, carry):
        visit(pl.ds(pl.multiple_of(i * step, step), step))
        return carry

    lax.fori_loop(0, rows // step, one, 0, unroll=5 if rows % (5 * step) == 0 else 2)


def lanes_at(index, width):
    return pl.ds(pl.multiple_of(index * width, width), width)


def call(kernel, grid, scalars, ins, outs, scratch=(), flops=0, aliases=None):
    in_specs = []
    for array, block, index in ins:
        if block == "any":
            in_specs.append(pl.BlockSpec(memory_space=pl.ANY))
        elif block is None:
            zeros = (0,) * array.ndim
            in_specs.append(
                pl.BlockSpec(array.shape, lambda *_, z=zeros: z, pipeline_mode=pl.Buffered(1))
            )
        else:
            in_specs.append(pl.BlockSpec(block, index))
    out_specs, out_shape = [], []
    for shape, dtype, block, index in outs:
        zeros = (0,) * len(shape)
        out_specs.append(
            pl.BlockSpec(shape, lambda *_, z=zeros: z) if block is None else pl.BlockSpec(block, index)
        )
        out_shape.append(jax.ShapeDtypeStruct(shape, dtype))
    moved = sum(a.size * a.dtype.itemsize for a, _, _ in ins)
    return pl.pallas_call(
        kernel,
        grid_spec=pltpu.PrefetchScalarGridSpec(
            num_scalar_prefetch=len(scalars),
            grid=grid,
            in_specs=in_specs,
            out_specs=out_specs,
            scratch_shapes=list(scratch),
        ),
        out_shape=out_shape,
        input_output_aliases=aliases or {},
        compiler_params=pltpu.CompilerParams(
            dimension_semantics=("arbitrary",) * len(grid), vmem_limit_bytes=VMEM_BYTES
        ),
        cost_estimate=pl.CostEstimate(flops=max(flops, 1), transcendentals=0, bytes_accessed=1),
    )(*scalars, *[a for a, _, _ in ins])


def tables_kernel(dims, table, info, mask_ref, one_ref, two_ref):
    groups, seqs, sub, nb, rows, tok_count, group_tokens = dims
    chunk = pl.program_id(0)
    me, ctx = info[0], info[1]
    span = nb * sub
    row = lax.broadcasted_iota(jnp.int32, (rows, 128), 0)
    col = lax.broadcasted_iota(jnp.int32, (rows, 128), 1)
    far = jnp.full((rows, 128), -9, jnp.int32)
    pos, first_src, second_src = far, far, far
    ends = [far] * (seqs - 1)
    names = [far] * seqs
    for b in range(nb):
        group = chunk * nb + b
        slot = jnp.int32(0)
        for s in range(groups):
            slot = slot + jnp.where(table[group, s] == me, s, 0)
        base = ctx * tok_count + slot * sub
        low, top = b * sub, (b + 1) * sub
        edge = span + 4 * b
        inner = (row >= low) & (row < top)
        before = (row >= edge) & (row < edge + 2)
        after = (row >= edge + 2) & (row < edge + 4)
        here = inner | before | after
        pos = jnp.where(inner, base + row - low, pos)
        pos = jnp.where(before, base - 2 + row - edge, pos)
        pos = jnp.where(after, base + sub + row - (edge + 2), pos)
        first_src = jnp.where(inner, jnp.where(row == low, edge + 1, row - 1), first_src)
        first_src = jnp.where(after, jnp.where(row == edge + 2, top - 1, row - 1), first_src)
        second_src = jnp.where(inner, jnp.where(row < low + 2, edge + row - low, row - 2), second_src)
        second_src = jnp.where(after, top - 2 + row - (edge + 2), second_src)
        end = jnp.int32(0)
        for j in range(seqs - 1):
            end = end + table[group, groups + j]
            ends[j] = jnp.where(here, end, ends[j])
        for j in range(seqs):
            names[j] = jnp.where(here, table[group, groups + seqs + j], names[j])

    def segment_of(positions):
        found = jnp.zeros((rows, 128), jnp.int32)
        for end in ends:
            found = found + jnp.where(positions >= end, 1, 0)
        return found

    segment = segment_of(pos)
    adapter = names[0]
    for j in range(1, seqs):
        adapter = jnp.where(segment == j, names[j], adapter)
    picked = (col >= adapter * RANK) & (col < adapter * RANK + RANK)
    mask_ref[...] = jnp.where(picked, 1.0, 0.0).astype(bf16)
    source = lax.broadcasted_iota(jnp.int32, (rows, rows), 1)
    for lag, src, ref in ((1, first_src, one_ref), (2, second_src, two_ref)):
        same = (pos >= lag) & (pos < group_tokens) & (segment_of(pos - lag) == segment)
        src = jnp.where(same, src, -9)
        ref[...] = jnp.where(source == src[:, :1], 1.0, 0.0).astype(bf16)


def edges_kernel(dims, table, info, edges_ref, first_ref, last_ref, next_ref, prev_ref):
    groups = dims
    me = info[0]
    for g in range(groups):
        slot = jnp.int32(0)
        for s in range(groups):
            slot = slot + jnp.where(table[g, s] == me, s, 0)
        first_ref[g] = edges_ref[table[g, 0], g, 0:4]
        last_ref[g] = edges_ref[table[g, groups - 1], g, 4:6]
        after = table[g, jnp.minimum(slot + 1, groups - 1)]
        before = table[g, jnp.maximum(slot - 1, 0)]
        rows = edges_ref[after, g, 0:4]
        next_ref[g] = jnp.where(slot < groups - 1, rows, jnp.zeros_like(rows))
        rows = edges_ref[before, g, 4:6]
        prev_ref[g] = jnp.where(slot > 0, rows, jnp.zeros_like(rows))


ACTUAL, STACK, INNER = 4, 12, 20


def stack_rows(info, own, got_first, got_second, halo_own, halo_got, stack, span, half, into):
    block = half // 4
    stack[:span, :half] = own[...]
    stack[:span, half:] = jnp.where(pl.program_id(0) == 0, got_first[...], got_second[...])
    stack[span:, :half] = halo_own[...]
    stack[span:, half:] = halo_got[...]
    for r in range(8):
        into[:, r * block : (r + 1) * block] = stack[:, lanes_at(info[STACK + r], block)]


def input_kernel(info, own, got_first, got_second, halo_own, halo_got, gain, first, mask, x_ref, lhs_ref, scale_ref, stack, first_rel, gain_rel):
    span, half = own.shape
    rows, width = x_ref.shape
    block = half // 4
    stack_rows(info, own, got_first, got_second, halo_own, halo_got, stack, span, half, x_ref)
    for r in range(8):
        first_rel[r * block : (r + 1) * block, :] = first[lanes_at(info[ACTUAL + r], block), :]
        gain_rel[:, r * block : (r + 1) * block] = gain[:, lanes_at(info[ACTUAL + r], block)]

    def visit(at):
        x = x_ref[at, :].astype(f32)
        scale = lax.rsqrt(jnp.mean(x * x, axis=-1, keepdims=True) + norm_eps)
        lhs_ref[at, :width] = (x * scale * gain_rel[0:1, :]).astype(bf16)
        scale_ref[at, :] = jnp.broadcast_to(scale, (scale.shape[0], 128))

    over_row_blocks(rows, 16, visit)
    lhs_ref[:, width:] = dot(lhs_ref[:, :width], first_rel[...]).astype(bf16) * mask[...]


def cotangent_kernel(info, own, got_first, got_second, halo_own, halo_got, second, mask, lhs_ref, stack, second_rel):
    span, half = own.shape
    width = 2 * half
    block = half // 4
    stack_rows(info, own, got_first, got_second, halo_own, halo_got, stack, span, half, lhs_ref)
    for r in range(8):
        second_rel[:, r * block : (r + 1) * block] = second[:, lanes_at(info[ACTUAL + r], block)]
    low = adapter_scale * dot_nt(lhs_ref[:, :width], second_rel[...])
    lhs_ref[:, width:] = low.astype(bf16) * mask[...]


def mixer_parts(refs, cuts):
    if len(cuts) == 1:
        return [[refs[0].at[j] for j in range(3)]], [refs[1]], refs[2:]
    ins = [[refs[0].at[k, j] for j in range(3)] for k in range(2)]
    outs = [refs[1].at[k] for k in range(2)]
    early = pl.program_id(0) < 2
    for k in range(4):
        first, second = refs[2 + 2 * k], refs[3 + 2 * k]
        tiles = [jnp.where(early, first[j], second[j]) for j in range(4)]
        ins.append(tiles[:3])
        outs.append(tiles[3])
    return ins, outs, refs[10:]


def mixer_kernel(cuts, lhs, one, two, taps, in_expand, out_shrink, *refs):
    in_parts, out_parts, refs = mixer_parts(refs, cuts)
    b_ref, c_ref, v_ref, conv_ref, gated_ref, part_first, part_second, acc = refs
    width = cuts[-1][1]
    step = pl.program_id(0)

    def project(j):
        total = dot(lhs[:, width:], in_expand[j] * jnp.asarray(adapter_scale, bf16))
        for (low, top), part in zip(cuts, in_parts):
            total = total + dot(lhs[:, low:top], part[j][...])
        return total

    b, c, v = project(0), project(1), project(2)
    b_ref[...] = b
    c_ref[...] = c
    v_ref[...] = v
    mixed = (b * v).astype(bf16)
    w = taps[...].astype(f32)
    conv = w[0:1] * mixed.astype(f32) + w[1:2] * dot(one[...], mixed) + w[2:3] * dot(two[...], mixed)
    conv_ref[...] = conv
    gated = (c * conv).astype(bf16)
    gated_ref[...] = gated

    @pl.when(step == 0)
    def _():
        acc[...] = jnp.zeros_like(acc)

    for (low, top), part in zip(cuts, out_parts):
        acc[:, low:top] += dot(gated, part[...])
    acc[:, width:] += dot(gated, out_shrink[...])

    @pl.when(step == pl.num_programs(0) - 1)
    def _():
        cut = part_first.shape[0]
        part_first[...] = acc[:cut, :].astype(bf16)
        part_second[...] = acc[cut:, :].astype(bf16)


def blocks_across(ref, value):
    for i in range(value.shape[1] // 128):
        ref[i] = value[:, i * 128 : (i + 1) * 128]


def blocks_down(ref, value):
    for i in range(value.shape[0] // 128):
        ref[i] = value[i * 128 : (i + 1) * 128, :]


def middle_kernel(info, x, part_first, part_second, got_first, got_second, mask, gain, out_second, ffn_first,
                  hidden_ref, lhs, low_ref, both_ref, added, first_rel, second_rel, gain_rel):
    width = x.shape[1]
    block = width // 8
    rank = mask.shape[1]
    for r in range(8):
        at = lanes_at(info[ACTUAL + r], block)
        here = slice(r * block, (r + 1) * block)
        first_rel[here, :] = ffn_first[at, :]
        second_rel[:, here] = out_second[:, at]
        gain_rel[:, here] = gain[:, at]
    cut = part_first.shape[0]
    for own, got, base in ((part_first, got_first, 0), (part_second, got_second, cut)):
        both_ref[base : base + own.shape[0], :] = own[...].astype(f32) + got[...].astype(f32)
    low = both_ref[:, width:].astype(bf16) * mask[...]
    low_ref[...] = low
    added[...] = dot(low, second_rel[...])

    def visit(at):
        hidden = x[at, :].astype(f32) + (both_ref[at, :width] + adapter_scale * added[at, :])
        hidden_ref[at, :] = hidden
        scale = lax.rsqrt(jnp.mean(hidden * hidden, axis=-1, keepdims=True) + norm_eps)
        lhs[at, :width] = (hidden * scale * gain_rel[0:1, :]).astype(bf16)

    over_row_blocks(x.shape[0], 16, visit)
    low = dot(lhs[:, :width], first_rel[...]).astype(bf16)
    lhs[:, width : width + rank] = low[:, :rank] * mask[...]
    lhs[:, width + rank :] = low[:, rank:] * mask[...]


def feed_kernel(cuts, span, info, lhs, glhs, ffn_expand, down_shrink, *refs):
    if len(cuts) == 1:
        gu_parts, down_parts, refs = [[refs[0].at[0], refs[0].at[1]]], [refs[1]], refs[2:]
        arrived = lambda: None
    else:
        gu_parts = [[refs[0].at[k, j] for j in range(2)] for k in range(2)]
        down_parts = [refs[1].at[k] for k in range(2)]
        count = len(FEED_CUTS)
        far, refs = refs[2 : 2 + 4 * count], refs[2 + 4 * count :]
        slots, sems, refs = refs[-2], refs[-1], refs[:-2]
        step, steps = pl.program_id(0), FEED_CUTS[-1][1]

        def fetch(tile):
            for i, (low, top) in enumerate(FEED_CUTS):

                @pl.when((tile >= low) & (tile < top))
                def _(i=i, low=low):
                    at = pl.ds(pl.multiple_of((tile - low) * TILE, TILE), TILE)
                    for k in range(4):
                        slot = lax.rem(tile, 2)
                        pltpu.make_async_copy(far[k * count + i].at[:, :, at], slots.at[slot, k], sems.at[slot, k]).start()

        @pl.when(step == 0)
        def _():
            fetch(step)

        @pl.when(step + 1 < steps)
        def _():
            fetch(step + 1)

        slot = lax.rem(step, 2)
        here = slots.at[slot]
        for k in range(4):
            gu_parts.append([here.at[k, 0], here.at[k, 1]])
            down_parts.append(here.at[k, 2])

        def arrived():
            for k in range(4):
                pltpu.make_async_copy(far[k * count].at[:, :, :TILE], slots.at[slot, k], sems.at[slot, k]).wait()
    f_ref, own_ref, send_ref, grads, acc_d, acc_f = refs
    width = cuts[-1][1]
    half = width // 2
    rank = down_shrink.shape[1]
    step = pl.program_id(0)

    @pl.when(step == 0)
    def _():
        acc_d[...] = jnp.zeros_like(acc_d)
        acc_f[...] = jnp.zeros_like(acc_f)

    arrived()
    lows = [lhs[:, width : width + rank], lhs[:, width + rank :]]
    half_scale = jnp.asarray(adapter_scale, bf16)

    def project(j):
        total = dot(lows[j], ffn_expand[j] * half_scale)
        for (low, top), w in zip(cuts, gu_parts):
            total = total + dot(lhs[:, low:top], w[j][...])
        return total

    gate, up = project(0), project(1)
    sig = jax.nn.sigmoid(gate)
    silu = gate * sig
    act = (silu * up).astype(bf16)
    g_low = glhs[:, width:]
    grad_act = dot_nt(g_low, down_shrink[...])
    for (low, top), w in zip(cuts, down_parts):
        grad_act = grad_act + dot_nt(glhs[:, low:top], w[...])
    gg = (grad_act * up * (sig * (1.0 + gate * (1.0 - sig)))).astype(bf16)
    gu = (grad_act * silu).astype(bf16)
    for (low, top), w in zip(cuts, down_parts):
        acc_d[:span, low:top] += dot(act[:span], w[...])
    acc_d[:span, width:] += dot(act[:span], down_shrink[...])
    for (low, top), w in zip(cuts, gu_parts):
        acc_f[:, low:top] += dot_nt(gg, w[0][...]) + dot_nt(gu, w[1][...])
    acc_f[:, width : width + rank] += dot_nt(gg, ffn_expand[0] * half_scale)
    acc_f[:, width + rank :] += dot_nt(gu, ffn_expand[1] * half_scale)
    blocks_down(grads.at[0], dot_tn(act[:span], g_low[:span]))
    blocks_across(grads.at[1], adapter_scale * dot_tn(lows[0][:span], gg[:span]))
    blocks_across(grads.at[2], adapter_scale * dot_tn(lows[1][:span], gu[:span]))

    @pl.when(step == pl.num_programs(0) - 1)
    def _():
        f_ref[...] = acc_f[...].astype(bf16)
        place = info[3]
        own_ref[:, :half] = acc_d[:span, lanes_at(place, half)].astype(bf16)
        send_ref[:, :half] = acc_d[:span, lanes_at(1 - place, half)].astype(bf16)
        own_ref[:, half:] = acc_d[:span, width:].astype(bf16)
        send_ref[:, half:] = acc_d[:span, width:].astype(bf16)


def back_kernel(cuts, span, info, part, got, hidden, glhs, lhs_two, out_low, lhs_one, mask, gain, out_second, ffn_first,
                one, two, taps, in_expand, out_shrink, b_ref, c_ref, v_ref, conv_ref, gated_ref, *refs):
    in_parts, out_parts, refs = mixer_parts(refs, cuts)
    (own_ref, send_ref, rank_ref, gh_ref, ffn_grad, second_grad, grads,
     acc, branch, first_rel, second_rel, gain_rel) = refs
    width = cuts[-1][1]
    half = width // 2
    block = width // 8
    rank = mask.shape[1]
    step = pl.program_id(0)
    place = info[3]

    @pl.when(step == 0)
    def _():
        for r in range(8):
            at = lanes_at(info[ACTUAL + r], block)
            here = slice(r * block, (r + 1) * block)
            first_rel[here, :] = ffn_first[at, :]
            second_rel[:, here] = out_second[:, at]
            gain_rel[:, here] = gain[:, at]
        low = (part[:, width:].astype(f32) + got[:, width:].astype(f32)).astype(bf16)
        low = jnp.concatenate([low[:, :rank] * mask[...], low[:, rank:] * mask[...]], axis=1)
        acc[:, :width] = dot_nt(low, first_rel[...])

        def visit(at):
            both = part[at, :width].astype(f32) + got[at, :width].astype(f32)
            h = hidden[at, :]
            scale = lax.rsqrt(jnp.mean(h * h, axis=-1, keepdims=True) + norm_eps)
            unit = h * scale
            grad_unit = (both + acc[at, :width]) * gain_rel[0:1, :]
            grad = glhs[at, :width].astype(f32) + scale * (
                grad_unit - unit * jnp.mean(grad_unit * unit, axis=-1, keepdims=True)
            )
            gh_ref[at, :] = grad
            branch[at, :width] = grad.astype(bf16)

        over_row_blocks(hidden.shape[0], 16, visit)
        b_low = adapter_scale * dot_nt(branch[:, :width], second_rel[...])
        branch[:, width:] = b_low.astype(bf16) * mask[...]
        for i in range(4):
            at = lanes_at(place * 4 + info[INNER + i], block)
            value = dot_tn(lhs_two[:span, at], low[:span])
            for k in range(2):
                blocks_down(ffn_grad.at[i, k], value[:, k * 128 : (k + 1) * 128])
            blocks_across(second_grad.at[i], adapter_scale * dot_tn(out_low[:span, :], branch[:span, at]))
        acc[...] = jnp.zeros_like(acc)

    total = dot_nt(branch[:, width:], out_shrink[...])
    for (low, top), w in zip(cuts, out_parts):
        total = total + dot_nt(branch[:, low:top], w[...])
    grad_c = total * conv_ref[...]
    conv = total * c_ref[...]
    w = taps[...].astype(f32)
    high = conv.astype(bf16)
    rest = (conv - high.astype(f32)).astype(bf16)
    mixed = (
        w[0:1] * conv
        + w[1:2] * (dot_tn(one[...], high) + dot_tn(one[...], rest))
        + w[2:3] * (dot_tn(two[...], high) + dot_tn(two[...], rest))
    )
    proj = [
        (mixed * v_ref[...]).astype(bf16)[:span],
        grad_c.astype(bf16)[:span],
        (mixed * b_ref[...]).astype(bf16)[:span],
    ]
    half_scale = jnp.asarray(adapter_scale, bf16)
    for (low, top), w in zip(cuts, in_parts):
        acc[:span, low:top] += dot_nt(proj[0], w[0][...]) + dot_nt(proj[1], w[1][...]) + dot_nt(proj[2], w[2][...])
    acc[:span, width:] += (
        dot_nt(proj[0], in_expand[0] * half_scale)
        + dot_nt(proj[1], in_expand[1] * half_scale)
        + dot_nt(proj[2], in_expand[2] * half_scale)
    )
    low_one = lhs_one[:span, width:]
    for j in range(3):
        blocks_across(grads.at[j], adapter_scale * dot_tn(low_one, proj[j]))
    blocks_down(grads.at[3], dot_tn(gated_ref[:span, :], branch[:span, width:]))

    @pl.when(step == pl.num_programs(0) - 1)
    def _():
        own_ref[...] = acc[:span, lanes_at(place, half)].astype(bf16)
        send_ref[...] = acc[:span, lanes_at(1 - place, half)].astype(bf16)
        rank_ref[:, :rank] = acc[:span, width:].astype(bf16)

        def visit(at):
            sums = acc[at, :width].astype(bf16).astype(f32) * lhs_one[at, :width].astype(f32)
            stat = jnp.sum(sums, axis=-1, keepdims=True)
            high = stat.astype(bf16).astype(f32)
            middle = (stat - high).astype(bf16).astype(f32)
            rest = stat - high - middle
            lane = lax.broadcasted_iota(jnp.int32, (stat.shape[0], 128), 1)
            packed = jnp.where(lane == 0, high, jnp.where(lane == 1, middle, jnp.where(lane == 2, rest, 0.0)))
            rank_ref[at, rank:] = packed.astype(bf16)

        over_row_blocks(span, 16, visit)


def rank_rows(own, got, mask):
    rank = mask.shape[1]
    sums = own[...].astype(f32) + got[...].astype(f32)
    return sums[:, :rank].astype(bf16) * mask[...], sums[:, rank:]


def output_kernel(info, *refs):
    output_rows(info, *refs[:8], *refs[-2:])


def output_rows(info, own, got, rank_own, rank_got, hidden, mask, g, second, out_ref, grad_ref):
    low, _ = rank_rows(rank_own, rank_got, mask)
    down = own[...].astype(f32) + got[...].astype(f32)
    out_ref[...] = (hidden[...] + (down + adapter_scale * dot(low, second[...]))).astype(bf16)
    blocks_across(grad_ref, adapter_scale * dot_tn(low, g[...]))


def rank_kernel(info, own, got, mask, normed, grad_ref):
    low, _ = rank_rows(own, got, mask)
    blocks_down(grad_ref, dot_tn(normed[...], low))


def final_kernel(width, info, *refs):
    final_rows(width, info, *refs[:11], refs[-1])


def final_rows(width, info, own, got, rank_own, rank_got, gh, x, low, scale, mask, gain, first, grad_ref):
    n_low, stat = rank_rows(rank_own, rank_got, mask)
    stat = jnp.sum(stat, axis=-1, keepdims=True)
    stat = stat + jnp.sum(n_low.astype(f32) * low[...].astype(f32), axis=-1, keepdims=True)
    stat = stat / width
    scale_rows = scale[:, 0:1]
    unit = x[...].astype(f32) * scale_rows
    grad = own[...].astype(f32) + got[...].astype(f32) + dot_nt(n_low, first[...])
    grad_ref[...] = gh[...] + scale_rows * (grad * gain[0:1, :].astype(f32) - unit * stat)


def places(info, pieces):
    me, ctx = info[0], info[1]
    for place in range(4 * pieces):
        c, x, z = place // (2 * pieces), place // pieces % 2, place % pieces
        far_c, far_x = (me % 2) ^ c, (me // 2) ^ x
        yield place, 2 * far_c + far_x, lax.rem(ctx + pieces - z, pieces)


def unpack_feed_kernel(tiles, total, expand_ref, first_ref):
    for h in range(tiles):
        for k in range(2):
            column = h * 256 + k * 128
            for j in range(3):
                row = ((h * 3 + j) * 2 + k) * 128
                value = total[row : row + 128, :].astype(f32)
                if j:
                    expand_ref[j - 1, :, column : column + 128] = value
                else:
                    first_ref[column : column + 128, :] = value


def gather_feed_kernel(pieces, tiles, info, own, x, c, cx, expand_ref, first_ref, kept):
    n = own.shape[1]
    for place, which, distance in places(info, pieces):
        for k, part in enumerate((own, x, c, cx)):

            @pl.when(which == k)
            def _(part=part, place=place, distance=distance):
                kept[place * n : (place + 1) * n, :] = part[distance]

    unpack_feed_kernel(tiles, kept, expand_ref, first_ref)


def gather_rows_kernel(pieces, info, own, x, c, cx, out):
    for place, which, distance in places(info, pieces):
        for k, part in enumerate((own, x, c, cx)):

            @pl.when(which == k)
            def _(part=part, place=place, distance=distance):
                out[place] = part[distance]


def unpack_early_kernel(pieces, info, own, x, c, cx, ffn_ref, second_ref, expand_ref, out_ref, kept):
    gather_rows_kernel(pieces, info, own, x, c, cx, kept)
    tens = info[2]
    for place in range(4 * pieces):
        i, k, part = place // 4, place // 2 % 2, place % 2
        for t in range(2):
            base = pl.multiple_of(jnp.where(tens == t, 0, 192), 64)
            ffn_ref[t * 1024 + i * 256 + part * 128 : t * 1024 + i * 256 + part * 128 + 128, k * 128 : (k + 1) * 128] = (
                kept[place, pl.ds(base, 128), :].astype(f32)
            )
            column = t * 1024 + i * 256 + k * 128
            second_ref[part * 64 : part * 64 + 64, column : column + 128] = kept[
                place, pl.ds(pl.multiple_of(base + 128, 64), 64), :
            ].astype(f32)
        h, j = place // 4, place % 4
        for k in range(2):
            value = kept[place, 384 + k * 128 : 512 + k * 128, :].astype(f32)
            column = h * 256 + k * 128
            if j < 3:
                expand_ref[j, :, column : column + 128] = value
            else:
                out_ref[column : column + 128, :] = value


def unpack_late_kernel(pieces, info, own, x, c, cx, first_ref, second_ref, kept):
    gather_rows_kernel(pieces, info, own, x, c, cx, kept)
    tens = info[2]
    for place in range(4 * pieces):
        for t in range(2):
            base = pl.multiple_of(jnp.where(tens == t, 0, 128), 128)
            row = t * 1024 + place * 64
            first_ref[row : row + 64, :] = kept[place, pl.ds(base, 64), :].astype(f32)
            row, column = place % 2 * 64, t * 1024 + place // 2 * 128
            second_ref[row : row + 64, column : column + 128] = kept[
                place, pl.ds(pl.multiple_of(base + 64, 64), 64), :
            ].astype(f32)


def after(array, *gates):
    return lax.optimization_barrier((array,) + gates)[0] if gates else array


def swap_tensor(array):
    return lax.ppermute(array, "tensor", [(0, 1), (1, 0)])


def body(
    block_input,
    cotangent,
    deal_order,
    seq_lengths,
    seq_adapter,
    mixer_gain,
    ffn_gain,
    conv_taps,
    in_weight,
    out_weight,
    gateup_weight,
    down_weight,
    input_adapter_shrink,
    in_expand,
    out_shrink,
    output_adapter_expand,
    ffn_shrink,
    ffn_expand,
    down_shrink,
    down_adapter_expand,
):
    tok_count, half = block_input.shape
    width = 2 * half
    rank = input_adapter_shrink.shape[1]
    hidden_units = gateup_weight.shape[2]
    groups = lax.axis_size("dp")
    pieces = lax.axis_size("ctx")
    sub = tok_count // groups
    group_tokens = pieces * tok_count
    seqs = seq_lengths.shape[0]
    nb = groups // CHUNKS
    span = nb * sub
    halo = -(-4 * nb // 16) * 16
    rows = span + halo
    special = groups == 4 and pieces % 2 == 0
    me = lax.axis_index("dp")
    ctx = lax.axis_index("ctx")
    tens = lax.axis_index("tensor")
    if special:
        xb, cb, zb = me // 2, me % 2, ctx % 2
    else:
        xb = cb = zb = jnp.int32(0)
    flip = xb ^ tens

    actual, in_stack, inner = [], [], []
    for rx in (0, 1):
        for rc in (0, 1):
            for rh in (0, 1):
                low = (rc ^ (cb & rx)) * 2 + (rh ^ (zb & rx))
                actual.append((rx ^ xb) * 4 + low)
                in_stack.append((rx ^ flip) * 4 + low)
    for bc in (0, 1):
        for bh in (0, 1):
            inner.append((bc ^ (cb & flip)) * 2 + (bh ^ (zb & flip)))
    info = jnp.stack([me, ctx, tens, flip, *actual, *in_stack, *inner]).astype(jnp.int32)

    core_route = [(0, 1), (1, 0), (2, 3), (3, 2)]
    x_route = [(0, 2), (2, 0), (1, 3), (3, 1)]
    z_route = [(i, i ^ 1) for i in range(pieces)]
    gates = []

    def wait(*values):
        gates[:] = values

    def begin(axis, route, array):
        return lax.ppermute(after(array, *gates), axis, route)

    def core(array):
        return begin("dp", core_route, array)

    def over_x(array):
        return begin("dp", x_route, array)

    def over_z(array):
        return begin("ctx", z_route, array)

    def over_y(array):
        return begin("tensor", [(0, 1), (1, 0)], array)

    def tiles_beside(array):
        tiles = array.reshape(-1, TILE, array.shape[1])
        return jnp.concatenate([tiles[i] for i in range(tiles.shape[0])], axis=1)

    def mixer_piece(k):
        at = slice(k * half // 2, (k + 1) * half // 2)
        return jnp.concatenate([mine(in_weight[:, :, at], 1), tiles_beside(mine(out_weight[at], 1))[None]], axis=0)

    def feed_piece(k):
        low, top = FEED_CUTS[k]
        at = slice(low * TILE, top * TILE)
        return jnp.concatenate([mine(gateup_weight[:, :, at], 1), tiles_beside(mine(down_weight[at], 1))[None]], axis=0)

    def chip_pair(array):
        return lax.all_gather(after(array, *gates), "dp", axis_index_groups=[[0, 1], [2, 3]])

    def mine(shard, axis):
        n = shard.shape[axis] // 2
        return lax.dynamic_slice_in_dim(shard, zb * n, n, axis)

    numbers = jnp.concatenate([deal_order[0], seq_lengths, seq_adapter])
    digits = jnp.concatenate([numbers // 64, numbers % 64]).astype(bf16)
    x_blocks = block_input.reshape(groups, sub, half)
    g_blocks = cotangent.reshape(groups, sub, half)
    digit_rows = jnp.zeros((groups, 2, half), bf16).at[0, 0, : digits.shape[0]].set(digits)
    edges = jnp.concatenate([x_blocks[:, :2], g_blocks[:, :2], x_blocks[:, sub - 2 :], digit_rows], axis=1)

    if special:
        in_own = chip_pair(in_weight)
        mixer_x, mixer_z, mixer_xc, mixer_zc = ([None] * 2 for _ in range(4))
        feed_x, feed_z, feed_xc, feed_zc = ([None] * len(FEED_CUTS) for _ in range(4))
        mixer_packed = [mixer_piece(k) for k in range(2)]
        feed_packed = [feed_piece(k) for k in range(len(FEED_CUTS))]
    x_got = [over_y(block_input[:span]), None]
    if special:
        mixer_x[0] = over_x(mixer_packed[0])
    all_edges = lax.all_gather(edges, "dp", axis=0, tiled=False)
    digits = all_edges[:, 0, 6, : 2 * numbers.shape[0]].astype(jnp.int32)
    table = digits[:, : numbers.shape[0]] * 64 + digits[:, numbers.shape[0] :]
    dims = (groups, seqs, sub, nb, rows, tok_count, group_tokens)
    per_chunk = lambda c, *_: (c, 0, 0)
    mask, one, two = call(
        functools.partial(tables_kernel, dims), (CHUNKS,), (table, info), [],
        [
            ((CHUNKS, rows, rank), bf16, (None, rows, rank), per_chunk),
            ((CHUNKS, rows, rows), bf16, (None, rows, rows), per_chunk),
            ((CHUNKS, rows, rows), bf16, (None, rows, rows), per_chunk),
        ],
    )
    first_heads, last_tails, next_near, prev_near = call(
        functools.partial(edges_kernel, groups), (1,), (table, info), [(all_edges, None, None)],
        [
            ((groups, 4, half), bf16, None, None),
            ((groups, 2, half), bf16, None, None),
            ((groups, 4, half), bf16, None, None),
            ((groups, 2, half), bf16, None, None),
        ],
    )
    stage = [all_edges, x_got[0]] + ([mixer_x[0], in_own, mixer_packed[1], feed_packed[0]] if special else [])
    wait(*stage)
    from_next = begin("ctx", [(i + 1, i) for i in range(pieces - 1)], first_heads)
    from_prev = begin("ctx", [(i, i + 1) for i in range(pieces - 1)], last_tails)
    x_got[1] = over_y(block_input[span:])
    stage = [from_next, from_prev, x_got[1]]
    if special:
        mixer_x[1], mixer_z[0] = over_x(mixer_packed[1]), over_z(mixer_x[0])
        out_own = chip_pair(out_weight)
        stage += [mixer_x[1], mixer_z[0], out_own]
    deal_all = table[:, :groups]
    at_end = (deal_all[:, groups - 1] == me)[:, None, None]
    at_start = (deal_all[:, 0] == me)[:, None, None]
    next_rows = jnp.where(at_end, from_next, next_near)
    prev_rows = jnp.where(at_start, from_prev, prev_near)
    halo_x = jnp.concatenate([prev_rows, next_rows[:, :2]], axis=1)
    halo_g = jnp.concatenate([jnp.zeros_like(prev_rows), next_rows[:, 2:]], axis=1)
    halo_own = jnp.stack([halo_x, halo_g]).reshape(2, CHUNKS, 4 * nb, half)
    halo_own = jnp.pad(halo_own, ((0, 0), (0, 0), (0, halo - 4 * nb), (0, 0)))
    wait(*stage)
    halo_got = over_y(halo_own)
    g_got = [over_y(after(cotangent[:span], halo_got)), None]
    stage = [g_got[0]]
    if special:
        feed_x[0], mixer_z[1] = over_x(feed_packed[0]), over_z(mixer_x[1])
        mixer_xc[0] = core(mixer_x[0])
        mixer_xc[1] = core(after(mixer_x[1], mixer_xc[0]))
        mixer_zc[0] = core(after(mixer_z[0], mixer_xc[1]))
        gu_own = chip_pair(gateup_weight)
        stage += [feed_x[0], mixer_z[1], mixer_xc[0], mixer_xc[1], mixer_zc[0], feed_packed[1]]

    gain_one, gain_two = mixer_gain[None, :].astype(f32), ffn_gain[None, :].astype(f32)
    ext_one, ext_two = width + rank, width + 2 * rank

    def stacked(array, last):
        return (array, (None,) + array.shape[1:], lambda c, *_: (c, 0, 0))

    def joined_inputs(own, got, which):
        def halo_of(array):
            return (array, (None, None, halo, half), lambda c, *_: (which, c, 0, 0))

        return [
            (own, (span, half), lambda c, *_: (c, 0)),
            (got[0], None, None),
            (got[1], None, None),
            halo_of(halo_own),
            halo_of(halo_got),
        ]

    x_full, lhs_one, scale = call(
        input_kernel, (CHUNKS,), (info,),
        joined_inputs(block_input, x_got, 0)
        + [(gain_one, None, None), (input_adapter_shrink, None, None), stacked(mask, rank)],
        [
            ((CHUNKS, rows, width), bf16, (None, rows, width), per_chunk),
            ((CHUNKS, rows, ext_one), bf16, (None, rows, ext_one), per_chunk),
            ((CHUNKS, rows, 128), f32, (None, rows, 128), per_chunk),
        ],
        [
            pltpu.VMEM((rows, width), bf16),
            pltpu.VMEM((width, rank), bf16),
            pltpu.VMEM((1, width), f32),
        ],
    )
    wait(*stage, lhs_one)
    g_got[1] = over_y(cotangent[span:])
    stage = [g_got[1]]
    if special:
        n = width // 8
        cuts = ((0, 2 * n), (2 * n, 4 * n), (4 * n, 5 * n), (5 * n, 6 * n), (6 * n, 7 * n), (7 * n, 8 * n))
        mixer_zc[1] = core(mixer_z[1])
        feed_x[1], feed_z[0], feed_xc[0] = over_x(feed_packed[1]), over_z(feed_x[0]), core(feed_x[0])
        stage += [feed_x[1], feed_z[0], feed_xc[0], feed_packed[2]]
        mixer_inputs = lambda: (
            [(in_own, (2, 3, in_own.shape[2], TILE), lambda h, *_: (0, 0, 0, h)),
             (out_own, (2, TILE, out_own.shape[2]), lambda h, *_: (0, h, 0))]
            + [(w, (4, TILE, TILE), (lambda h, *_: (0, 0, jnp.minimum(h, 1))) if i == 0 else (lambda h, *_: (0, 0, jnp.maximum(h - 2, 0))))
               for part in (mixer_x, mixer_z, mixer_xc, mixer_zc) for i, w in enumerate(part)]
        )
    else:
        cuts = ((0, width),)
        in_parts = [lax.all_gather(in_weight, "dp", axis=1, tiled=True)]
        out_parts = [lax.all_gather(out_weight, "dp", axis=1, tiled=True)]
        gu_parts = [lax.all_gather(gateup_weight, "dp", axis=1, tiled=True)]
        down_parts = [lax.all_gather(down_weight, "dp", axis=1, tiled=True)]
        mixer_inputs = lambda: [columns(in_parts[0]), row_tiles(out_parts[0])]

    def picked(array, c):
        return (array, (None,) + array.shape[1:], lambda *_: (c, 0, 0))

    def columns(array):
        return (array, array.shape[:-1] + (TILE,), lambda h, *_: (0,) * (array.ndim - 1) + (h,))

    def row_tiles(array):
        lead = array.ndim - 2
        return (array, array.shape[:lead] + (TILE, array.shape[-1]), lambda h, *_: (0,) * lead + (h, 0))

    def feed_step(k):
        count = len(FEED_CUTS)
        if k < count:
            feed_x[k] = over_x(feed_packed[k])
            stage.extend([feed_x[k]] + feed_packed[k + 1 : k + 2])
        if 0 <= k - 1 < count:
            feed_z[k - 1], feed_xc[k - 1] = over_z(feed_x[k - 1]), core(feed_x[k - 1])
            stage.extend([feed_z[k - 1], feed_xc[k - 1]])
        if 0 <= k - 2 < count:
            feed_zc[k - 2] = core(feed_z[k - 2])
            stage.append(feed_zc[k - 2])

    mixer_steps = half // TILE
    feed_steps = hidden_units // TILE
    column_out = lambda h, *_: (0, h)
    row_halves = (rows // 32 * 16, rows - rows // 32 * 16)
    chunks = []
    for c in range(CHUNKS):
        gate_b, gate_c, values, conv, gated, *part = call(
            functools.partial(mixer_kernel, cuts), (mixer_steps,), (),
            [picked(lhs_one, c), picked(one, c), picked(two, c), columns(conv_taps), columns(in_expand), row_tiles(out_shrink)]
            + mixer_inputs(),
            [((rows, half), f32, (rows, TILE), column_out)] * 4
            + [((rows, half), bf16, (rows, TILE), column_out)]
            + [((n, ext_one), bf16, None, None) for n in row_halves],
            [pltpu.VMEM((rows, ext_one), f32)],
            flops=2 * rows * half * ext_one * 4,
        )
        chunks.append(dict(b=gate_b, c=gate_c, v=values, conv=conv, gated=gated, part=part))
        if c == 0:
            wait(*stage, *part)
            chunks[0]["got"] = [over_y(part[0]), None]
            stage = [chunks[0]["got"][0]]
            if special:
                feed_step(2)
                down_own = chip_pair(down_weight)
    def middle(i):
        c = chunks[i]
        c["hidden"], c["lhs"], c["low"] = call(
            middle_kernel, (1,), (info,),
            [picked(x_full, i)] + [(w, None, None) for w in (*c["part"], *c["got"])]
            + [picked(mask, i), (gain_two, None, None), (output_adapter_expand, None, None), (ffn_shrink, None, None)],
            [((rows, width), f32, None, None), ((rows, ext_two), bf16, None, None), ((rows, rank), bf16, None, None)],
            [
                pltpu.VMEM((rows, ext_one), f32),
                pltpu.VMEM((rows, width), f32),
                pltpu.VMEM((width, 2 * rank), bf16),
                pltpu.VMEM((rank, width), bf16),
                pltpu.VMEM((1, width), f32),
            ],
        )

    wait(*stage, *chunks[1]["part"])
    chunks[0]["got"][1] = over_y(chunks[0]["part"][1])
    stage = [chunks[0]["got"][1]]
    if special:
        feed_step(3)
    wait(*stage)
    chunks[1]["got"] = [over_y(chunks[1]["part"][0]), None]
    stage = [chunks[1]["got"][0]]
    if special:
        feed_step(4)
    (glhs,) = call(
        cotangent_kernel, (CHUNKS,), (info,),
        joined_inputs(cotangent, g_got, 1) + [(down_adapter_expand, None, None), stacked(mask, rank)],
        [((CHUNKS, rows, ext_one), bf16, (None, rows, ext_one), per_chunk)],
        [pltpu.VMEM((rows, width), bf16), pltpu.VMEM((rank, width), bf16)],
    )

    wait(*stage, glhs)
    chunks[1]["got"][1] = over_y(chunks[1]["part"][1])
    stage = [chunks[1]["got"][1]]
    middle(0)
    middle(1)
    if special:
        feed_step(5)
        wait(*stage, chunks[0]["lhs"])
        stage = [chunks[1]["lhs"]]
        feed_step(6)
        wait(*stage)
        feed_step(7)
        whole = [(gu_own, (2, 2, gu_own.shape[2], TILE), lambda h, *_: (0, 0, 0, h)),
                 (down_own, (2, TILE, down_own.shape[2]), lambda h, *_: (0, h, 0))]
        feed_inputs = whole + [(w, "any", None) for part in (feed_x, feed_z, feed_xc, feed_zc) for w in part]
    else:
        feed_inputs = [columns(gu_parts[0]), row_tiles(down_parts[0])]

    for i, c in enumerate(chunks):
        f_part, d_own, d_send, grads = call(
            functools.partial(feed_kernel, cuts, span), (feed_steps,), (info,),
            [(c["lhs"], None, None), picked(glhs, i), columns(ffn_expand), row_tiles(down_shrink)]
            + feed_inputs,
            [
                ((rows, ext_two), bf16, None, None),
                ((span, half + rank), bf16, None, None),
                ((span, half + rank), bf16, None, None),
                ((feed_steps, 3, 2, 128, 128), f32, (None, 3, 2, 128, 128), lambda h, *_: (h, 0, 0, 0, 0)),
            ],
            [
                pltpu.VMEM((rows, ext_one), f32),
                pltpu.VMEM((rows, ext_two), f32),
            ]
            + ([pltpu.VMEM((2, 4, 3, TILE, TILE), bf16), pltpu.SemaphoreType.DMA((2, 4))] if special else []),
            flops=2 * rows * hidden_units * ext_two * 6,
        )
        c.update(f_own=f_part, d_own=d_own, d_send=d_send, feed_grads=grads)
    def summed(name):
        return sum(c[name] for c in chunks).astype(bf16)

    def take(array, i):
        return lax.dynamic_index_in_dim(array, i, 0, keepdims=False)

    def add(*terms):
        return sum(t.astype(f32) for t in terms).astype(bf16)

    core_bit, x_bit = me % 2, me // 2
    shifts = [[(i, (i + k) % pieces) for i in range(pieces)] for k in range(1, pieces)]

    def cut(*arrays):
        return jnp.concatenate([a.reshape(2, 2, pieces, -1, 128) for a in arrays], axis=3)

    def scatter_core(total):
        return add(take(total, core_bit), lax.ppermute(take(total, 1 - core_bit), "dp", core_route))

    def scatter_x(total):
        return add(take(total, x_bit), lax.ppermute(take(total, 1 - x_bit), "dp", x_route))

    def scatter_z(total):
        sent = [lax.ppermute(take(total, (ctx + k) % pieces), "ctx", route) for k, route in enumerate(shifts, 1)]
        return add(take(total, ctx), *sent)

    def gather_z(total):
        return jnp.stack([total] + [lax.ppermute(total, "ctx", route) for route in shifts])

    def gather_chip(total):
        over_x = lax.ppermute(total, "dp", x_route)
        return [total, over_x] + [lax.ppermute(v, "dp", core_route) for v in (total, over_x)]

    for c in chunks:
        c["f_got"] = swap_tensor(c["f_own"])
    feed = summed("feed_grads")
    if special:
        feed_sum = scatter_core(cut(after(feed, chunks[0]["f_got"])))
    for i, c in enumerate(chunks):
        f_got = after(c["f_got"], *([feed_sum] if special else []), *([chunks[0]["n_rank"]] if i else []))
        n_own, n_send, n_rank, grad_hidden, ffn_grad, second_grad, grads = call(
            functools.partial(back_kernel, cuts, span), (mixer_steps,), (info,),
            [(c["f_own"], None, None), (f_got, None, None), (c["hidden"], None, None), picked(glhs, i),
             (c["lhs"], None, None), (c["low"], None, None), picked(lhs_one, i), picked(mask, i),
             (gain_two, None, None), (output_adapter_expand, None, None), (ffn_shrink, None, None),
             picked(one, i), picked(two, i), columns(conv_taps), columns(in_expand), row_tiles(out_shrink),
             columns(c["b"]), columns(c["c"]), columns(c["v"]), columns(c["conv"]), columns(c["gated"])]
            + mixer_inputs(),
            [
                ((span, half), bf16, None, None),
                ((span, half), bf16, None, None),
                ((span, 2 * rank), bf16, None, None),
                ((rows, width), f32, None, None),
                ((4, 2, 2, 128, 128), f32, None, None),
                ((4, 2, 128, 128), f32, None, None),
                ((mixer_steps, 4, 2, 128, 128), f32, (None, 4, 2, 128, 128), lambda h, *_: (h, 0, 0, 0, 0)),
            ],
            [
                pltpu.VMEM((rows, ext_one), f32),
                pltpu.VMEM((rows, ext_one), bf16),
                pltpu.VMEM((width, 2 * rank), bf16),
                pltpu.VMEM((rank, width), bf16),
                pltpu.VMEM((1, width), f32),
            ],
            flops=2 * rows * half * ext_one * 4,
        )
        c.update(n_own=n_own, n_send=n_send, n_rank=n_rank, gh=grad_hidden, ffn_grad=ffn_grad, second_grad=second_grad, mixer_grads=grads)
        if special:
            feed_sum = scatter_x(feed_sum) if i == 0 else feed_sum
    for c in chunks:
        c["d_got"] = swap_tensor(after(c["d_send"], chunks[0]["f_got"]))
    chunks[0]["n_got"] = swap_tensor(chunks[0]["n_send"])
    if special:
        feed_sum = scatter_z(feed_sum)
        early = cut(after(summed("ffn_grad"), feed_sum, *(c["d_got"] for c in chunks)), summed("second_grad"), summed("mixer_grads"))
        early = scatter_core(early)
        first_step = (early,)
    else:
        first_step = ()

    block = half // 4
    in_half = lambda i, info: (0, info[INNER + i])
    in_full = lambda i, info: (0, info[3] * 4 + info[INNER + i])
    whole_block = lambda i, info: (0, 0)
    grad_out = ((4, 2, 128, 128), f32, (None, 2, 128, 128), lambda i, info: (i, 0, 0, 0))
    for k, c in enumerate(chunks):
        in_stack_full = lambda i, info, k=k: (k, 0, info[3] * 4 + info[INNER + i])
        masks = (mask, (None, span, rank), lambda i, info, k=k: (k, 0, 0))
        d_got = after(c["d_got"], *first_step)
        c["out"], c["down_grad"] = call(
            output_kernel, (4,), (info,),
            [
                (c["d_own"], (span, block), in_half),
                (d_got, (span, block), in_half),
                (c["d_own"], (span, rank), lambda i, info: (0, half // rank)),
                (d_got, (span, rank), lambda i, info: (0, half // rank)),
                (c["hidden"], (span, block), in_full),
                masks,
                (glhs, (None, span, block), in_stack_full),
                (down_adapter_expand, (rank, block), lambda i, info: (0, info[2] * 4 + i)),
            ]
            + ([(chunks[0]["out"], "any", None)] if k else []),
            [((tok_count, half), bf16, (span, block), lambda i, info, k=k: (k, i)), grad_out],
            flops=5 * 10**9,
            aliases={9: 0} if k else None,
        )
    wait()
    if special:
        feed_sum = gather_z(after(feed_sum, early))
        early = after(scatter_x(early), feed_sum, chunks[-1]["out"], chunks[0]["n_got"])
        second_step = (early,)
    else:
        second_step = ()
    for c in chunks[::-1]:
        c["rank_got"] = swap_tensor(after(c["n_rank"], *second_step))
    for k, c in enumerate(chunks):
        in_stack_full = lambda i, info, k=k: (k, 0, info[3] * 4 + info[INNER + i])
        masks = (mask, (None, span, rank), lambda i, info, k=k: (k, 0, 0))
        ranks = [(w, (span, 2 * rank), whole_block) for w in (c["n_rank"], c["rank_got"])]
        (c["in_grad"],) = call(
            rank_kernel, (4,), (info,), ranks + [masks, (lhs_one, (None, span, block), in_stack_full)], [grad_out],
            flops=5 * 10**9,
        )
    if special:
        feed_parts = [feed_sum, begin("dp", x_route, after(feed_sum, early))]
        early = after(scatter_z(early), feed_parts[1], *(c["in_grad"] for c in chunks))
        late = scatter_core(cut(summed("in_grad"), summed("down_grad")))
        h = 3 * 1024 // (4 * pieces)
        early = jnp.concatenate([early[:h], swap_tensor(early[:h]), early[h:]], axis=0)
        third_step = (early,)
    else:
        third_step = ()
    chunks[1]["n_got"] = swap_tensor(after(chunks[1]["n_send"], *third_step))
    for k, c in enumerate(chunks):
        in_stack_full = lambda i, info, k=k: (k, 0, info[3] * 4 + info[INNER + i])
        masks = (mask, (None, span, rank), lambda i, info, k=k: (k, 0, 0))
        ranks = [(w, (span, 2 * rank), whole_block) for w in (c["n_rank"], c["rank_got"])]
        n_got = after(c["n_got"], *third_step)
        (c["grad"],) = call(
            functools.partial(final_kernel, width), (4,), (info,),
            [(c["n_own"], (span, block), in_half), (n_got, (span, block), in_half)]
            + ranks
            + [
                (c["gh"], (span, block), in_full),
                (x_full, (None, span, block), in_stack_full),
                (lhs_one, (None, span, rank), lambda i, info, k=k: (k, 0, width // rank)),
                (scale, (None, span, 128), lambda i, info, k=k: (k, 0, 0)),
                masks,
                (gain_one, (1, block), lambda i, info: (0, info[2] * 4 + i)),
                (input_adapter_shrink, (block, rank), lambda i, info: (info[2] * 4 + i, 0)),
            ]
            + ([(chunks[0]["grad"], "any", None)] if k else []),
            [((tok_count, half), f32, (span, block), lambda i, info, k=k: (k, i))],
            flops=6 * 10**9,
            aliases={12: 0} if k else None,
        )
    block_output, input_grad = chunks[-1]["out"], chunks[-1]["grad"]

    if special:
        late = scatter_x(after(late, early))
        gathered = after(gather_z(early), chunks[0]["grad"], chunks[1]["n_got"])
        late = scatter_z(after(late, gathered))
        n = 4 * pieces
        feed_parts = [after(v, gathered) for v in feed_parts]
        feed_parts += [lax.ppermute(v, "dp", core_route) for v in feed_parts]
        expand_grad, first_grad = call(
            functools.partial(gather_feed_kernel, pieces, feed_steps), (1,), (info,),
            [(v, None, None) for v in feed_parts],
            [((2, rank, hidden_units), f32, None, None), ((hidden_units, rank), f32, None, None)],
            [pltpu.VMEM((feed.size // 128, 128), bf16)],
            flops=5 * 10**9,
        )
        late = jnp.concatenate([late, swap_tensor(late)], axis=0)
        over = after(lax.ppermute(gathered, "dp", x_route), expand_grad, chunks[1]["grad"])
        parts = [gathered, over] + [lax.ppermute(v, "dp", core_route) for v in (gathered, over)]
        ffn_grad, second_grad, mixer_grad, out_grad = call(
            functools.partial(unpack_early_kernel, pieces), (1,), (info,), [(v, None, None) for v in parts],
            [((width, 2 * rank), f32, None, None), ((rank, width), f32, None, None), ((3, rank, half), f32, None, None),
             ((half, rank), f32, None, None)],
            [pltpu.VMEM((n,) + early.shape, bf16)],
        )
        parts = gather_chip(gather_z(late))
        in_grad, down_grad = call(
            functools.partial(unpack_late_kernel, pieces), (1,), (info,), [(v, None, None) for v in parts],
            [((width, rank), f32, None, None), ((rank, width), f32, None, None)],
            [pltpu.VMEM((n,) + late.shape, bf16)],
        )
    else:
        names = ("mixer_grads", "ffn_grad", "second_grad", "in_grad", "down_grad")
        feed, mixer, ffn_grad, second_grad, in_grad, down_grad = lax.psum(
            (feed, *(summed(name) for name in names)), ("dp", "ctx")
        )

        def whole(part, axis):
            got = swap_tensor(part)
            pair = [jnp.where(tens == 0, part, got), jnp.where(tens == 0, got, part)]
            return jnp.concatenate(pair, axis=axis).astype(f32)

        def across(blocks):
            return blocks.reshape(-1, 128, 128).transpose(1, 0, 2).reshape(128, -1)

        ffn_grad = whole(ffn_grad.transpose(0, 2, 3, 1, 4).reshape(half, 2 * rank), 0)
        second_grad, down_grad = whole(across(second_grad), 1), whole(across(down_grad), 1)
        in_grad = whole(in_grad.reshape(half, rank), 0)
        mixer_grad = jnp.stack([across(mixer[:, j]) for j in range(3)]).astype(f32)
        out_grad = mixer[:, 3].reshape(half, rank).astype(f32)
        expand_grad = jnp.stack([across(feed[:, j]) for j in (1, 2)]).astype(f32)
        first_grad = feed[:, 0].reshape(hidden_units, rank).astype(f32)
    return (
        block_output,
        input_grad,
        in_grad,
        mixer_grad,
        out_grad,
        second_grad,
        ffn_grad,
        expand_grad,
        first_grad,
        down_grad,
    )


def solution(mesh):
    placed = (
        P(("dp", "ctx"), "tensor"),
        P(("dp", "ctx"), "tensor"),
        P("dp", None),
        P("dp"),
        P("dp"),
        P(),
        P(),
        P(None, "tensor"),
        P(None, "dp", "tensor"),
        P("tensor", "dp"),
        P(None, "dp", "tensor"),
        P("tensor", "dp"),
        P(),
        P(None, None, "tensor"),
        P("tensor", None),
        P(),
        P(),
        P(None, None, "tensor"),
        P("tensor", None),
        P(),
    )
    return jax.shard_map(
        body,
        mesh=mesh,
        in_specs=placed,
        out_specs=(
            P(("dp", "ctx"), "tensor"),
            P(("dp", "ctx"), "tensor"),
            P(),
            P(None, None, "tensor"),
            P("tensor", None),
            P(),
            P(),
            P(None, None, "tensor"),
            P("tensor", None),
            P(),
        ),
        check_vma=False,
    )
```

```python
import functools

import jax
import jax.numpy as jnp
from jax import lax
from jax.experimental import pallas as pl
from jax.experimental.pallas import tpu as pltpu
from jax.sharding import PartitionSpec as P

RANK = 16
CHUNKS = 2
TILE = 256
FEED_CUTS = ((0, 2), (2, 4), (4, 6), (6, 8), (8, 10), (10, 11))
VMEM_BYTES = 56 * 1024 * 1024

norm_eps = 1e-05
adapter_scale = 0.5

f32 = jnp.float32
bf16 = jnp.bfloat16


def dot(left, right):
    return jnp.dot(left, right, preferred_element_type=f32)


def dot_nt(left, right):
    return lax.dot_general(left, right, (((1,), (1,)), ((), ())), preferred_element_type=f32)


def dot_tn(left, right):
    return lax.dot_general(left, right, (((0,), (0,)), ((), ())), preferred_element_type=f32)


def over_row_blocks(rows, step, visit):
    def one(i, carry):
        visit(pl.ds(pl.multiple_of(i * step, step), step))
        return carry

    lax.fori_loop(0, rows // step, one, 0, unroll=5 if rows % (5 * step) == 0 else 2)


def lanes_at(index, width):
    return pl.ds(pl.multiple_of(index * width, width), width)


def call(kernel, grid, scalars, ins, outs, scratch=(), flops=0, aliases=None):
    in_specs = []
    for array, block, index in ins:
        if block == "any":
            in_specs.append(pl.BlockSpec(memory_space=pl.ANY))
        elif block is None:
            zeros = (0,) * array.ndim
            in_specs.append(
                pl.BlockSpec(array.shape, lambda *_, z=zeros: z, pipeline_mode=pl.Buffered(1))
            )
        else:
            in_specs.append(pl.BlockSpec(block, index))
    out_specs, out_shape = [], []
    for shape, dtype, block, index in outs:
        zeros = (0,) * len(shape)
        out_specs.append(
            pl.BlockSpec(shape, lambda *_, z=zeros: z) if block is None else pl.BlockSpec(block, index)
        )
        out_shape.append(jax.ShapeDtypeStruct(shape, dtype))
    moved = sum(a.size * a.dtype.itemsize for a, _, _ in ins)
    return pl.pallas_call(
        kernel,
        grid_spec=pltpu.PrefetchScalarGridSpec(
            num_scalar_prefetch=len(scalars),
            grid=grid,
            in_specs=in_specs,
            out_specs=out_specs,
            scratch_shapes=list(scratch),
        ),
        out_shape=out_shape,
        input_output_aliases=aliases or {},
        compiler_params=pltpu.CompilerParams(
            dimension_semantics=("arbitrary",) * len(grid), vmem_limit_bytes=VMEM_BYTES
        ),
        cost_estimate=pl.CostEstimate(flops=max(flops, 1), transcendentals=0, bytes_accessed=1),
    )(*scalars, *[a for a, _, _ in ins])


def tables_kernel(dims, table, info, mask_ref, one_ref, two_ref):
    groups, seqs, sub, nb, rows, tok_count, group_tokens = dims
    chunk = pl.program_id(0)
    me, ctx = info[0], info[1]
    span = nb * sub
    row = lax.broadcasted_iota(jnp.int32, (rows, 128), 0)
    col = lax.broadcasted_iota(jnp.int32, (rows, 128), 1)
    far = jnp.full((rows, 128), -9, jnp.int32)
    pos, first_src, second_src = far, far, far
    ends = [far] * (seqs - 1)
    names = [far] * seqs
    for b in range(nb):
        group = chunk * nb + b
        slot = jnp.int32(0)
        for s in range(groups):
            slot = slot + jnp.where(table[group, s] == me, s, 0)
        base = ctx * tok_count + slot * sub
        low, top = b * sub, (b + 1) * sub
        edge = span + 4 * b
        inner = (row >= low) & (row < top)
        before = (row >= edge) & (row < edge + 2)
        after = (row >= edge + 2) & (row < edge + 4)
        here = inner | before | after
        pos = jnp.where(inner, base + row - low, pos)
        pos = jnp.where(before, base - 2 + row - edge, pos)
        pos = jnp.where(after, base + sub + row - (edge + 2), pos)
        first_src = jnp.where(inner, jnp.where(row == low, edge + 1, row - 1), first_src)
        first_src = jnp.where(after, jnp.where(row == edge + 2, top - 1, row - 1), first_src)
        second_src = jnp.where(inner, jnp.where(row < low + 2, edge + row - low, row - 2), second_src)
        second_src = jnp.where(after, top - 2 + row - (edge + 2), second_src)
        end = jnp.int32(0)
        for j in range(seqs - 1):
            end = end + table[group, groups + j]
            ends[j] = jnp.where(here, end, ends[j])
        for j in range(seqs):
            names[j] = jnp.where(here, table[group, groups + seqs + j], names[j])

    def segment_of(positions):
        found = jnp.zeros((rows, 128), jnp.int32)
        for end in ends:
            found = found + jnp.where(positions >= end, 1, 0)
        return found

    segment = segment_of(pos)
    adapter = names[0]
    for j in range(1, seqs):
        adapter = jnp.where(segment == j, names[j], adapter)
    picked = (col >= adapter * RANK) & (col < adapter * RANK + RANK)
    mask_ref[...] = jnp.where(picked, 1.0, 0.0).astype(bf16)
    source = lax.broadcasted_iota(jnp.int32, (rows, rows), 1)
    for lag, src, ref in ((1, first_src, one_ref), (2, second_src, two_ref)):
        same = (pos >= lag) & (pos < group_tokens) & (segment_of(pos - lag) == segment)
        src = jnp.where(same, src, -9)
        ref[...] = jnp.where(source == src[:, :1], 1.0, 0.0).astype(bf16)


def edges_kernel(dims, table, info, edges_ref, first_ref, last_ref, next_ref, prev_ref):
    groups = dims
    me = info[0]
    for g in range(groups):
        slot = jnp.int32(0)
        for s in range(groups):
            slot = slot + jnp.where(table[g, s] == me, s, 0)
        first_ref[g] = edges_ref[table[g, 0], g, 0:4]
        last_ref[g] = edges_ref[table[g, groups - 1], g, 4:6]
        after = table[g, jnp.minimum(slot + 1, groups - 1)]
        before = table[g, jnp.maximum(slot - 1, 0)]
        rows = edges_ref[after, g, 0:4]
        next_ref[g] = jnp.where(slot < groups - 1, rows, jnp.zeros_like(rows))
        rows = edges_ref[before, g, 4:6]
        prev_ref[g] = jnp.where(slot > 0, rows, jnp.zeros_like(rows))


ACTUAL, STACK, INNER = 4, 12, 20


def stack_rows(info, own, got_first, got_second, halo_own, halo_got, stack, span, half, into):
    block = half // 4
    stack[:span, :half] = own[...]
    stack[:span, half:] = jnp.where(pl.program_id(0) == 0, got_first[...], got_second[...])
    stack[span:, :half] = halo_own[...]
    stack[span:, half:] = halo_got[...]
    for r in range(8):
        into[:, r * block : (r + 1) * block] = stack[:, lanes_at(info[STACK + r], block)]


def input_kernel(info, own, got_first, got_second, halo_own, halo_got, gain, first, mask, x_ref, lhs_ref, scale_ref, stack, first_rel, gain_rel):
    span, half = own.shape
    rows, width = x_ref.shape
    block = half // 4
    stack_rows(info, own, got_first, got_second, halo_own, halo_got, stack, span, half, x_ref)
    for r in range(8):
        first_rel[r * block : (r + 1) * block, :] = first[lanes_at(info[ACTUAL + r], block), :]
        gain_rel[:, r * block : (r + 1) * block] = gain[:, lanes_at(info[ACTUAL + r], block)]

    def visit(at):
        x = x_ref[at, :].astype(f32)
        scale = lax.rsqrt(jnp.mean(x * x, axis=-1, keepdims=True) + norm_eps)
        lhs_ref[at, :width] = (x * scale * gain_rel[0:1, :]).astype(bf16)
        scale_ref[at, :] = jnp.broadcast_to(scale, (scale.shape[0], 128))

    over_row_blocks(rows, 16, visit)
    lhs_ref[:, width:] = dot(lhs_ref[:, :width], first_rel[...]).astype(bf16) * mask[...]


def cotangent_kernel(info, own, got_first, got_second, halo_own, halo_got, second, mask, lhs_ref, stack, second_rel):
    span, half = own.shape
    width = 2 * half
    block = half // 4
    stack_rows(info, own, got_first, got_second, halo_own, halo_got, stack, span, half, lhs_ref)
    for r in range(8):
        second_rel[:, r * block : (r + 1) * block] = second[:, lanes_at(info[ACTUAL + r], block)]
    low = adapter_scale * dot_nt(lhs_ref[:, :width], second_rel[...])
    lhs_ref[:, width:] = low.astype(bf16) * mask[...]


def mixer_parts(refs, cuts):
    if len(cuts) == 1:
        return [[refs[0].at[j] for j in range(3)]], [refs[1]], refs[2:]
    ins = [[refs[0].at[k, j] for j in range(3)] for k in range(2)]
    outs = [refs[1].at[k] for k in range(2)]
    early = pl.program_id(0) < 2
    for k in range(4):
        first, second = refs[2 + 2 * k], refs[3 + 2 * k]
        tiles = [jnp.where(early, first[j], second[j]) for j in range(4)]
        ins.append(tiles[:3])
        outs.append(tiles[3])
    return ins, outs, refs[10:]


def mixer_kernel(cuts, lhs, one, two, taps, in_expand, out_shrink, *refs):
    in_parts, out_parts, refs = mixer_parts(refs, cuts)
    b_ref, c_ref, v_ref, conv_ref, gated_ref, part_first, part_second, acc = refs
    width = cuts[-1][1]
    step = pl.program_id(0)

    def project(j):
        total = dot(lhs[:, width:], in_expand[j] * jnp.asarray(adapter_scale, bf16))
        for (low, top), part in zip(cuts, in_parts):
            total = total + dot(lhs[:, low:top], part[j][...])
        return total

    b, c, v = project(0), project(1), project(2)
    b_ref[...] = b
    c_ref[...] = c
    v_ref[...] = v
    mixed = (b * v).astype(bf16)
    w = taps[...].astype(f32)
    conv = w[0:1] * mixed.astype(f32) + w[1:2] * dot(one[...], mixed) + w[2:3] * dot(two[...], mixed)
    conv_ref[...] = conv
    gated = (c * conv).astype(bf16)
    gated_ref[...] = gated

    @pl.when(step == 0)
    def _():
        acc[...] = jnp.zeros_like(acc)

    for (low, top), part in zip(cuts, out_parts):
        acc[:, low:top] += dot(gated, part[...])
    acc[:, width:] += dot(gated, out_shrink[...])

    @pl.when(step == pl.num_programs(0) - 1)
    def _():
        cut = part_first.shape[0]
        part_first[...] = acc[:cut, :].astype(bf16)
        part_second[...] = acc[cut:, :].astype(bf16)


def blocks_across(ref, value, earlier=None, *at):
    for i in range(value.shape[1] // 128):
        block = value[:, i * 128 : (i + 1) * 128]
        block = block if earlier is None else block + earlier[(*at, i)]
        ref[(*at, i)] = block.astype(ref.dtype)


def blocks_down(ref, value, earlier=None, *at):
    for i in range(value.shape[0] // 128):
        block = value[i * 128 : (i + 1) * 128, :]
        block = block if earlier is None else block + earlier[(*at, i)]
        ref[(*at, i)] = block.astype(ref.dtype)


def middle_kernel(info, x, part_first, part_second, got_first, got_second, mask, gain, out_second, ffn_first,
                  hidden_ref, lhs, low_ref, both_ref, added, first_rel, second_rel, gain_rel):
    width = x.shape[1]
    block = width // 8
    rank = mask.shape[1]
    for r in range(8):
        at = lanes_at(info[ACTUAL + r], block)
        here = slice(r * block, (r + 1) * block)
        first_rel[here, :] = ffn_first[at, :]
        second_rel[:, here] = out_second[:, at]
        gain_rel[:, here] = gain[:, at]
    cut = part_first.shape[0]
    for own, got, base in ((part_first, got_first, 0), (part_second, got_second, cut)):
        both_ref[base : base + own.shape[0], :] = own[...].astype(f32) + got[...].astype(f32)
    low = both_ref[:, width:].astype(bf16) * mask[...]
    low_ref[...] = low
    added[...] = dot(low, second_rel[...])

    def visit(at):
        hidden = x[at, :].astype(f32) + (both_ref[at, :width] + adapter_scale * added[at, :])
        hidden_ref[at, :] = hidden
        scale = lax.rsqrt(jnp.mean(hidden * hidden, axis=-1, keepdims=True) + norm_eps)
        lhs[at, :width] = (hidden * scale * gain_rel[0:1, :]).astype(bf16)

    over_row_blocks(x.shape[0], 16, visit)
    low = dot(lhs[:, :width], first_rel[...]).astype(bf16)
    lhs[:, width : width + rank] = low[:, :rank] * mask[...]
    lhs[:, width + rank :] = low[:, rank:] * mask[...]


def feed_kernel(cuts, span, later, info, lhs, glhs, ffn_expand, down_shrink, *refs):
    earlier = refs[0] if later else None
    refs = refs[1:] if later else refs
    if len(cuts) == 1:
        gu_parts, down_parts, refs = [[refs[0].at[0], refs[0].at[1]]], [refs[1]], refs[2:]
        arrived = lambda: None
    else:
        gu_parts = [[refs[0].at[k, j] for j in range(2)] for k in range(2)]
        down_parts = [refs[1].at[k] for k in range(2)]
        count = len(FEED_CUTS)
        far, refs = refs[2 : 2 + 4 * count], refs[2 + 4 * count :]
        slots, sems, refs = refs[-2], refs[-1], refs[:-2]
        step, steps = pl.program_id(0), FEED_CUTS[-1][1]

        def fetch(tile):
            for i, (low, top) in enumerate(FEED_CUTS):

                @pl.when((tile >= low) & (tile < top))
                def _(i=i, low=low):
                    at = pl.ds(pl.multiple_of((tile - low) * TILE, TILE), TILE)
                    for k in range(4):
                        slot = lax.rem(tile, 2)
                        pltpu.make_async_copy(far[k * count + i].at[:, :, at], slots.at[slot, k], sems.at[slot, k]).start()

        @pl.when(step == 0)
        def _():
            fetch(step)

        @pl.when(step + 1 < steps)
        def _():
            fetch(step + 1)

        slot = lax.rem(step, 2)
        here = slots.at[slot]
        for k in range(4):
            gu_parts.append([here.at[k, 0], here.at[k, 1]])
            down_parts.append(here.at[k, 2])

        def arrived():
            for k in range(4):
                pltpu.make_async_copy(far[k * count].at[:, :, :TILE], slots.at[slot, k], sems.at[slot, k]).wait()
    f_ref, own_ref, send_ref, grads, acc_d, acc_f = refs
    width = cuts[-1][1]
    half = width // 2
    rank = down_shrink.shape[1]
    step = pl.program_id(0)

    @pl.when(step == 0)
    def _():
        acc_d[...] = jnp.zeros_like(acc_d)
        acc_f[...] = jnp.zeros_like(acc_f)

    arrived()
    lows = [lhs[:, width : width + rank], lhs[:, width + rank :]]
    half_scale = jnp.asarray(adapter_scale, bf16)

    def project(j):
        total = dot(lows[j], ffn_expand[j] * half_scale)
        for (low, top), w in zip(cuts, gu_parts):
            total = total + dot(lhs[:, low:top], w[j][...])
        return total

    gate, up = project(0), project(1)
    sig = jax.nn.sigmoid(gate)
    silu = gate * sig
    act = (silu * up).astype(bf16)
    g_low = glhs[:, width:]
    grad_act = dot_nt(g_low, down_shrink[...])
    for (low, top), w in zip(cuts, down_parts):
        grad_act = grad_act + dot_nt(glhs[:, low:top], w[...])
    gg = (grad_act * up * (sig * (1.0 + gate * (1.0 - sig)))).astype(bf16)
    gu = (grad_act * silu).astype(bf16)
    for (low, top), w in zip(cuts, down_parts):
        acc_d[:span, low:top] += dot(act[:span], w[...])
    acc_d[:span, width:] += dot(act[:span], down_shrink[...])
    for (low, top), w in zip(cuts, gu_parts):
        acc_f[:, low:top] += dot_nt(gg, w[0][...]) + dot_nt(gu, w[1][...])
    acc_f[:, width : width + rank] += dot_nt(gg, ffn_expand[0] * half_scale)
    acc_f[:, width + rank :] += dot_nt(gu, ffn_expand[1] * half_scale)
    blocks_down(grads, dot_tn(act[:span], g_low[:span]), earlier, 0)
    blocks_across(grads, adapter_scale * dot_tn(lows[0][:span], gg[:span]), earlier, 1)
    blocks_across(grads, adapter_scale * dot_tn(lows[1][:span], gu[:span]), earlier, 2)

    @pl.when(step == pl.num_programs(0) - 1)
    def _():
        f_ref[...] = acc_f[...].astype(bf16)
        place = info[3]
        own_ref[:, :half] = acc_d[:span, lanes_at(place, half)].astype(bf16)
        send_ref[:, :half] = acc_d[:span, lanes_at(1 - place, half)].astype(bf16)
        own_ref[:, half:] = acc_d[:span, width:].astype(bf16)
        send_ref[:, half:] = acc_d[:span, width:].astype(bf16)


def back_kernel(cuts, span, later, info, part, got, hidden, glhs, lhs_two, out_low, lhs_one, mask, gain, out_second, ffn_first,
                one, two, taps, in_expand, out_shrink, b_ref, c_ref, v_ref, conv_ref, gated_ref, *refs):
    in_parts, out_parts, refs = mixer_parts(refs, cuts)
    ffn_earlier, second_earlier, grads_earlier = refs[:3] if later else (None,) * 3
    refs = refs[3:] if later else refs
    (own_ref, send_ref, rank_ref, gh_ref, ffn_grad, second_grad, grads,
     acc, branch, first_rel, second_rel, gain_rel) = refs
    width = cuts[-1][1]
    half = width // 2
    block = width // 8
    rank = mask.shape[1]
    step = pl.program_id(0)
    place = info[3]

    @pl.when(step == 0)
    def _():
        for r in range(8):
            at = lanes_at(info[ACTUAL + r], block)
            here = slice(r * block, (r + 1) * block)
            first_rel[here, :] = ffn_first[at, :]
            second_rel[:, here] = out_second[:, at]
            gain_rel[:, here] = gain[:, at]
        low = (part[:, width:].astype(f32) + got[:, width:].astype(f32)).astype(bf16)
        low = jnp.concatenate([low[:, :rank] * mask[...], low[:, rank:] * mask[...]], axis=1)
        acc[:, :width] = dot_nt(low, first_rel[...])

        def visit(at):
            both = part[at, :width].astype(f32) + got[at, :width].astype(f32)
            h = hidden[at, :]
            scale = lax.rsqrt(jnp.mean(h * h, axis=-1, keepdims=True) + norm_eps)
            unit = h * scale
            grad_unit = (both + acc[at, :width]) * gain_rel[0:1, :]
            grad = glhs[at, :width].astype(f32) + scale * (
                grad_unit - unit * jnp.mean(grad_unit * unit, axis=-1, keepdims=True)
            )
            gh_ref[at, :] = grad
            branch[at, :width] = grad.astype(bf16)

        over_row_blocks(hidden.shape[0], 16, visit)
        b_low = adapter_scale * dot_nt(branch[:, :width], second_rel[...])
        branch[:, width:] = b_low.astype(bf16) * mask[...]
        for i in range(4):
            at = lanes_at(place * 4 + info[INNER + i], block)
            value = dot_tn(lhs_two[:span, at], low[:span])
            for k in range(2):
                blocks_down(ffn_grad, value[:, k * 128 : (k + 1) * 128], ffn_earlier, i, k)
            blocks_across(second_grad, adapter_scale * dot_tn(out_low[:span, :], branch[:span, at]), second_earlier, i)
        acc[...] = jnp.zeros_like(acc)

    total = dot_nt(branch[:, width:], out_shrink[...])
    for (low, top), w in zip(cuts, out_parts):
        total = total + dot_nt(branch[:, low:top], w[...])
    grad_c = total * conv_ref[...]
    conv = total * c_ref[...]
    w = taps[...].astype(f32)
    high = conv.astype(bf16)
    rest = (conv - high.astype(f32)).astype(bf16)
    mixed = (
        w[0:1] * conv
        + w[1:2] * (dot_tn(one[...], high) + dot_tn(one[...], rest))
        + w[2:3] * (dot_tn(two[...], high) + dot_tn(two[...], rest))
    )
    proj = [
        (mixed * v_ref[...]).astype(bf16)[:span],
        grad_c.astype(bf16)[:span],
        (mixed * b_ref[...]).astype(bf16)[:span],
    ]
    half_scale = jnp.asarray(adapter_scale, bf16)
    for (low, top), w in zip(cuts, in_parts):
        acc[:span, low:top] += dot_nt(proj[0], w[0][...]) + dot_nt(proj[1], w[1][...]) + dot_nt(proj[2], w[2][...])
    acc[:span, width:] += (
        dot_nt(proj[0], in_expand[0] * half_scale)
        + dot_nt(proj[1], in_expand[1] * half_scale)
        + dot_nt(proj[2], in_expand[2] * half_scale)
    )
    low_one = lhs_one[:span, width:]
    for j in range(3):
        blocks_across(grads, adapter_scale * dot_tn(low_one, proj[j]), grads_earlier, j)
    blocks_down(grads, dot_tn(gated_ref[:span, :], branch[:span, width:]), grads_earlier, 3)

    @pl.when(step == pl.num_programs(0) - 1)
    def _():
        own_ref[...] = acc[:span, lanes_at(place, half)].astype(bf16)
        send_ref[...] = acc[:span, lanes_at(1 - place, half)].astype(bf16)
        rank_ref[:, :rank] = acc[:span, width:].astype(bf16)

        def visit(at):
            sums = acc[at, :width].astype(bf16).astype(f32) * lhs_one[at, :width].astype(f32)
            stat = jnp.sum(sums, axis=-1, keepdims=True)
            high = stat.astype(bf16).astype(f32)
            middle = (stat - high).astype(bf16).astype(f32)
            rest = stat - high - middle
            lane = lax.broadcasted_iota(jnp.int32, (stat.shape[0], 128), 1)
            packed = jnp.where(lane == 0, high, jnp.where(lane == 1, middle, jnp.where(lane == 2, rest, 0.0)))
            rank_ref[at, rank:] = packed.astype(bf16)

        over_row_blocks(span, 16, visit)


def rank_rows(own, got, mask):
    rank = mask.shape[1]
    sums = own[...].astype(f32) + got[...].astype(f32)
    return sums[:, :rank].astype(bf16) * mask[...], sums[:, rank:]


def output_kernel(info, *refs):
    output_rows(info, *refs[:8], *refs[-2:])


def output_rows(info, own, got, rank_own, rank_got, hidden, mask, g, second, out_ref, grad_ref):
    low, _ = rank_rows(rank_own, rank_got, mask)
    down = own[...].astype(f32) + got[...].astype(f32)
    out_ref[...] = (hidden[...] + (down + adapter_scale * dot(low, second[...]))).astype(bf16)
    blocks_across(grad_ref, adapter_scale * dot_tn(low, g[...]))


def rank_kernel(info, own, got, mask, normed, grad_ref):
    low, _ = rank_rows(own, got, mask)
    blocks_down(grad_ref, dot_tn(normed[...], low))


def final_kernel(width, info, *refs):
    final_rows(width, info, *refs[:11], refs[-1])


def final_rows(width, info, own, got, rank_own, rank_got, gh, x, low, scale, mask, gain, first, grad_ref):
    n_low, stat = rank_rows(rank_own, rank_got, mask)
    stat = jnp.sum(stat, axis=-1, keepdims=True)
    stat = stat + jnp.sum(n_low.astype(f32) * low[...].astype(f32), axis=-1, keepdims=True)
    stat = stat / width
    scale_rows = scale[:, 0:1]
    unit = x[...].astype(f32) * scale_rows
    grad = own[...].astype(f32) + got[...].astype(f32) + dot_nt(n_low, first[...])
    grad_ref[...] = gh[...] + scale_rows * (grad * gain[0:1, :].astype(f32) - unit * stat)


def places(info, pieces):
    me, ctx = info[0], info[1]
    for place in range(4 * pieces):
        c, x, z = place // (2 * pieces), place // pieces % 2, place % pieces
        far_c, far_x = (me % 2) ^ c, (me // 2) ^ x
        yield place, 2 * far_c + far_x, lax.rem(ctx + pieces - z, pieces)


def unpack_feed_kernel(tiles, total, expand_ref, first_ref):
    for h in range(tiles):
        for k in range(2):
            column = h * 256 + k * 128
            for j in range(3):
                row = ((h * 3 + j) * 2 + k) * 128
                value = total[row : row + 128, :].astype(f32)
                if j:
                    expand_ref[j - 1, :, column : column + 128] = value
                else:
                    first_ref[column : column + 128, :] = value


def gather_feed_kernel(pieces, tiles, info, own, x, c, cx, expand_ref, first_ref, kept):
    n = own.shape[1]
    for place, which, distance in places(info, pieces):
        for k, part in enumerate((own, x, c, cx)):

            @pl.when(which == k)
            def _(part=part, place=place, distance=distance):
                kept[place * n : (place + 1) * n, :] = part[distance]

    unpack_feed_kernel(tiles, kept, expand_ref, first_ref)


def gather_rows_kernel(pieces, info, own, x, c, cx, out):
    for place, which, distance in places(info, pieces):
        for k, part in enumerate((own, x, c, cx)):

            @pl.when(which == k)
            def _(part=part, place=place, distance=distance):
                out[place] = part[distance]


def unpack_early_kernel(pieces, info, own, x, c, cx, ffn_ref, second_ref, expand_ref, out_ref, kept):
    gather_rows_kernel(pieces, info, own, x, c, cx, kept)
    tens = info[2]
    for place in range(4 * pieces):
        i, k, part = place // 4, place // 2 % 2, place % 2
        for t in range(2):
            base = pl.multiple_of(jnp.where(tens == t, 0, 192), 64)
            ffn_ref[t * 1024 + i * 256 + part * 128 : t * 1024 + i * 256 + part * 128 + 128, k * 128 : (k + 1) * 128] = (
                kept[place, pl.ds(base, 128), :].astype(f32)
            )
            column = t * 1024 + i * 256 + k * 128
            second_ref[part * 64 : part * 64 + 64, column : column + 128] = kept[
                place, pl.ds(pl.multiple_of(base + 128, 64), 64), :
            ].astype(f32)
        h, j = place // 4, place % 4
        for k in range(2):
            value = kept[place, 384 + k * 128 : 512 + k * 128, :].astype(f32)
            column = h * 256 + k * 128
            if j < 3:
                expand_ref[j, :, column : column + 128] = value
            else:
                out_ref[column : column + 128, :] = value


def unpack_late_kernel(pieces, info, own, x, c, cx, first_ref, second_ref, kept):
    gather_rows_kernel(pieces, info, own, x, c, cx, kept)
    tens = info[2]
    for place in range(4 * pieces):
        for t in range(2):
            base = pl.multiple_of(jnp.where(tens == t, 0, 128), 128)
            row = t * 1024 + place * 64
            first_ref[row : row + 64, :] = kept[place, pl.ds(base, 64), :].astype(f32)
            row, column = place % 2 * 64, t * 1024 + place // 2 * 128
            second_ref[row : row + 64, column : column + 128] = kept[
                place, pl.ds(pl.multiple_of(base + 64, 64), 64), :
            ].astype(f32)


def after(array, *gates):
    return lax.optimization_barrier((array,) + gates)[0] if gates else array


def swap_tensor(array):
    return lax.ppermute(array, "tensor", [(0, 1), (1, 0)])


def body(
    block_input,
    cotangent,
    deal_order,
    seq_lengths,
    seq_adapter,
    mixer_gain,
    ffn_gain,
    conv_taps,
    in_weight,
    out_weight,
    gateup_weight,
    down_weight,
    input_adapter_shrink,
    in_expand,
    out_shrink,
    output_adapter_expand,
    ffn_shrink,
    ffn_expand,
    down_shrink,
    down_adapter_expand,
):
    tok_count, half = block_input.shape
    width = 2 * half
    rank = input_adapter_shrink.shape[1]
    hidden_units = gateup_weight.shape[2]
    groups = lax.axis_size("dp")
    pieces = lax.axis_size("ctx")
    sub = tok_count // groups
    group_tokens = pieces * tok_count
    seqs = seq_lengths.shape[0]
    nb = groups // CHUNKS
    span = nb * sub
    halo = -(-4 * nb // 16) * 16
    rows = span + halo
    special = groups == 4 and pieces % 2 == 0
    me = lax.axis_index("dp")
    ctx = lax.axis_index("ctx")
    tens = lax.axis_index("tensor")
    if special:
        xb, cb, zb = me // 2, me % 2, ctx % 2
    else:
        xb = cb = zb = jnp.int32(0)
    flip = xb ^ tens

    actual, in_stack, inner = [], [], []
    for rx in (0, 1):
        for rc in (0, 1):
            for rh in (0, 1):
                low = (rc ^ (cb & rx)) * 2 + (rh ^ (zb & rx))
                actual.append((rx ^ xb) * 4 + low)
                in_stack.append((rx ^ flip) * 4 + low)
    for bc in (0, 1):
        for bh in (0, 1):
            inner.append((bc ^ (cb & flip)) * 2 + (bh ^ (zb & flip)))
    info = jnp.stack([me, ctx, tens, flip, *actual, *in_stack, *inner]).astype(jnp.int32)

    core_route = [(0, 1), (1, 0), (2, 3), (3, 2)]
    x_route = [(0, 2), (2, 0), (1, 3), (3, 1)]
    z_route = [(i, i ^ 1) for i in range(pieces)]
    gates = []

    def wait(*values):
        gates[:] = values

    def begin(axis, route, array):
        return lax.ppermute(after(array, *gates), axis, route)

    def core(array):
        return begin("dp", core_route, array)

    def over_x(array):
        return begin("dp", x_route, array)

    def over_z(array):
        return begin("ctx", z_route, array)

    def over_y(array):
        return begin("tensor", [(0, 1), (1, 0)], array)

    def tiles_beside(array):
        tiles = array.reshape(-1, TILE, array.shape[1])
        return jnp.concatenate([tiles[i] for i in range(tiles.shape[0])], axis=1)

    def mixer_piece(k):
        at = slice(k * half // 2, (k + 1) * half // 2)
        return jnp.concatenate([mine(in_weight[:, :, at], 1), tiles_beside(mine(out_weight[at], 1))[None]], axis=0)

    def feed_piece(k):
        low, top = FEED_CUTS[k]
        at = slice(low * TILE, top * TILE)
        return jnp.concatenate([mine(gateup_weight[:, :, at], 1), tiles_beside(mine(down_weight[at], 1))[None]], axis=0)

    def chip_pair(array):
        return lax.all_gather(after(array, *gates), "dp", axis_index_groups=[[0, 1], [2, 3]])

    def mine(shard, axis):
        n = shard.shape[axis] // 2
        return lax.dynamic_slice_in_dim(shard, zb * n, n, axis)

    numbers = jnp.concatenate([deal_order[0], seq_lengths, seq_adapter])
    digits = jnp.concatenate([numbers // 64, numbers % 64]).astype(bf16)
    x_blocks = block_input.reshape(groups, sub, half)
    g_blocks = cotangent.reshape(groups, sub, half)
    digit_rows = jnp.zeros((groups, 2, half), bf16).at[0, 0, : digits.shape[0]].set(digits)
    edges = jnp.concatenate([x_blocks[:, :2], g_blocks[:, :2], x_blocks[:, sub - 2 :], digit_rows], axis=1)

    if special:
        in_own = chip_pair(in_weight)
        mixer_x, mixer_z, mixer_xc, mixer_zc = ([None] * 2 for _ in range(4))
        feed_x, feed_z, feed_xc, feed_zc = ([None] * len(FEED_CUTS) for _ in range(4))
        mixer_packed = [mixer_piece(k) for k in range(2)]
        feed_packed = [feed_piece(k) for k in range(len(FEED_CUTS))]
    x_got = [over_y(block_input[:span]), None]
    if special:
        mixer_x[0] = over_x(mixer_packed[0])
    all_edges = lax.all_gather(edges, "dp", axis=0, tiled=False)
    digits = all_edges[:, 0, 6, : 2 * numbers.shape[0]].astype(jnp.int32)
    table = digits[:, : numbers.shape[0]] * 64 + digits[:, numbers.shape[0] :]
    dims = (groups, seqs, sub, nb, rows, tok_count, group_tokens)
    per_chunk = lambda c, *_: (c, 0, 0)
    mask, one, two = call(
        functools.partial(tables_kernel, dims), (CHUNKS,), (table, info), [],
        [
            ((CHUNKS, rows, rank), bf16, (None, rows, rank), per_chunk),
            ((CHUNKS, rows, rows), bf16, (None, rows, rows), per_chunk),
            ((CHUNKS, rows, rows), bf16, (None, rows, rows), per_chunk),
        ],
    )
    first_heads, last_tails, next_near, prev_near = call(
        functools.partial(edges_kernel, groups), (1,), (table, info), [(all_edges, None, None)],
        [
            ((groups, 4, half), bf16, None, None),
            ((groups, 2, half), bf16, None, None),
            ((groups, 4, half), bf16, None, None),
            ((groups, 2, half), bf16, None, None),
        ],
    )
    stage = [all_edges, x_got[0]] + ([mixer_x[0], in_own, mixer_packed[1], feed_packed[0]] if special else [])
    wait(*stage)
    from_next = begin("ctx", [(i + 1, i) for i in range(pieces - 1)], first_heads)
    from_prev = begin("ctx", [(i, i + 1) for i in range(pieces - 1)], last_tails)
    x_got[1] = over_y(block_input[span:])
    stage = [from_next, from_prev, x_got[1]]
    if special:
        mixer_x[1], mixer_z[0] = over_x(mixer_packed[1]), over_z(mixer_x[0])
        out_own = chip_pair(out_weight)
        stage += [mixer_x[1], mixer_z[0], out_own]
    deal_all = table[:, :groups]
    at_end = (deal_all[:, groups - 1] == me)[:, None, None]
    at_start = (deal_all[:, 0] == me)[:, None, None]
    next_rows = jnp.where(at_end, from_next, next_near)
    prev_rows = jnp.where(at_start, from_prev, prev_near)
    halo_x = jnp.concatenate([prev_rows, next_rows[:, :2]], axis=1)
    halo_g = jnp.concatenate([jnp.zeros_like(prev_rows), next_rows[:, 2:]], axis=1)
    halo_own = jnp.stack([halo_x, halo_g]).reshape(2, CHUNKS, 4 * nb, half)
    halo_own = jnp.pad(halo_own, ((0, 0), (0, 0), (0, halo - 4 * nb), (0, 0)))
    wait(*stage)
    halo_got = over_y(halo_own)
    g_got = [over_y(after(cotangent[:span], halo_got)), None]
    stage = [g_got[0]]
    if special:
        feed_x[0], mixer_z[1] = over_x(feed_packed[0]), over_z(mixer_x[1])
        mixer_xc[0] = core(mixer_x[0])
        mixer_xc[1] = core(after(mixer_x[1], mixer_xc[0]))
        mixer_zc[0] = core(after(mixer_z[0], mixer_xc[1]))
        gu_own = chip_pair(gateup_weight)
        stage += [feed_x[0], mixer_z[1], mixer_xc[0], mixer_xc[1], mixer_zc[0], feed_packed[1]]

    gain_one, gain_two = mixer_gain[None, :].astype(f32), ffn_gain[None, :].astype(f32)
    ext_one, ext_two = width + rank, width + 2 * rank

    def stacked(array, last):
        return (array, (None,) + array.shape[1:], lambda c, *_: (c, 0, 0))

    def joined_inputs(own, got, which):
        def halo_of(array):
            return (array, (None, None, halo, half), lambda c, *_: (which, c, 0, 0))

        return [
            (own, (span, half), lambda c, *_: (c, 0)),
            (got[0], None, None),
            (got[1], None, None),
            halo_of(halo_own),
            halo_of(halo_got),
        ]

    x_full, lhs_one, scale = call(
        input_kernel, (CHUNKS,), (info,),
        joined_inputs(block_input, x_got, 0)
        + [(gain_one, None, None), (input_adapter_shrink, None, None), stacked(mask, rank)],
        [
            ((CHUNKS, rows, width), bf16, (None, rows, width), per_chunk),
            ((CHUNKS, rows, ext_one), bf16, (None, rows, ext_one), per_chunk),
            ((CHUNKS, rows, 128), f32, (None, rows, 128), per_chunk),
        ],
        [
            pltpu.VMEM((rows, width), bf16),
            pltpu.VMEM((width, rank), bf16),
            pltpu.VMEM((1, width), f32),
        ],
    )
    wait(*stage, lhs_one)
    g_got[1] = over_y(cotangent[span:])
    stage = [g_got[1]]
    if special:
        n = width // 8
        cuts = ((0, 2 * n), (2 * n, 4 * n), (4 * n, 5 * n), (5 * n, 6 * n), (6 * n, 7 * n), (7 * n, 8 * n))
        mixer_zc[1] = core(mixer_z[1])
        feed_x[1], feed_z[0], feed_xc[0] = over_x(feed_packed[1]), over_z(feed_x[0]), core(feed_x[0])
        stage += [feed_x[1], feed_z[0], feed_xc[0], feed_packed[2]]
        mixer_inputs = lambda: (
            [(in_own, (2, 3, in_own.shape[2], TILE), lambda h, *_: (0, 0, 0, h)),
             (out_own, (2, TILE, out_own.shape[2]), lambda h, *_: (0, h, 0))]
            + [(w, (4, TILE, TILE), (lambda h, *_: (0, 0, jnp.minimum(h, 1))) if i == 0 else (lambda h, *_: (0, 0, jnp.maximum(h - 2, 0))))
               for part in (mixer_x, mixer_z, mixer_xc, mixer_zc) for i, w in enumerate(part)]
        )
    else:
        cuts = ((0, width),)
        in_parts = [lax.all_gather(in_weight, "dp", axis=1, tiled=True)]
        out_parts = [lax.all_gather(out_weight, "dp", axis=1, tiled=True)]
        gu_parts = [lax.all_gather(gateup_weight, "dp", axis=1, tiled=True)]
        down_parts = [lax.all_gather(down_weight, "dp", axis=1, tiled=True)]
        mixer_inputs = lambda: [columns(in_parts[0]), row_tiles(out_parts[0])]

    def picked(array, c):
        return (array, (None,) + array.shape[1:], lambda *_: (c, 0, 0))

    def columns(array):
        return (array, array.shape[:-1] + (TILE,), lambda h, *_: (0,) * (array.ndim - 1) + (h,))

    def row_tiles(array):
        lead = array.ndim - 2
        return (array, array.shape[:lead] + (TILE, array.shape[-1]), lambda h, *_: (0,) * lead + (h, 0))

    def feed_step(k):
        count = len(FEED_CUTS)
        if k < count:
            feed_x[k] = over_x(feed_packed[k])
            stage.extend([feed_x[k]] + feed_packed[k + 1 : k + 2])
        if 0 <= k - 1 < count:
            feed_z[k - 1], feed_xc[k - 1] = over_z(feed_x[k - 1]), core(feed_x[k - 1])
            stage.extend([feed_z[k - 1], feed_xc[k - 1]])
        if 0 <= k - 2 < count:
            feed_zc[k - 2] = core(feed_z[k - 2])
            stage.append(feed_zc[k - 2])

    mixer_steps = half // TILE
    feed_steps = hidden_units // TILE
    column_out = lambda h, *_: (0, h)
    row_halves = (rows // 32 * 16, rows - rows // 32 * 16)
    chunks = []
    for c in range(CHUNKS):
        gate_b, gate_c, values, conv, gated, *part = call(
            functools.partial(mixer_kernel, cuts), (mixer_steps,), (),
            [picked(lhs_one, c), picked(one, c), picked(two, c), columns(conv_taps), columns(in_expand), row_tiles(out_shrink)]
            + mixer_inputs(),
            [((rows, half), f32, (rows, TILE), column_out)] * 4
            + [((rows, half), bf16, (rows, TILE), column_out)]
            + [((n, ext_one), bf16, None, None) for n in row_halves],
            [pltpu.VMEM((rows, ext_one), f32)],
            flops=2 * rows * half * ext_one * 4,
        )
        chunks.append(dict(b=gate_b, c=gate_c, v=values, conv=conv, gated=gated, part=part))
        if c == 0:
            wait(*stage, *part)
            chunks[0]["got"] = [over_y(part[0]), None]
            stage = [chunks[0]["got"][0]]
            if special:
                feed_step(2)
                down_own = chip_pair(down_weight)
    def middle(i):
        c = chunks[i]
        c["hidden"], c["lhs"], c["low"] = call(
            middle_kernel, (1,), (info,),
            [picked(x_full, i)] + [(w, None, None) for w in (*c["part"], *c["got"])]
            + [picked(mask, i), (gain_two, None, None), (output_adapter_expand, None, None), (ffn_shrink, None, None)],
            [((rows, width), f32, None, None), ((rows, ext_two), bf16, None, None), ((rows, rank), bf16, None, None)],
            [
                pltpu.VMEM((rows, ext_one), f32),
                pltpu.VMEM((rows, width), f32),
                pltpu.VMEM((width, 2 * rank), bf16),
                pltpu.VMEM((rank, width), bf16),
                pltpu.VMEM((1, width), f32),
            ],
        )

    wait(*stage, *chunks[1]["part"])
    chunks[0]["got"][1] = over_y(chunks[0]["part"][1])
    stage = [chunks[0]["got"][1]]
    if special:
        feed_step(3)
    wait(*stage)
    chunks[1]["got"] = [over_y(chunks[1]["part"][0]), None]
    stage = [chunks[1]["got"][0]]
    if special:
        feed_step(4)
    (glhs,) = call(
        cotangent_kernel, (CHUNKS,), (info,),
        joined_inputs(cotangent, g_got, 1) + [(down_adapter_expand, None, None), stacked(mask, rank)],
        [((CHUNKS, rows, ext_one), bf16, (None, rows, ext_one), per_chunk)],
        [pltpu.VMEM((rows, width), bf16), pltpu.VMEM((rank, width), bf16)],
    )

    wait(*stage, glhs)
    chunks[1]["got"][1] = over_y(chunks[1]["part"][1])
    stage = [chunks[1]["got"][1]]
    middle(0)
    middle(1)
    if special:
        feed_step(5)
        wait(*stage, chunks[0]["lhs"])
        stage = [chunks[1]["lhs"]]
        feed_step(6)
        wait(*stage)
        feed_step(7)
        whole = [(gu_own, (2, 2, gu_own.shape[2], TILE), lambda h, *_: (0, 0, 0, h)),
                 (down_own, (2, TILE, down_own.shape[2]), lambda h, *_: (0, h, 0))]
        feed_inputs = whole + [(w, "any", None) for part in (feed_x, feed_z, feed_xc, feed_zc) for w in part]
    else:
        feed_inputs = [columns(gu_parts[0]), row_tiles(down_parts[0])]

    for i, c in enumerate(chunks):
        f_part, d_own, d_send, grads = call(
            functools.partial(feed_kernel, cuts, span, i > 0), (feed_steps,), (info,),
            [(c["lhs"], None, None), picked(glhs, i), columns(ffn_expand), row_tiles(down_shrink)]
            + ([(chunks[0]["feed_grads"], (None, 3, 2, 128, 128), lambda h, *_: (h, 0, 0, 0, 0))] if i else [])
            + feed_inputs,
            [
                ((rows, ext_two), bf16, None, None),
                ((span, half + rank), bf16, None, None),
                ((span, half + rank), bf16, None, None),
                ((feed_steps, 3, 2, 128, 128), bf16 if i else f32, (None, 3, 2, 128, 128), lambda h, *_: (h, 0, 0, 0, 0)),
            ],
            [
                pltpu.VMEM((rows, ext_one), f32),
                pltpu.VMEM((rows, ext_two), f32),
            ]
            + ([pltpu.VMEM((2, 4, 3, TILE, TILE), bf16), pltpu.SemaphoreType.DMA((2, 4))] if special else []),
            flops=2 * rows * hidden_units * ext_two * 6,
        )
        c.update(f_own=f_part, d_own=d_own, d_send=d_send, feed_grads=grads)
    def summed(name):
        return sum(c[name] for c in chunks).astype(bf16)

    def take(array, i):
        return lax.dynamic_index_in_dim(array, i, 0, keepdims=False)

    def add(*terms):
        return sum(t.astype(f32) for t in terms).astype(bf16)

    core_bit, x_bit = me % 2, me // 2
    shifts = [[(i, (i + k) % pieces) for i in range(pieces)] for k in range(1, pieces)]

    def cut(*arrays):
        return jnp.concatenate([a.reshape(2, 2, pieces, -1, 128) for a in arrays], axis=3)

    def scatter_core(total):
        return add(take(total, core_bit), lax.ppermute(take(total, 1 - core_bit), "dp", core_route))

    def scatter_x(total):
        return add(take(total, x_bit), lax.ppermute(take(total, 1 - x_bit), "dp", x_route))

    def scatter_z(total):
        sent = [lax.ppermute(take(total, (ctx + k) % pieces), "ctx", route) for k, route in enumerate(shifts, 1)]
        return add(take(total, ctx), *sent)

    def gather_z(total):
        return jnp.stack([total] + [lax.ppermute(total, "ctx", route) for route in shifts])

    def gather_chip(total):
        over_x = lax.ppermute(total, "dp", x_route)
        return [total, over_x] + [lax.ppermute(v, "dp", core_route) for v in (total, over_x)]

    for c in chunks:
        c["f_got"] = swap_tensor(c["f_own"])
    feed = chunks[-1]["feed_grads"]
    if special:
        feed_sum = scatter_core(cut(after(feed, chunks[0]["f_got"])))
    for i, c in enumerate(chunks):
        f_got = after(c["f_got"], *([feed_sum] if special else []), *([chunks[0]["n_rank"]] if i else []))
        n_own, n_send, n_rank, grad_hidden, ffn_grad, second_grad, grads = call(
            functools.partial(back_kernel, cuts, span, i > 0), (mixer_steps,), (info,),
            [(c["f_own"], None, None), (f_got, None, None), (c["hidden"], None, None), picked(glhs, i),
             (c["lhs"], None, None), (c["low"], None, None), picked(lhs_one, i), picked(mask, i),
             (gain_two, None, None), (output_adapter_expand, None, None), (ffn_shrink, None, None),
             picked(one, i), picked(two, i), columns(conv_taps), columns(in_expand), row_tiles(out_shrink),
             columns(c["b"]), columns(c["c"]), columns(c["v"]), columns(c["conv"]), columns(c["gated"])]
            + mixer_inputs()
            + ([(chunks[0]["ffn_grad"], None, None), (chunks[0]["second_grad"], None, None),
                (chunks[0]["mixer_grads"], (None, 4, 2, 128, 128), lambda h, *_: (h, 0, 0, 0, 0))] if i else []),
            [
                ((span, half), bf16, None, None),
                ((span, half), bf16, None, None),
                ((span, 2 * rank), bf16, None, None),
                ((rows, width), f32, None, None),
                ((4, 2, 2, 128, 128), bf16 if i else f32, None, None),
                ((4, 2, 128, 128), bf16 if i else f32, None, None),
                ((mixer_steps, 4, 2, 128, 128), bf16 if i else f32, (None, 4, 2, 128, 128), lambda h, *_: (h, 0, 0, 0, 0)),
            ],
            [
                pltpu.VMEM((rows, ext_one), f32),
                pltpu.VMEM((rows, ext_one), bf16),
                pltpu.VMEM((width, 2 * rank), bf16),
                pltpu.VMEM((rank, width), bf16),
                pltpu.VMEM((1, width), f32),
            ],
            flops=2 * rows * half * ext_one * 4,
        )
        c.update(n_own=n_own, n_send=n_send, n_rank=n_rank, gh=grad_hidden, ffn_grad=ffn_grad, second_grad=second_grad, mixer_grads=grads)
        if special:
            feed_sum = scatter_x(feed_sum) if i == 0 else feed_sum
    for c in chunks:
        c["d_got"] = swap_tensor(after(c["d_send"], chunks[0]["f_got"]))
    chunks[0]["n_got"] = swap_tensor(chunks[0]["n_send"])
    if special:
        feed_sum = scatter_z(feed_sum)
        last = chunks[-1]
        early = cut(after(last["ffn_grad"], feed_sum, *(c["d_got"] for c in chunks)), last["second_grad"], last["mixer_grads"])
        early = scatter_core(early)
        first_step = (early,)
    else:
        first_step = ()

    block = half // 4
    in_half = lambda i, info: (0, info[INNER + i])
    in_full = lambda i, info: (0, info[3] * 4 + info[INNER + i])
    whole_block = lambda i, info: (0, 0)
    grad_out = ((4, 2, 128, 128), f32, (None, 2, 128, 128), lambda i, info: (i, 0, 0, 0))
    for k, c in enumerate(chunks):
        in_stack_full = lambda i, info, k=k: (k, 0, info[3] * 4 + info[INNER + i])
        masks = (mask, (None, span, rank), lambda i, info, k=k: (k, 0, 0))
        d_got = after(c["d_got"], *first_step)
        c["out"], c["down_grad"] = call(
            output_kernel, (4,), (info,),
            [
                (c["d_own"], (span, block), in_half),
                (d_got, (span, block), in_half),
                (c["d_own"], (span, rank), lambda i, info: (0, half // rank)),
                (d_got, (span, rank), lambda i, info: (0, half // rank)),
                (c["hidden"], (span, block), in_full),
                masks,
                (glhs, (None, span, block), in_stack_full),
                (down_adapter_expand, (rank, block), lambda i, info: (0, info[2] * 4 + i)),
            ]
            + ([(chunks[0]["out"], "any", None)] if k else []),
            [((tok_count, half), bf16, (span, block), lambda i, info, k=k: (k, i)), grad_out],
            flops=5 * 10**9,
            aliases={9: 0} if k else None,
        )
    wait()
    if special:
        feed_sum = gather_z(after(feed_sum, early))
        early = after(scatter_x(early), feed_sum, chunks[-1]["out"], chunks[0]["n_got"])
        second_step = (early,)
    else:
        second_step = ()
    for c in chunks[::-1]:
        c["rank_got"] = swap_tensor(after(c["n_rank"], *second_step))
    for k, c in enumerate(chunks):
        in_stack_full = lambda i, info, k=k: (k, 0, info[3] * 4 + info[INNER + i])
        masks = (mask, (None, span, rank), lambda i, info, k=k: (k, 0, 0))
        ranks = [(w, (span, 2 * rank), whole_block) for w in (c["n_rank"], c["rank_got"])]
        (c["in_grad"],) = call(
            rank_kernel, (4,), (info,), ranks + [masks, (lhs_one, (None, span, block), in_stack_full)], [grad_out],
            flops=5 * 10**9,
        )
    if special:
        feed_parts = [feed_sum, begin("dp", x_route, after(feed_sum, early))]
        early = after(scatter_z(early), feed_parts[1], *(c["in_grad"] for c in chunks))
        late = scatter_core(cut(summed("in_grad"), summed("down_grad")))
        h = 3 * 1024 // (4 * pieces)
        early = jnp.concatenate([early[:h], swap_tensor(early[:h]), early[h:]], axis=0)
        third_step = (early,)
    else:
        third_step = ()
    chunks[1]["n_got"] = swap_tensor(after(chunks[1]["n_send"], *third_step))
    for k, c in enumerate(chunks):
        in_stack_full = lambda i, info, k=k: (k, 0, info[3] * 4 + info[INNER + i])
        masks = (mask, (None, span, rank), lambda i, info, k=k: (k, 0, 0))
        ranks = [(w, (span, 2 * rank), whole_block) for w in (c["n_rank"], c["rank_got"])]
        n_got = after(c["n_got"], *third_step)
        (c["grad"],) = call(
            functools.partial(final_kernel, width), (4,), (info,),
            [(c["n_own"], (span, block), in_half), (n_got, (span, block), in_half)]
            + ranks
            + [
                (c["gh"], (span, block), in_full),
                (x_full, (None, span, block), in_stack_full),
                (lhs_one, (None, span, rank), lambda i, info, k=k: (k, 0, width // rank)),
                (scale, (None, span, 128), lambda i, info, k=k: (k, 0, 0)),
                masks,
                (gain_one, (1, block), lambda i, info: (0, info[2] * 4 + i)),
                (input_adapter_shrink, (block, rank), lambda i, info: (info[2] * 4 + i, 0)),
            ]
            + ([(chunks[0]["grad"], "any", None)] if k else []),
            [((tok_count, half), f32, (span, block), lambda i, info, k=k: (k, i))],
            flops=6 * 10**9,
            aliases={12: 0} if k else None,
        )
    block_output, input_grad = chunks[-1]["out"], chunks[-1]["grad"]

    if special:
        late = scatter_x(after(late, early))
        gathered = after(gather_z(early), chunks[0]["grad"], chunks[1]["n_got"])
        late = scatter_z(after(late, gathered))
        n = 4 * pieces
        feed_parts = [after(v, gathered) for v in feed_parts]
        feed_parts += [lax.ppermute(v, "dp", core_route) for v in feed_parts]
        expand_grad, first_grad = call(
            functools.partial(gather_feed_kernel, pieces, feed_steps), (1,), (info,),
            [(v, None, None) for v in feed_parts],
            [((2, rank, hidden_units), f32, None, None), ((hidden_units, rank), f32, None, None)],
            [pltpu.VMEM((feed.size // 128, 128), bf16)],
            flops=5 * 10**9,
        )
        late = jnp.concatenate([late, swap_tensor(late)], axis=0)
        over = after(lax.ppermute(gathered, "dp", x_route), expand_grad, chunks[1]["grad"])
        parts = [gathered, over] + [lax.ppermute(v, "dp", core_route) for v in (gathered, over)]
        ffn_grad, second_grad, mixer_grad, out_grad = call(
            functools.partial(unpack_early_kernel, pieces), (1,), (info,), [(v, None, None) for v in parts],
            [((width, 2 * rank), f32, None, None), ((rank, width), f32, None, None), ((3, rank, half), f32, None, None),
             ((half, rank), f32, None, None)],
            [pltpu.VMEM((n,) + early.shape, bf16)],
        )
        late = gather_z(late)
        over = after(lax.ppermute(late, "dp", x_route), ffn_grad)
        parts = [late, over] + [lax.ppermute(v, "dp", core_route) for v in (late, over)]
        in_grad, down_grad = call(
            functools.partial(unpack_late_kernel, pieces), (1,), (info,), [(v, None, None) for v in parts],
            [((width, rank), f32, None, None), ((rank, width), f32, None, None)],
            [pltpu.VMEM((n,) + late.shape[1:], bf16)],
        )
    else:
        last = chunks[-1]
        feed, mixer, ffn_grad, second_grad, in_grad, down_grad = lax.psum(
            (feed, last["mixer_grads"], last["ffn_grad"], last["second_grad"], summed("in_grad"), summed("down_grad")),
            ("dp", "ctx"),
        )

        def whole(part, axis):
            got = swap_tensor(part)
            pair = [jnp.where(tens == 0, part, got), jnp.where(tens == 0, got, part)]
            return jnp.concatenate(pair, axis=axis).astype(f32)

        def across(blocks):
            return blocks.reshape(-1, 128, 128).transpose(1, 0, 2).reshape(128, -1)

        ffn_grad = whole(ffn_grad.transpose(0, 2, 3, 1, 4).reshape(half, 2 * rank), 0)
        second_grad, down_grad = whole(across(second_grad), 1), whole(across(down_grad), 1)
        in_grad = whole(in_grad.reshape(half, rank), 0)
        mixer_grad = jnp.stack([across(mixer[:, j]) for j in range(3)]).astype(f32)
        out_grad = mixer[:, 3].reshape(half, rank).astype(f32)
        expand_grad = jnp.stack([across(feed[:, j]) for j in (1, 2)]).astype(f32)
        first_grad = feed[:, 0].reshape(hidden_units, rank).astype(f32)
    return (
        block_output,
        input_grad,
        in_grad,
        mixer_grad,
        out_grad,
        second_grad,
        ffn_grad,
        expand_grad,
        first_grad,
        down_grad,
    )


def solution(mesh):
    placed = (
        P(("dp", "ctx"), "tensor"),
        P(("dp", "ctx"), "tensor"),
        P("dp", None),
        P("dp"),
        P("dp"),
        P(),
        P(),
        P(None, "tensor"),
        P(None, "dp", "tensor"),
        P("tensor", "dp"),
        P(None, "dp", "tensor"),
        P("tensor", "dp"),
        P(),
        P(None, None, "tensor"),
        P("tensor", None),
        P(),
        P(),
        P(None, None, "tensor"),
        P("tensor", None),
        P(),
    )
    return jax.shard_map(
        body,
        mesh=mesh,
        in_specs=placed,
        out_specs=(
            P(("dp", "ctx"), "tensor"),
            P(("dp", "ctx"), "tensor"),
            P(),
            P(None, None, "tensor"),
            P("tensor", None),
            P(),
            P(),
            P(None, None, "tensor"),
            P("tensor", None),
            P(),
        ),
        check_vma=False,
    )
```

```python
import functools

import jax
import jax.numpy as jnp
from jax import lax
from jax.experimental import pallas as pl
from jax.experimental.pallas import tpu as pltpu
from jax.sharding import PartitionSpec as P

RANK = 16
CHUNKS = 2
TILE = 256
FEED_CUTS = ((0, 2), (2, 4), (4, 6), (6, 8), (8, 10), (10, 11))
VMEM_BYTES = 56 * 1024 * 1024

norm_eps = 1e-05
adapter_scale = 0.5

f32 = jnp.float32
bf16 = jnp.bfloat16


def dot(left, right):
    return jnp.dot(left, right, preferred_element_type=f32)


def dot_nt(left, right):
    return lax.dot_general(left, right, (((1,), (1,)), ((), ())), preferred_element_type=f32)


def dot_tn(left, right):
    return lax.dot_general(left, right, (((0,), (0,)), ((), ())), preferred_element_type=f32)


def over_row_blocks(rows, step, visit):
    def one(i, carry):
        visit(pl.ds(pl.multiple_of(i * step, step), step))
        return carry

    lax.fori_loop(0, rows // step, one, 0, unroll=5 if rows % (5 * step) == 0 else 2)


def lanes_at(index, width):
    return pl.ds(pl.multiple_of(index * width, width), width)


def call(kernel, grid, scalars, ins, outs, scratch=(), flops=0, aliases=None):
    in_specs = []
    for array, block, index in ins:
        if block == "any":
            in_specs.append(pl.BlockSpec(memory_space=pl.ANY))
        elif block is None:
            zeros = (0,) * array.ndim
            in_specs.append(
                pl.BlockSpec(array.shape, lambda *_, z=zeros: z, pipeline_mode=pl.Buffered(1))
            )
        else:
            in_specs.append(pl.BlockSpec(block, index))
    out_specs, out_shape = [], []
    for shape, dtype, block, index in outs:
        zeros = (0,) * len(shape)
        out_specs.append(
            pl.BlockSpec(shape, lambda *_, z=zeros: z) if block is None else pl.BlockSpec(block, index)
        )
        out_shape.append(jax.ShapeDtypeStruct(shape, dtype))
    moved = sum(a.size * a.dtype.itemsize for a, _, _ in ins)
    return pl.pallas_call(
        kernel,
        grid_spec=pltpu.PrefetchScalarGridSpec(
            num_scalar_prefetch=len(scalars),
            grid=grid,
            in_specs=in_specs,
            out_specs=out_specs,
            scratch_shapes=list(scratch),
        ),
        out_shape=out_shape,
        input_output_aliases=aliases or {},
        compiler_params=pltpu.CompilerParams(
            dimension_semantics=("arbitrary",) * len(grid), vmem_limit_bytes=VMEM_BYTES
        ),
        cost_estimate=pl.CostEstimate(flops=max(flops, 1), transcendentals=0, bytes_accessed=1),
    )(*scalars, *[a for a, _, _ in ins])


def tables_kernel(dims, table, info, mask_ref, one_ref, two_ref):
    groups, seqs, sub, nb, rows, tok_count, group_tokens = dims
    chunk = pl.program_id(0)
    me, ctx = info[0], info[1]
    span = nb * sub
    row = lax.broadcasted_iota(jnp.int32, (rows, 128), 0)
    col = lax.broadcasted_iota(jnp.int32, (rows, 128), 1)
    far = jnp.full((rows, 128), -9, jnp.int32)
    pos, first_src, second_src = far, far, far
    ends = [far] * (seqs - 1)
    names = [far] * seqs
    for b in range(nb):
        group = chunk * nb + b
        slot = jnp.int32(0)
        for s in range(groups):
            slot = slot + jnp.where(table[group, s] == me, s, 0)
        base = ctx * tok_count + slot * sub
        low, top = b * sub, (b + 1) * sub
        edge = span + 4 * b
        inner = (row >= low) & (row < top)
        before = (row >= edge) & (row < edge + 2)
        after = (row >= edge + 2) & (row < edge + 4)
        here = inner | before | after
        pos = jnp.where(inner, base + row - low, pos)
        pos = jnp.where(before, base - 2 + row - edge, pos)
        pos = jnp.where(after, base + sub + row - (edge + 2), pos)
        first_src = jnp.where(inner, jnp.where(row == low, edge + 1, row - 1), first_src)
        first_src = jnp.where(after, jnp.where(row == edge + 2, top - 1, row - 1), first_src)
        second_src = jnp.where(inner, jnp.where(row < low + 2, edge + row - low, row - 2), second_src)
        second_src = jnp.where(after, top - 2 + row - (edge + 2), second_src)
        end = jnp.int32(0)
        for j in range(seqs - 1):
            end = end + table[group, groups + j]
            ends[j] = jnp.where(here, end, ends[j])
        for j in range(seqs):
            names[j] = jnp.where(here, table[group, groups + seqs + j], names[j])

    def segment_of(positions):
        found = jnp.zeros((rows, 128), jnp.int32)
        for end in ends:
            found = found + jnp.where(positions >= end, 1, 0)
        return found

    segment = segment_of(pos)
    adapter = names[0]
    for j in range(1, seqs):
        adapter = jnp.where(segment == j, names[j], adapter)
    picked = (col >= adapter * RANK) & (col < adapter * RANK + RANK)
    mask_ref[...] = jnp.where(picked, 1.0, 0.0).astype(bf16)
    source = lax.broadcasted_iota(jnp.int32, (rows, rows), 1)
    for lag, src, ref in ((1, first_src, one_ref), (2, second_src, two_ref)):
        same = (pos >= lag) & (pos < group_tokens) & (segment_of(pos - lag) == segment)
        src = jnp.where(same, src, -9)
        ref[...] = jnp.where(source == src[:, :1], 1.0, 0.0).astype(bf16)


def edges_kernel(dims, table, info, edges_ref, first_ref, last_ref, next_ref, prev_ref):
    groups = dims
    me = info[0]
    for g in range(groups):
        slot = jnp.int32(0)
        for s in range(groups):
            slot = slot + jnp.where(table[g, s] == me, s, 0)
        first_ref[g] = edges_ref[table[g, 0], g, 0:4]
        last_ref[g] = edges_ref[table[g, groups - 1], g, 4:6]
        after = table[g, jnp.minimum(slot + 1, groups - 1)]
        before = table[g, jnp.maximum(slot - 1, 0)]
        rows = edges_ref[after, g, 0:4]
        next_ref[g] = jnp.where(slot < groups - 1, rows, jnp.zeros_like(rows))
        rows = edges_ref[before, g, 4:6]
        prev_ref[g] = jnp.where(slot > 0, rows, jnp.zeros_like(rows))


ACTUAL, STACK, INNER = 4, 12, 20


def stack_rows(info, own, got_first, got_second, halo_own, halo_got, stack, span, half, into):
    block = half // 4
    stack[:span, :half] = own[...]
    stack[:span, half:] = jnp.where(pl.program_id(0) == 0, got_first[...], got_second[...])
    stack[span:, :half] = halo_own[...]
    stack[span:, half:] = halo_got[...]
    for r in range(8):
        into[:, r * block : (r + 1) * block] = stack[:, lanes_at(info[STACK + r], block)]


def input_kernel(info, own, got_first, got_second, halo_own, halo_got, gain, first, mask, x_ref, lhs_ref, scale_ref, stack, first_rel, gain_rel):
    span, half = own.shape
    rows, width = x_ref.shape
    block = half // 4
    stack_rows(info, own, got_first, got_second, halo_own, halo_got, stack, span, half, x_ref)
    for r in range(8):
        first_rel[r * block : (r + 1) * block, :] = first[lanes_at(info[ACTUAL + r], block), :]
        gain_rel[:, r * block : (r + 1) * block] = gain[:, lanes_at(info[ACTUAL + r], block)]

    def visit(at):
        x = x_ref[at, :].astype(f32)
        scale = lax.rsqrt(jnp.mean(x * x, axis=-1, keepdims=True) + norm_eps)
        lhs_ref[at, :width] = (x * scale * gain_rel[0:1, :]).astype(bf16)
        scale_ref[at, :] = jnp.broadcast_to(scale, (scale.shape[0], 128))

    over_row_blocks(rows, 16, visit)
    lhs_ref[:, width:] = dot(lhs_ref[:, :width], first_rel[...]).astype(bf16) * mask[...]


def cotangent_kernel(info, own, got_first, got_second, halo_own, halo_got, second, mask, lhs_ref, stack, second_rel):
    span, half = own.shape
    width = 2 * half
    block = half // 4
    stack_rows(info, own, got_first, got_second, halo_own, halo_got, stack, span, half, lhs_ref)
    for r in range(8):
        second_rel[:, r * block : (r + 1) * block] = second[:, lanes_at(info[ACTUAL + r], block)]
    low = adapter_scale * dot_nt(lhs_ref[:, :width], second_rel[...])
    lhs_ref[:, width:] = low.astype(bf16) * mask[...]


def mixer_parts(refs, cuts):
    if len(cuts) == 1:
        return [[refs[0].at[j] for j in range(3)]], [refs[1]], refs[2:]
    ins = [[refs[0].at[k, j] for j in range(3)] for k in range(2)]
    outs = [refs[1].at[k] for k in range(2)]
    early = pl.program_id(0) < 2
    for k in range(4):
        first, second = refs[2 + 2 * k], refs[3 + 2 * k]
        tiles = [jnp.where(early, first[j], second[j]) for j in range(4)]
        ins.append(tiles[:3])
        outs.append(tiles[3])
    return ins, outs, refs[10:]


def held_mixer_parts(refs, cuts):
    if len(cuts) == 1:
        return *mixer_parts(refs, cuts), lambda: None
    in_own, out_own, *far = refs[:10]
    *refs, near, out_near, distant, sems = refs[10:]
    step = pl.program_id(0)

    def copies(tile):
        at = pl.ds(tile * TILE, TILE)
        yield pltpu.make_async_copy(in_own.at[:, :, :, at], near.at[:, :, :, at], sems.at[tile, 0])
        yield pltpu.make_async_copy(out_own.at[:, at, :], out_near.at[:, at, :], sems.at[tile, 1])
        for k in range(4):
            part = far[2 * k + tile // 2].at[:, :, pl.ds(tile % 2 * TILE, TILE)]
            yield pltpu.make_async_copy(part, distant.at[k, :, :, at], sems.at[tile, 2 + k])

    @pl.when(step == 0)
    def _():
        for tile in range(4):
            for copy in copies(tile):
                copy.start()

    def arrived():
        for tile in range(4):

            @pl.when(step == tile)
            def _(tile=tile):
                for copy in copies(tile):
                    copy.wait()

    at = pl.ds(pl.multiple_of(step * TILE, TILE), TILE)
    ins = [[near.at[k, j, :, at] for j in range(3)] for k in range(2)]
    outs = [out_near.at[k, at, :] for k in range(2)]
    for k in range(4):
        ins.append([distant.at[k, j, :, at] for j in range(3)])
        outs.append(distant.at[k, 3, :, at])
    return ins, outs, refs, arrived


def mixer_kernel(cuts, lhs, one, two, taps, in_expand, out_shrink, *refs):
    in_parts, out_parts, refs = mixer_parts(refs, cuts)
    b_ref, c_ref, v_ref, conv_ref, gated_ref, part_first, part_second, acc = refs
    width = cuts[-1][1]
    step = pl.program_id(0)

    def project(j):
        total = dot(lhs[:, width:], in_expand[j] * jnp.asarray(adapter_scale, bf16))
        for (low, top), part in zip(cuts, in_parts):
            total = total + dot(lhs[:, low:top], part[j][...])
        return total

    b, c, v = project(0), project(1), project(2)
    b_ref[...] = b
    c_ref[...] = c
    v_ref[...] = v
    mixed = (b * v).astype(bf16)
    w = taps[...].astype(f32)
    conv = w[0:1] * mixed.astype(f32) + w[1:2] * dot(one[...], mixed) + w[2:3] * dot(two[...], mixed)
    conv_ref[...] = conv
    gated = (c * conv).astype(bf16)
    gated_ref[...] = gated

    @pl.when(step == 0)
    def _():
        acc[...] = jnp.zeros_like(acc)

    for (low, top), part in zip(cuts, out_parts):
        acc[:, low:top] += dot(gated, part[...])
    acc[:, width:] += dot(gated, out_shrink[...])

    @pl.when(step == pl.num_programs(0) - 1)
    def _():
        cut = part_first.shape[0]
        part_first[...] = acc[:cut, :].astype(bf16)
        part_second[...] = acc[cut:, :].astype(bf16)


def blocks_across(ref, value, earlier=None, *at):
    for i in range(value.shape[1] // 128):
        block = value[:, i * 128 : (i + 1) * 128]
        block = block if earlier is None else block + earlier[(*at, i)]
        ref[(*at, i)] = block.astype(ref.dtype)


def blocks_down(ref, value, earlier=None, *at):
    for i in range(value.shape[0] // 128):
        block = value[i * 128 : (i + 1) * 128, :]
        block = block if earlier is None else block + earlier[(*at, i)]
        ref[(*at, i)] = block.astype(ref.dtype)


def middle_kernel(info, x, part_first, part_second, got_first, got_second, mask, gain, out_second, ffn_first,
                  hidden_ref, lhs, low_ref, both_ref, added, first_rel, second_rel, gain_rel):
    width = x.shape[1]
    block = width // 8
    rank = mask.shape[1]
    for r in range(8):
        at = lanes_at(info[ACTUAL + r], block)
        here = slice(r * block, (r + 1) * block)
        first_rel[here, :] = ffn_first[at, :]
        second_rel[:, here] = out_second[:, at]
        gain_rel[:, here] = gain[:, at]
    cut = part_first.shape[0]
    for own, got, base in ((part_first, got_first, 0), (part_second, got_second, cut)):
        both_ref[base : base + own.shape[0], :] = own[...].astype(f32) + got[...].astype(f32)
    low = both_ref[:, width:].astype(bf16) * mask[...]
    low_ref[...] = low
    added[...] = dot(low, second_rel[...])

    def visit(at):
        hidden = x[at, :].astype(f32) + (both_ref[at, :width] + adapter_scale * added[at, :])
        hidden_ref[at, :] = hidden
        scale = lax.rsqrt(jnp.mean(hidden * hidden, axis=-1, keepdims=True) + norm_eps)
        lhs[at, :width] = (hidden * scale * gain_rel[0:1, :]).astype(bf16)

    over_row_blocks(x.shape[0], 16, visit)
    low = dot(lhs[:, :width], first_rel[...]).astype(bf16)
    lhs[:, width : width + rank] = low[:, :rank] * mask[...]
    lhs[:, width + rank :] = low[:, rank:] * mask[...]


def feed_kernel(cuts, span, later, info, lhs, glhs, ffn_expand, down_shrink, *refs):
    earlier = refs[0] if later else None
    refs = refs[1:] if later else refs
    if len(cuts) == 1:
        gu_parts, down_parts, refs = [[refs[0].at[0], refs[0].at[1]]], [refs[1]], refs[2:]
        arrived = lambda: None
    else:
        gu_parts = [[refs[0].at[k, j] for j in range(2)] for k in range(2)]
        down_parts = [refs[1].at[k] for k in range(2)]
        count = len(FEED_CUTS)
        far, refs = refs[2 : 2 + 4 * count], refs[2 + 4 * count :]
        slots, sems, refs = refs[-2], refs[-1], refs[:-2]
        step, steps = pl.program_id(0), FEED_CUTS[-1][1]

        def fetch(tile):
            for i, (low, top) in enumerate(FEED_CUTS):

                @pl.when((tile >= low) & (tile < top))
                def _(i=i, low=low):
                    at = pl.ds(pl.multiple_of((tile - low) * TILE, TILE), TILE)
                    for k in range(4):
                        slot = lax.rem(tile, 2)
                        pltpu.make_async_copy(far[k * count + i].at[:, :, at], slots.at[slot, k], sems.at[slot, k]).start()

        @pl.when(step == 0)
        def _():
            fetch(step)

        @pl.when(step + 1 < steps)
        def _():
            fetch(step + 1)

        slot = lax.rem(step, 2)
        here = slots.at[slot]
        for k in range(4):
            gu_parts.append([here.at[k, 0], here.at[k, 1]])
            down_parts.append(here.at[k, 2])

        def arrived():
            for k in range(4):
                pltpu.make_async_copy(far[k * count].at[:, :, :TILE], slots.at[slot, k], sems.at[slot, k]).wait()
    f_ref, own_ref, send_ref, grads, acc_d, acc_f = refs
    width = cuts[-1][1]
    half = width // 2
    rank = down_shrink.shape[1]
    step = pl.program_id(0)

    @pl.when(step == 0)
    def _():
        acc_d[...] = jnp.zeros_like(acc_d)
        acc_f[...] = jnp.zeros_like(acc_f)

    arrived()
    lows = [lhs[:, width : width + rank], lhs[:, width + rank :]]
    half_scale = jnp.asarray(adapter_scale, bf16)

    def project(j):
        total = dot(lows[j], ffn_expand[j] * half_scale)
        for (low, top), w in zip(cuts, gu_parts):
            total = total + dot(lhs[:, low:top], w[j][...])
        return total

    gate, up = project(0), project(1)
    sig = jax.nn.sigmoid(gate)
    silu = gate * sig
    act = (silu * up).astype(bf16)
    g_low = glhs[:, width:]
    grad_act = dot_nt(g_low, down_shrink[...])
    for (low, top), w in zip(cuts, down_parts):
        grad_act = grad_act + dot_nt(glhs[:, low:top], w[...])
    gg = (grad_act * up * (sig * (1.0 + gate * (1.0 - sig)))).astype(bf16)
    gu = (grad_act * silu).astype(bf16)
    for (low, top), w in zip(cuts, down_parts):
        acc_d[:span, low:top] += dot(act[:span], w[...])
    acc_d[:span, width:] += dot(act[:span], down_shrink[...])
    for (low, top), w in zip(cuts, gu_parts):
        acc_f[:, low:top] += dot_nt(gg, w[0][...]) + dot_nt(gu, w[1][...])
    acc_f[:, width : width + rank] += dot_nt(gg, ffn_expand[0] * half_scale)
    acc_f[:, width + rank :] += dot_nt(gu, ffn_expand[1] * half_scale)
    blocks_down(grads, dot_tn(act[:span], g_low[:span]), earlier, 0)
    blocks_across(grads, adapter_scale * dot_tn(lows[0][:span], gg[:span]), earlier, 1)
    blocks_across(grads, adapter_scale * dot_tn(lows[1][:span], gu[:span]), earlier, 2)

    @pl.when(step == pl.num_programs(0) - 1)
    def _():
        f_ref[...] = acc_f[...].astype(bf16)
        place = info[3]
        own_ref[:, :half] = acc_d[:span, lanes_at(place, half)].astype(bf16)
        send_ref[:, :half] = acc_d[:span, lanes_at(1 - place, half)].astype(bf16)
        own_ref[:, half:] = acc_d[:span, width:].astype(bf16)
        send_ref[:, half:] = acc_d[:span, width:].astype(bf16)


def back_kernel(cuts, span, later, info, part, got, hidden, glhs, lhs_two, out_low, lhs_one, mask, gain, out_second, ffn_first,
                one, two, taps, in_expand, out_shrink, b_ref, c_ref, v_ref, conv_ref, gated_ref, *refs):
    in_parts, out_parts, refs, arrived = held_mixer_parts(refs, cuts)
    ffn_earlier, second_earlier, grads_earlier = refs[:3] if later else (None,) * 3
    refs = refs[3:] if later else refs
    (own_ref, send_ref, rank_ref, gh_ref, ffn_grad, second_grad, grads,
     acc, branch, first_rel, second_rel, gain_rel) = refs
    width = cuts[-1][1]
    half = width // 2
    block = width // 8
    rank = mask.shape[1]
    step = pl.program_id(0)
    place = info[3]

    @pl.when(step == 0)
    def _():
        for r in range(8):
            at = lanes_at(info[ACTUAL + r], block)
            here = slice(r * block, (r + 1) * block)
            first_rel[here, :] = ffn_first[at, :]
            second_rel[:, here] = out_second[:, at]
            gain_rel[:, here] = gain[:, at]
        low = (part[:, width:].astype(f32) + got[:, width:].astype(f32)).astype(bf16)
        low = jnp.concatenate([low[:, :rank] * mask[...], low[:, rank:] * mask[...]], axis=1)
        acc[:, :width] = dot_nt(low, first_rel[...])

        def visit(at):
            both = part[at, :width].astype(f32) + got[at, :width].astype(f32)
            h = hidden[at, :]
            scale = lax.rsqrt(jnp.mean(h * h, axis=-1, keepdims=True) + norm_eps)
            unit = h * scale
            grad_unit = (both + acc[at, :width]) * gain_rel[0:1, :]
            grad = glhs[at, :width].astype(f32) + scale * (
                grad_unit - unit * jnp.mean(grad_unit * unit, axis=-1, keepdims=True)
            )
            gh_ref[at, :] = grad
            branch[at, :width] = grad.astype(bf16)

        over_row_blocks(hidden.shape[0], 16, visit)
        b_low = adapter_scale * dot_nt(branch[:, :width], second_rel[...])
        branch[:, width:] = b_low.astype(bf16) * mask[...]
        for i in range(4):
            at = lanes_at(place * 4 + info[INNER + i], block)
            value = dot_tn(lhs_two[:span, at], low[:span])
            for k in range(2):
                blocks_down(ffn_grad, value[:, k * 128 : (k + 1) * 128], ffn_earlier, i, k)
            blocks_across(second_grad, adapter_scale * dot_tn(out_low[:span, :], branch[:span, at]), second_earlier, i)
        acc[...] = jnp.zeros_like(acc)

    arrived()
    total = dot_nt(branch[:, width:], out_shrink[...])
    for (low, top), w in zip(cuts, out_parts):
        total = total + dot_nt(branch[:, low:top], w[...])
    grad_c = total * conv_ref[...]
    conv = total * c_ref[...]
    w = taps[...].astype(f32)
    high = conv.astype(bf16)
    rest = (conv - high.astype(f32)).astype(bf16)
    mixed = (
        w[0:1] * conv
        + w[1:2] * (dot_tn(one[...], high) + dot_tn(one[...], rest))
        + w[2:3] * (dot_tn(two[...], high) + dot_tn(two[...], rest))
    )
    proj = [
        (mixed * v_ref[...]).astype(bf16)[:span],
        grad_c.astype(bf16)[:span],
        (mixed * b_ref[...]).astype(bf16)[:span],
    ]
    half_scale = jnp.asarray(adapter_scale, bf16)
    for (low, top), w in zip(cuts, in_parts):
        acc[:span, low:top] += dot_nt(proj[0], w[0][...]) + dot_nt(proj[1], w[1][...]) + dot_nt(proj[2], w[2][...])
    acc[:span, width:] += (
        dot_nt(proj[0], in_expand[0] * half_scale)
        + dot_nt(proj[1], in_expand[1] * half_scale)
        + dot_nt(proj[2], in_expand[2] * half_scale)
    )
    low_one = lhs_one[:span, width:]
    for j in range(3):
        blocks_across(grads, adapter_scale * dot_tn(low_one, proj[j]), grads_earlier, j)
    blocks_down(grads, dot_tn(gated_ref[:span, :], branch[:span, width:]), grads_earlier, 3)

    @pl.when(step == pl.num_programs(0) - 1)
    def _():
        own_ref[...] = acc[:span, lanes_at(place, half)].astype(bf16)
        send_ref[...] = acc[:span, lanes_at(1 - place, half)].astype(bf16)
        rank_ref[:, :rank] = acc[:span, width:].astype(bf16)

        def visit(at):
            sums = acc[at, :width].astype(bf16).astype(f32) * lhs_one[at, :width].astype(f32)
            stat = jnp.sum(sums, axis=-1, keepdims=True)
            high = stat.astype(bf16).astype(f32)
            middle = (stat - high).astype(bf16).astype(f32)
            rest = stat - high - middle
            lane = lax.broadcasted_iota(jnp.int32, (stat.shape[0], 128), 1)
            packed = jnp.where(lane == 0, high, jnp.where(lane == 1, middle, jnp.where(lane == 2, rest, 0.0)))
            rank_ref[at, rank:] = packed.astype(bf16)

        over_row_blocks(span, 16, visit)


def rank_rows(own, got, mask):
    rank = mask.shape[1]
    sums = own[...].astype(f32) + got[...].astype(f32)
    return sums[:, :rank].astype(bf16) * mask[...], sums[:, rank:]


def output_kernel(info, *refs):
    output_rows(info, *refs[:8], *refs[-2:])


def output_rows(info, own, got, rank_own, rank_got, hidden, mask, g, second, out_ref, grad_ref):
    low, _ = rank_rows(rank_own, rank_got, mask)
    down = own[...].astype(f32) + got[...].astype(f32)
    out_ref[...] = (hidden[...] + (down + adapter_scale * dot(low, second[...]))).astype(bf16)
    blocks_across(grad_ref, adapter_scale * dot_tn(low, g[...]))


def rank_kernel(info, own, got, mask, normed, grad_ref):
    low, _ = rank_rows(own, got, mask)
    blocks_down(grad_ref, dot_tn(normed[...], low))


def final_kernel(width, info, *refs):
    final_rows(width, info, *refs[:11], refs[-1])


def final_rows(width, info, own, got, rank_own, rank_got, gh, x, low, scale, mask, gain, first, grad_ref):
    n_low, stat = rank_rows(rank_own, rank_got, mask)
    stat = jnp.sum(stat, axis=-1, keepdims=True)
    stat = stat + jnp.sum(n_low.astype(f32) * low[...].astype(f32), axis=-1, keepdims=True)
    stat = stat / width
    scale_rows = scale[:, 0:1]
    unit = x[...].astype(f32) * scale_rows
    grad = own[...].astype(f32) + got[...].astype(f32) + dot_nt(n_low, first[...])
    grad_ref[...] = gh[...] + scale_rows * (grad * gain[0:1, :].astype(f32) - unit * stat)


def places(info, pieces):
    me, ctx = info[0], info[1]
    for place in range(4 * pieces):
        c, x, z = place // (2 * pieces), place // pieces % 2, place % pieces
        far_c, far_x = (me % 2) ^ c, (me // 2) ^ x
        yield place, 2 * far_c + far_x, lax.rem(ctx + pieces - z, pieces)


def unpack_feed_kernel(tiles, total, expand_ref, first_ref):
    for h in range(tiles):
        for k in range(2):
            column = h * 256 + k * 128
            for j in range(3):
                row = ((h * 3 + j) * 2 + k) * 128
                value = total[row : row + 128, :].astype(f32)
                if j:
                    expand_ref[j - 1, :, column : column + 128] = value
                else:
                    first_ref[column : column + 128, :] = value


def gather_feed_kernel(pieces, tiles, info, own, x, c, cx, expand_ref, first_ref, kept):
    n = own.shape[1]
    for place, which, distance in places(info, pieces):
        for k, part in enumerate((own, x, c, cx)):

            @pl.when(which == k)
            def _(part=part, place=place, distance=distance):
                kept[place * n : (place + 1) * n, :] = part[distance]

    unpack_feed_kernel(tiles, kept, expand_ref, first_ref)


def gather_rows_kernel(pieces, info, own, x, c, cx, out):
    for place, which, distance in places(info, pieces):
        for k, part in enumerate((own, x, c, cx)):

            @pl.when(which == k)
            def _(part=part, place=place, distance=distance):
                out[place] = part[distance]


def unpack_early_kernel(pieces, info, own, x, c, cx, ffn_ref, second_ref, expand_ref, out_ref, kept):
    gather_rows_kernel(pieces, info, own, x, c, cx, kept)
    tens = info[2]
    for place in range(4 * pieces):
        i, k, part = place // 4, place // 2 % 2, place % 2
        for t in range(2):
            base = pl.multiple_of(jnp.where(tens == t, 0, 192), 64)
            ffn_ref[t * 1024 + i * 256 + part * 128 : t * 1024 + i * 256 + part * 128 + 128, k * 128 : (k + 1) * 128] = (
                kept[place, pl.ds(base, 128), :].astype(f32)
            )
            column = t * 1024 + i * 256 + k * 128
            second_ref[part * 64 : part * 64 + 64, column : column + 128] = kept[
                place, pl.ds(pl.multiple_of(base + 128, 64), 64), :
            ].astype(f32)
        h, j = place // 4, place % 4
        for k in range(2):
            value = kept[place, 384 + k * 128 : 512 + k * 128, :].astype(f32)
            column = h * 256 + k * 128
            if j < 3:
                expand_ref[j, :, column : column + 128] = value
            else:
                out_ref[column : column + 128, :] = value


def unpack_late_kernel(pieces, info, own, x, c, cx, first_ref, second_ref, kept):
    gather_rows_kernel(pieces, info, own, x, c, cx, kept)
    tens = info[2]
    for place in range(4 * pieces):
        for t in range(2):
            base = pl.multiple_of(jnp.where(tens == t, 0, 128), 128)
            row = t * 1024 + place * 64
            first_ref[row : row + 64, :] = kept[place, pl.ds(base, 64), :].astype(f32)
            row, column = place % 2 * 64, t * 1024 + place // 2 * 128
            second_ref[row : row + 64, column : column + 128] = kept[
                place, pl.ds(pl.multiple_of(base + 64, 64), 64), :
            ].astype(f32)


def after(array, *gates):
    return lax.optimization_barrier((array,) + gates)[0] if gates else array


def swap_tensor(array):
    return lax.ppermute(array, "tensor", [(0, 1), (1, 0)])


def body(
    block_input,
    cotangent,
    deal_order,
    seq_lengths,
    seq_adapter,
    mixer_gain,
    ffn_gain,
    conv_taps,
    in_weight,
    out_weight,
    gateup_weight,
    down_weight,
    input_adapter_shrink,
    in_expand,
    out_shrink,
    output_adapter_expand,
    ffn_shrink,
    ffn_expand,
    down_shrink,
    down_adapter_expand,
):
    tok_count, half = block_input.shape
    width = 2 * half
    rank = input_adapter_shrink.shape[1]
    hidden_units = gateup_weight.shape[2]
    groups = lax.axis_size("dp")
    pieces = lax.axis_size("ctx")
    sub = tok_count // groups
    group_tokens = pieces * tok_count
    seqs = seq_lengths.shape[0]
    nb = groups // CHUNKS
    span = nb * sub
    halo = -(-4 * nb // 16) * 16
    rows = span + halo
    special = groups == 4 and pieces % 2 == 0
    me = lax.axis_index("dp")
    ctx = lax.axis_index("ctx")
    tens = lax.axis_index("tensor")
    if special:
        xb, cb, zb = me // 2, me % 2, ctx % 2
    else:
        xb = cb = zb = jnp.int32(0)
    flip = xb ^ tens

    actual, in_stack, inner = [], [], []
    for rx in (0, 1):
        for rc in (0, 1):
            for rh in (0, 1):
                low = (rc ^ (cb & rx)) * 2 + (rh ^ (zb & rx))
                actual.append((rx ^ xb) * 4 + low)
                in_stack.append((rx ^ flip) * 4 + low)
    for bc in (0, 1):
        for bh in (0, 1):
            inner.append((bc ^ (cb & flip)) * 2 + (bh ^ (zb & flip)))
    info = jnp.stack([me, ctx, tens, flip, *actual, *in_stack, *inner]).astype(jnp.int32)

    core_route = [(0, 1), (1, 0), (2, 3), (3, 2)]
    x_route = [(0, 2), (2, 0), (1, 3), (3, 1)]
    z_route = [(i, i ^ 1) for i in range(pieces)]
    gates = []

    def wait(*values):
        gates[:] = values

    def begin(axis, route, array):
        return lax.ppermute(after(array, *gates), axis, route)

    def core(array):
        return begin("dp", core_route, array)

    def over_x(array):
        return begin("dp", x_route, array)

    def over_z(array):
        return begin("ctx", z_route, array)

    def over_y(array):
        return begin("tensor", [(0, 1), (1, 0)], array)

    def tiles_beside(array):
        tiles = array.reshape(-1, TILE, array.shape[1])
        return jnp.concatenate([tiles[i] for i in range(tiles.shape[0])], axis=1)

    def mixer_piece(k):
        at = slice(k * half // 2, (k + 1) * half // 2)
        return jnp.concatenate([mine(in_weight[:, :, at], 1), tiles_beside(mine(out_weight[at], 1))[None]], axis=0)

    def feed_piece(k):
        low, top = FEED_CUTS[k]
        at = slice(low * TILE, top * TILE)
        return jnp.concatenate([mine(gateup_weight[:, :, at], 1), tiles_beside(mine(down_weight[at], 1))[None]], axis=0)

    def chip_pair(array):
        return lax.all_gather(after(array, *gates), "dp", axis_index_groups=[[0, 1], [2, 3]])

    def mine(shard, axis):
        n = shard.shape[axis] // 2
        return lax.dynamic_slice_in_dim(shard, zb * n, n, axis)

    numbers = jnp.concatenate([deal_order[0], seq_lengths, seq_adapter])
    digits = jnp.concatenate([numbers // 64, numbers % 64]).astype(bf16)
    x_blocks = block_input.reshape(groups, sub, half)
    g_blocks = cotangent.reshape(groups, sub, half)
    digit_rows = jnp.zeros((groups, 2, half), bf16).at[0, 0, : digits.shape[0]].set(digits)
    edges = jnp.concatenate([x_blocks[:, :2], g_blocks[:, :2], x_blocks[:, sub - 2 :], digit_rows], axis=1)

    if special:
        in_own = chip_pair(in_weight)
        mixer_x, mixer_z, mixer_xc, mixer_zc = ([None] * 2 for _ in range(4))
        feed_x, feed_z, feed_xc, feed_zc = ([None] * len(FEED_CUTS) for _ in range(4))
        mixer_packed = [mixer_piece(k) for k in range(2)]
        feed_packed = [feed_piece(k) for k in range(len(FEED_CUTS))]
    x_got = [over_y(block_input[:span]), None]
    if special:
        mixer_x[0] = over_x(mixer_packed[0])
    all_edges = lax.all_gather(edges, "dp", axis=0, tiled=False)
    digits = all_edges[:, 0, 6, : 2 * numbers.shape[0]].astype(jnp.int32)
    table = digits[:, : numbers.shape[0]] * 64 + digits[:, numbers.shape[0] :]
    dims = (groups, seqs, sub, nb, rows, tok_count, group_tokens)
    per_chunk = lambda c, *_: (c, 0, 0)
    mask, one, two = call(
        functools.partial(tables_kernel, dims), (CHUNKS,), (table, info), [],
        [
            ((CHUNKS, rows, rank), bf16, (None, rows, rank), per_chunk),
            ((CHUNKS, rows, rows), bf16, (None, rows, rows), per_chunk),
            ((CHUNKS, rows, rows), bf16, (None, rows, rows), per_chunk),
        ],
    )
    first_heads, last_tails, next_near, prev_near = call(
        functools.partial(edges_kernel, groups), (1,), (table, info), [(all_edges, None, None)],
        [
            ((groups, 4, half), bf16, None, None),
            ((groups, 2, half), bf16, None, None),
            ((groups, 4, half), bf16, None, None),
            ((groups, 2, half), bf16, None, None),
        ],
    )
    stage = [all_edges, x_got[0]] + ([mixer_x[0], in_own, mixer_packed[1], feed_packed[0]] if special else [])
    wait(*stage)
    from_next = begin("ctx", [(i + 1, i) for i in range(pieces - 1)], first_heads)
    from_prev = begin("ctx", [(i, i + 1) for i in range(pieces - 1)], last_tails)
    x_got[1] = over_y(block_input[span:])
    stage = [from_next, from_prev, x_got[1]]
    if special:
        mixer_x[1], mixer_z[0] = over_x(mixer_packed[1]), over_z(mixer_x[0])
        out_own = chip_pair(out_weight)
        stage += [mixer_x[1], mixer_z[0], out_own]
    deal_all = table[:, :groups]
    at_end = (deal_all[:, groups - 1] == me)[:, None, None]
    at_start = (deal_all[:, 0] == me)[:, None, None]
    next_rows = jnp.where(at_end, from_next, next_near)
    prev_rows = jnp.where(at_start, from_prev, prev_near)
    halo_x = jnp.concatenate([prev_rows, next_rows[:, :2]], axis=1)
    halo_g = jnp.concatenate([jnp.zeros_like(prev_rows), next_rows[:, 2:]], axis=1)
    halo_own = jnp.stack([halo_x, halo_g]).reshape(2, CHUNKS, 4 * nb, half)
    halo_own = jnp.pad(halo_own, ((0, 0), (0, 0), (0, halo - 4 * nb), (0, 0)))
    wait(*stage)
    halo_got = over_y(halo_own)
    g_got = [over_y(after(cotangent[:span], halo_got)), None]
    stage = [g_got[0]]
    if special:
        feed_x[0], mixer_z[1] = over_x(feed_packed[0]), over_z(mixer_x[1])
        mixer_xc[0] = core(mixer_x[0])
        mixer_xc[1] = core(after(mixer_x[1], mixer_xc[0]))
        mixer_zc[0] = core(after(mixer_z[0], mixer_xc[1]))
        gu_own = chip_pair(gateup_weight)
        stage += [feed_x[0], mixer_z[1], mixer_xc[0], mixer_xc[1], mixer_zc[0], feed_packed[1]]

    gain_one, gain_two = mixer_gain[None, :].astype(f32), ffn_gain[None, :].astype(f32)
    ext_one, ext_two = width + rank, width + 2 * rank

    def stacked(array, last):
        return (array, (None,) + array.shape[1:], lambda c, *_: (c, 0, 0))

    def joined_inputs(own, got, which):
        def halo_of(array):
            return (array, (None, None, halo, half), lambda c, *_: (which, c, 0, 0))

        return [
            (own, (span, half), lambda c, *_: (c, 0)),
            (got[0], None, None),
            (got[1], None, None),
            halo_of(halo_own),
            halo_of(halo_got),
        ]

    x_full, lhs_one, scale = call(
        input_kernel, (CHUNKS,), (info,),
        joined_inputs(block_input, x_got, 0)
        + [(gain_one, None, None), (input_adapter_shrink, None, None), stacked(mask, rank)],
        [
            ((CHUNKS, rows, width), bf16, (None, rows, width), per_chunk),
            ((CHUNKS, rows, ext_one), bf16, (None, rows, ext_one), per_chunk),
            ((CHUNKS, rows, 128), f32, (None, rows, 128), per_chunk),
        ],
        [
            pltpu.VMEM((rows, width), bf16),
            pltpu.VMEM((width, rank), bf16),
            pltpu.VMEM((1, width), f32),
        ],
    )
    wait(*stage, lhs_one)
    g_got[1] = over_y(cotangent[span:])
    stage = [g_got[1]]
    if special:
        n = width // 8
        cuts = ((0, 2 * n), (2 * n, 4 * n), (4 * n, 5 * n), (5 * n, 6 * n), (6 * n, 7 * n), (7 * n, 8 * n))
        mixer_zc[1] = core(mixer_z[1])
        feed_x[1], feed_z[0], feed_xc[0] = over_x(feed_packed[1]), over_z(feed_x[0]), core(feed_x[0])
        stage += [feed_x[1], feed_z[0], feed_xc[0], feed_packed[2]]
        mixer_inputs = lambda: (
            [(in_own, (2, 3, in_own.shape[2], TILE), lambda h, *_: (0, 0, 0, h)),
             (out_own, (2, TILE, out_own.shape[2]), lambda h, *_: (0, h, 0))]
            + [(w, (4, TILE, TILE), (lambda h, *_: (0, 0, jnp.minimum(h, 1))) if i == 0 else (lambda h, *_: (0, 0, jnp.maximum(h - 2, 0))))
               for part in (mixer_x, mixer_z, mixer_xc, mixer_zc) for i, w in enumerate(part)]
        )
    else:
        cuts = ((0, width),)
        in_parts = [lax.all_gather(in_weight, "dp", axis=1, tiled=True)]
        out_parts = [lax.all_gather(out_weight, "dp", axis=1, tiled=True)]
        gu_parts = [lax.all_gather(gateup_weight, "dp", axis=1, tiled=True)]
        down_parts = [lax.all_gather(down_weight, "dp", axis=1, tiled=True)]
        mixer_inputs = lambda: [columns(in_parts[0]), row_tiles(out_parts[0])]

    def picked(array, c):
        return (array, (None,) + array.shape[1:], lambda *_: (c, 0, 0))

    def columns(array):
        return (array, array.shape[:-1] + (TILE,), lambda h, *_: (0,) * (array.ndim - 1) + (h,))

    def row_tiles(array):
        lead = array.ndim - 2
        return (array, array.shape[:lead] + (TILE, array.shape[-1]), lambda h, *_: (0,) * lead + (h, 0))

    def feed_step(k):
        count = len(FEED_CUTS)
        if k < count:
            feed_x[k] = over_x(feed_packed[k])
            stage.extend([feed_x[k]] + feed_packed[k + 1 : k + 2])
        if 0 <= k - 1 < count:
            feed_z[k - 1], feed_xc[k - 1] = over_z(feed_x[k - 1]), core(feed_x[k - 1])
            stage.extend([feed_z[k - 1], feed_xc[k - 1]])
        if 0 <= k - 2 < count:
            feed_zc[k - 2] = core(feed_z[k - 2])
            stage.append(feed_zc[k - 2])

    mixer_steps = half // TILE
    feed_steps = hidden_units // TILE
    column_out = lambda h, *_: (0, h)
    row_halves = (rows // 32 * 16, rows - rows // 32 * 16)
    chunks = []
    for c in range(CHUNKS):
        gate_b, gate_c, values, conv, gated, *part = call(
            functools.partial(mixer_kernel, cuts), (mixer_steps,), (),
            [picked(lhs_one, c), picked(one, c), picked(two, c), columns(conv_taps), columns(in_expand), row_tiles(out_shrink)]
            + mixer_inputs(),
            [((rows, half), f32, (rows, TILE), column_out)] * 4
            + [((rows, half), bf16, (rows, TILE), column_out)]
            + [((n, ext_one), bf16, None, None) for n in row_halves],
            [pltpu.VMEM((rows, ext_one), f32)],
            flops=2 * rows * half * ext_one * 4,
        )
        chunks.append(dict(b=gate_b, c=gate_c, v=values, conv=conv, gated=gated, part=part))
        if c == 0:
            wait(*stage, *part)
            chunks[0]["got"] = [over_y(part[0]), None]
            stage = [chunks[0]["got"][0]]
            if special:
                feed_step(2)
                down_own = chip_pair(down_weight)
    def middle(i):
        c = chunks[i]
        c["hidden"], c["lhs"], c["low"] = call(
            middle_kernel, (1,), (info,),
            [picked(x_full, i)] + [(w, None, None) for w in (*c["part"], *c["got"])]
            + [picked(mask, i), (gain_two, None, None), (output_adapter_expand, None, None), (ffn_shrink, None, None)],
            [((rows, width), f32, None, None), ((rows, ext_two), bf16, None, None), ((rows, rank), bf16, None, None)],
            [
                pltpu.VMEM((rows, ext_one), f32),
                pltpu.VMEM((rows, width), f32),
                pltpu.VMEM((width, 2 * rank), bf16),
                pltpu.VMEM((rank, width), bf16),
                pltpu.VMEM((1, width), f32),
            ],
        )

    wait(*stage, *chunks[1]["part"])
    chunks[0]["got"][1] = over_y(chunks[0]["part"][1])
    stage = [chunks[0]["got"][1]]
    if special:
        feed_step(3)
    wait(*stage)
    chunks[1]["got"] = [over_y(chunks[1]["part"][0]), None]
    stage = [chunks[1]["got"][0]]
    if special:
        feed_step(4)
    (glhs,) = call(
        cotangent_kernel, (CHUNKS,), (info,),
        joined_inputs(cotangent, g_got, 1) + [(down_adapter_expand, None, None), stacked(mask, rank)],
        [((CHUNKS, rows, ext_one), bf16, (None, rows, ext_one), per_chunk)],
        [pltpu.VMEM((rows, width), bf16), pltpu.VMEM((rank, width), bf16)],
    )

    wait(*stage, glhs)
    chunks[1]["got"][1] = over_y(chunks[1]["part"][1])
    stage = [chunks[1]["got"][1]]
    middle(0)
    middle(1)
    if special:
        feed_step(5)
        wait(*stage, chunks[0]["lhs"])
        stage = [chunks[1]["lhs"]]
        feed_step(6)
        wait(*stage)
        feed_step(7)
        whole = [(gu_own, (2, 2, gu_own.shape[2], TILE), lambda h, *_: (0, 0, 0, h)),
                 (down_own, (2, TILE, down_own.shape[2]), lambda h, *_: (0, h, 0))]
        feed_inputs = whole + [(w, "any", None) for part in (feed_x, feed_z, feed_xc, feed_zc) for w in part]
    else:
        feed_inputs = [columns(gu_parts[0]), row_tiles(down_parts[0])]

    for i, c in enumerate(chunks):
        f_part, d_own, d_send, grads = call(
            functools.partial(feed_kernel, cuts, span, i > 0), (feed_steps,), (info,),
            [(c["lhs"], None, None), picked(glhs, i), columns(ffn_expand), row_tiles(down_shrink)]
            + ([(chunks[0]["feed_grads"], (None, 3, 2, 128, 128), lambda h, *_: (h, 0, 0, 0, 0))] if i else [])
            + feed_inputs,
            [
                ((rows, ext_two), bf16, None, None),
                ((span, half + rank), bf16, None, None),
                ((span, half + rank), bf16, None, None),
                ((feed_steps, 3, 2, 128, 128), bf16 if i else f32, (None, 3, 2, 128, 128), lambda h, *_: (h, 0, 0, 0, 0)),
            ],
            [
                pltpu.VMEM((rows, ext_one), f32),
                pltpu.VMEM((rows, ext_two), f32),
            ]
            + ([pltpu.VMEM((2, 4, 3, TILE, TILE), bf16), pltpu.SemaphoreType.DMA((2, 4))] if special else []),
            flops=2 * rows * hidden_units * ext_two * 6,
        )
        c.update(f_own=f_part, d_own=d_own, d_send=d_send, feed_grads=grads)
    def summed(name):
        return sum(c[name] for c in chunks).astype(bf16)

    def take(array, i):
        return lax.dynamic_index_in_dim(array, i, 0, keepdims=False)

    def add(*terms):
        return sum(t.astype(f32) for t in terms).astype(bf16)

    core_bit, x_bit = me % 2, me // 2
    shifts = [[(i, (i + k) % pieces) for i in range(pieces)] for k in range(1, pieces)]

    def cut(*arrays):
        return jnp.concatenate([a.reshape(2, 2, pieces, -1, 128) for a in arrays], axis=3)

    def scatter_core(total):
        return add(take(total, core_bit), lax.ppermute(take(total, 1 - core_bit), "dp", core_route))

    def scatter_x(total):
        return add(take(total, x_bit), lax.ppermute(take(total, 1 - x_bit), "dp", x_route))

    def scatter_z(total):
        sent = [lax.ppermute(take(total, (ctx + k) % pieces), "ctx", route) for k, route in enumerate(shifts, 1)]
        return add(take(total, ctx), *sent)

    def gather_z(total):
        return jnp.stack([total] + [lax.ppermute(total, "ctx", route) for route in shifts])

    def gather_chip(total):
        over_x = lax.ppermute(total, "dp", x_route)
        return [total, over_x] + [lax.ppermute(v, "dp", core_route) for v in (total, over_x)]

    for c in chunks:
        c["f_got"] = swap_tensor(c["f_own"])
    feed = chunks[-1]["feed_grads"]
    if special:
        feed_sum = scatter_core(cut(after(feed, chunks[0]["f_got"])))
    held_scratch = []
    if special:
        held = [in_own, out_own] + [w for part in (mixer_x, mixer_z, mixer_xc, mixer_zc) for w in part]
        held_inputs = [(w, "any", None) for w in held]
        held_scratch = [
            pltpu.VMEM(in_own.shape, bf16),
            pltpu.VMEM(out_own.shape, bf16),
            pltpu.VMEM((4, 4, TILE, half), bf16),
            pltpu.SemaphoreType.DMA((4, 6)),
        ]
    for i, c in enumerate(chunks):
        f_got = after(c["f_got"], *([feed_sum] if special else []), *([chunks[0]["n_rank"]] if i else []))
        n_own, n_send, n_rank, grad_hidden, ffn_grad, second_grad, grads = call(
            functools.partial(back_kernel, cuts, span, i > 0), (mixer_steps,), (info,),
            [(c["f_own"], None, None), (f_got, None, None), (c["hidden"], None, None), picked(glhs, i),
             (c["lhs"], None, None), (c["low"], None, None), picked(lhs_one, i), picked(mask, i),
             (gain_two, None, None), (output_adapter_expand, None, None), (ffn_shrink, None, None),
             picked(one, i), picked(two, i), columns(conv_taps), columns(in_expand), row_tiles(out_shrink),
             columns(c["b"]), columns(c["c"]), columns(c["v"]), columns(c["conv"]), columns(c["gated"])]
            + (held_inputs if special else mixer_inputs())
            + ([(chunks[0]["ffn_grad"], None, None), (chunks[0]["second_grad"], None, None),
                (chunks[0]["mixer_grads"], (None, 4, 2, 128, 128), lambda h, *_: (h, 0, 0, 0, 0))] if i else []),
            [
                ((span, half), bf16, None, None),
                ((span, half), bf16, None, None),
                ((span, 2 * rank), bf16, None, None),
                ((rows, width), f32, None, None),
                ((4, 2, 2, 128, 128), bf16 if i else f32, None, None),
                ((4, 2, 128, 128), bf16 if i else f32, None, None),
                ((mixer_steps, 4, 2, 128, 128), bf16 if i else f32, (None, 4, 2, 128, 128), lambda h, *_: (h, 0, 0, 0, 0)),
            ],
            [
                pltpu.VMEM((rows, ext_one), f32),
                pltpu.VMEM((rows, ext_one), bf16),
                pltpu.VMEM((width, 2 * rank), bf16),
                pltpu.VMEM((rank, width), bf16),
                pltpu.VMEM((1, width), f32),
            ]
            + held_scratch,
            flops=2 * rows * half * ext_one * 4,
        )
        c.update(n_own=n_own, n_send=n_send, n_rank=n_rank, gh=grad_hidden, ffn_grad=ffn_grad, second_grad=second_grad, mixer_grads=grads)
        if special:
            feed_sum = scatter_x(feed_sum) if i == 0 else feed_sum
    for c in chunks:
        c["d_got"] = swap_tensor(after(c["d_send"], chunks[0]["f_got"]))
    chunks[0]["n_got"] = swap_tensor(chunks[0]["n_send"])
    if special:
        feed_sum = scatter_z(feed_sum)
        last = chunks[-1]
        early = cut(after(last["ffn_grad"], feed_sum, *(c["d_got"] for c in chunks)), last["second_grad"], last["mixer_grads"])
        early = scatter_core(early)
        first_step = (early,)
    else:
        first_step = ()

    block = half // 4
    in_half = lambda i, info: (0, info[INNER + i])
    in_full = lambda i, info: (0, info[3] * 4 + info[INNER + i])
    whole_block = lambda i, info: (0, 0)
    grad_out = ((4, 2, 128, 128), f32, (None, 2, 128, 128), lambda i, info: (i, 0, 0, 0))
    for k, c in enumerate(chunks):
        in_stack_full = lambda i, info, k=k: (k, 0, info[3] * 4 + info[INNER + i])
        masks = (mask, (None, span, rank), lambda i, info, k=k: (k, 0, 0))
        d_got = after(c["d_got"], *first_step)
        c["out"], c["down_grad"] = call(
            output_kernel, (4,), (info,),
            [
                (c["d_own"], (span, block), in_half),
                (d_got, (span, block), in_half),
                (c["d_own"], (span, rank), lambda i, info: (0, half // rank)),
                (d_got, (span, rank), lambda i, info: (0, half // rank)),
                (c["hidden"], (span, block), in_full),
                masks,
                (glhs, (None, span, block), in_stack_full),
                (down_adapter_expand, (rank, block), lambda i, info: (0, info[2] * 4 + i)),
            ]
            + ([(chunks[0]["out"], "any", None)] if k else []),
            [((tok_count, half), bf16, (span, block), lambda i, info, k=k: (k, i)), grad_out],
            flops=5 * 10**9,
            aliases={9: 0} if k else None,
        )
    wait()
    if special:
        feed_sum = gather_z(after(feed_sum, early))
        early = after(scatter_x(early), feed_sum, chunks[-1]["out"], chunks[0]["n_got"])
        second_step = (early,)
    else:
        second_step = ()
    for c in chunks[::-1]:
        c["rank_got"] = swap_tensor(after(c["n_rank"], *second_step))
    for k, c in enumerate(chunks):
        in_stack_full = lambda i, info, k=k: (k, 0, info[3] * 4 + info[INNER + i])
        masks = (mask, (None, span, rank), lambda i, info, k=k: (k, 0, 0))
        ranks = [(w, (span, 2 * rank), whole_block) for w in (c["n_rank"], c["rank_got"])]
        (c["in_grad"],) = call(
            rank_kernel, (4,), (info,), ranks + [masks, (lhs_one, (None, span, block), in_stack_full)], [grad_out],
            flops=5 * 10**9,
        )
    if special:
        feed_parts = [feed_sum, begin("dp", x_route, after(feed_sum, early))]
        early = after(scatter_z(early), feed_parts[1], *(c["in_grad"] for c in chunks))
        late = scatter_core(cut(summed("in_grad"), summed("down_grad")))
        h = 3 * 1024 // (4 * pieces)
        early = jnp.concatenate([early[:h], swap_tensor(early[:h]), early[h:]], axis=0)
        third_step = (early,)
    else:
        third_step = ()
    chunks[1]["n_got"] = swap_tensor(after(chunks[1]["n_send"], *third_step))
    for k, c in enumerate(chunks):
        in_stack_full = lambda i, info, k=k: (k, 0, info[3] * 4 + info[INNER + i])
        masks = (mask, (None, span, rank), lambda i, info, k=k: (k, 0, 0))
        ranks = [(w, (span, 2 * rank), whole_block) for w in (c["n_rank"], c["rank_got"])]
        n_got = after(c["n_got"], *third_step)
        (c["grad"],) = call(
            functools.partial(final_kernel, width), (4,), (info,),
            [(c["n_own"], (span, block), in_half), (n_got, (span, block), in_half)]
            + ranks
            + [
                (c["gh"], (span, block), in_full),
                (x_full, (None, span, block), in_stack_full),
                (lhs_one, (None, span, rank), lambda i, info, k=k: (k, 0, width // rank)),
                (scale, (None, span, 128), lambda i, info, k=k: (k, 0, 0)),
                masks,
                (gain_one, (1, block), lambda i, info: (0, info[2] * 4 + i)),
                (input_adapter_shrink, (block, rank), lambda i, info: (info[2] * 4 + i, 0)),
            ]
            + ([(chunks[0]["grad"], "any", None)] if k else []),
            [((tok_count, half), f32, (span, block), lambda i, info, k=k: (k, i))],
            flops=6 * 10**9,
            aliases={12: 0} if k else None,
        )
    block_output, input_grad = chunks[-1]["out"], chunks[-1]["grad"]

    if special:
        late = scatter_x(after(late, early))
        gathered = after(gather_z(early), chunks[0]["grad"], chunks[1]["n_got"])
        late = scatter_z(after(late, gathered))
        n = 4 * pieces
        feed_parts = [after(v, gathered) for v in feed_parts]
        feed_parts += [lax.ppermute(v, "dp", core_route) for v in feed_parts]
        expand_grad, first_grad = call(
            functools.partial(gather_feed_kernel, pieces, feed_steps), (1,), (info,),
            [(v, None, None) for v in feed_parts],
            [((2, rank, hidden_units), f32, None, None), ((hidden_units, rank), f32, None, None)],
            [pltpu.VMEM((feed.size // 128, 128), bf16)],
            flops=5 * 10**9,
        )
        late = jnp.concatenate([late, swap_tensor(late)], axis=0)
        over = after(lax.ppermute(gathered, "dp", x_route), expand_grad, chunks[1]["grad"])
        parts = [gathered, over] + [lax.ppermute(v, "dp", core_route) for v in (gathered, over)]
        ffn_grad, second_grad, mixer_grad, out_grad = call(
            functools.partial(unpack_early_kernel, pieces), (1,), (info,), [(v, None, None) for v in parts],
            [((width, 2 * rank), f32, None, None), ((rank, width), f32, None, None), ((3, rank, half), f32, None, None),
             ((half, rank), f32, None, None)],
            [pltpu.VMEM((n,) + early.shape, bf16)],
        )
        late = gather_z(late)
        over = after(lax.ppermute(late, "dp", x_route), ffn_grad)
        parts = [late, over] + [lax.ppermute(v, "dp", core_route) for v in (late, over)]
        in_grad, down_grad = call(
            functools.partial(unpack_late_kernel, pieces), (1,), (info,), [(v, None, None) for v in parts],
            [((width, rank), f32, None, None), ((rank, width), f32, None, None)],
            [pltpu.VMEM((n,) + late.shape[1:], bf16)],
        )
    else:
        last = chunks[-1]
        feed, mixer, ffn_grad, second_grad, in_grad, down_grad = lax.psum(
            (feed, last["mixer_grads"], last["ffn_grad"], last["second_grad"], summed("in_grad"), summed("down_grad")),
            ("dp", "ctx"),
        )

        def whole(part, axis):
            got = swap_tensor(part)
            pair = [jnp.where(tens == 0, part, got), jnp.where(tens == 0, got, part)]
            return jnp.concatenate(pair, axis=axis).astype(f32)

        def across(blocks):
            return blocks.reshape(-1, 128, 128).transpose(1, 0, 2).reshape(128, -1)

        ffn_grad = whole(ffn_grad.transpose(0, 2, 3, 1, 4).reshape(half, 2 * rank), 0)
        second_grad, down_grad = whole(across(second_grad), 1), whole(across(down_grad), 1)
        in_grad = whole(in_grad.reshape(half, rank), 0)
        mixer_grad = jnp.stack([across(mixer[:, j]) for j in range(3)]).astype(f32)
        out_grad = mixer[:, 3].reshape(half, rank).astype(f32)
        expand_grad = jnp.stack([across(feed[:, j]) for j in (1, 2)]).astype(f32)
        first_grad = feed[:, 0].reshape(hidden_units, rank).astype(f32)
    return (
        block_output,
        input_grad,
        in_grad,
        mixer_grad,
        out_grad,
        second_grad,
        ffn_grad,
        expand_grad,
        first_grad,
        down_grad,
    )


def solution(mesh):
    placed = (
        P(("dp", "ctx"), "tensor"),
        P(("dp", "ctx"), "tensor"),
        P("dp", None),
        P("dp"),
        P("dp"),
        P(),
        P(),
        P(None, "tensor"),
        P(None, "dp", "tensor"),
        P("tensor", "dp"),
        P(None, "dp", "tensor"),
        P("tensor", "dp"),
        P(),
        P(None, None, "tensor"),
        P("tensor", None),
        P(),
        P(),
        P(None, None, "tensor"),
        P("tensor", None),
        P(),
    )
    return jax.shard_map(
        body,
        mesh=mesh,
        in_specs=placed,
        out_specs=(
            P(("dp", "ctx"), "tensor"),
            P(("dp", "ctx"), "tensor"),
            P(),
            P(None, None, "tensor"),
            P("tensor", None),
            P(),
            P(),
            P(None, None, "tensor"),
            P("tensor", None),
            P(),
        ),
        check_vma=False,
    )
```
